32 devices in a mesh: dp: 16 (over z, y, core), tensor: 2 (over x).
Axes of the slice: x: 2, y: 2, z: 4, core: 2. Of those that a mesh axis runs over, the one named last changes fastest.
Arguments:
- block_input: bfloat16 [32768, 1024], P(('dp', 'tensor')), may hold values from -6 to 6
- mixer_gain: float32 [1024], replicated, may hold values from 0.25 to 1.75
- in_weight: bfloat16 [1024, 3, 1024], P(None, None, 'tensor'), may hold values from -0.1875 to 0.1875
- conv_kernel: bfloat16 [3, 1024], P(None, 'tensor'), may hold values from -3.5 to 3.5
- out_weight: bfloat16 [1024, 1024], P('tensor'), may hold values from -0.1875 to 0.1875
- ffn_gain: float32 [1024], replicated, may hold values from 0.25 to 1.75
- gate_weight: bfloat16 [1024, 4608], P(None, 'tensor'), may hold values from -0.1875 to 0.1875
- up_weight: bfloat16 [1024, 4608], P(None, 'tensor'), may hold values from -0.1875 to 0.1875
- down_weight: bfloat16 [4608, 1024], P('tensor'), may hold values from -0.09375 to 0.09375
- output_grad: bfloat16 [32768, 1024], P(('dp', 'tensor')), may hold values from -6 to 6
- lengths: int32 [32], P('dp'), may hold values from 256 to 1024, as said below
Outputs:
- block_output: bfloat16 [32768, 1024], P(('dp', 'tensor'))
- input_grad: bfloat16 [32768, 1024], P(('dp', 'tensor'))
- mixer_gain_grad: float32 [1024], replicated
- in_weight_grad: float32 [1024, 3, 1024], P(None, None, 'tensor')
- conv_kernel_grad: float32 [3, 1024], P(None, 'tensor')
- out_weight_grad: float32 [1024, 1024], P('tensor')
- ffn_gain_grad: float32 [1024], replicated
- gate_weight_grad: float32 [1024, 4608], P(None, 'tensor')
- up_weight_grad: float32 [1024, 4608], P(None, 'tensor')
- down_weight_grad: float32 [4608, 1024], P('tensor')
The draws below stay inside these ranges and needn't reach their ends.
Inputs may be any that keep to these rules, and one draw needn't show every extreme that they name: `lengths`: each slot holds one sequence at positions 0 to its length - 1; some slot has length 1024 and some 1024 // 4.
All inputs are finite; a program needn't handle non-finite values.
Results may differ from the reference program's by a relative error of at most 0.022.
Values may be sent and summed in bfloat16 or wider, within the bound.
A program may use at most 256 MiB of HBM per device.

```python
import jax
import jax.numpy as jnp
from jax import lax

D = 1024
FF = 4608
KERNEL = 3
SLOT_LEN = 1024
SLOTS_DEV = 2
SLOTS = 32
TOKENS = 32768
N_DP = 16


def draw_lengths(key, part):
    values = jax.random.randint(key, (SLOTS,), SLOT_LEN // 4, SLOT_LEN + 1, dtype=jnp.int32)
    values = values.at[0].set(SLOT_LEN)
    values = values.at[SLOTS - 1].set(SLOT_LEN // 4)
    return values


def levels(key, dims, cuts, smallest, top_value):
    gain = 1.0
    for dim, blocks in cuts:
        draws = jax.random.uniform(jax.random.fold_in(jax.random.fold_in(key, 6), dim), (blocks,), jnp.float32, smallest / len(cuts), top_value / len(cuts))
        gain = gain * jnp.repeat(jnp.exp(draws), dims[dim] // blocks).reshape((-1,) + (1,) * (len(dims) - 1 - dim))
    return gain


def normal_values(stream_key, extent, deviation, reach, split=(), kind=jnp.bfloat16):
    loudness = levels(stream_key, extent, split, -0.22, 0.18) if split else 1.0
    array = jax.random.normal(stream_key, extent, jnp.float32) * deviation * loudness
    return jnp.minimum(jnp.maximum(array, -reach), reach).astype(kind)


def setup_inputs(seed: int = 0) -> dict:
    splits = jax.random.split(jax.random.key(seed), 12)
    block_input = normal_values(splits[0], (TOKENS, D), 1.0, 6.0, ((0, 32),))
    mixer_gain = jnp.clip(1.0 + 0.15 * jax.random.normal(splits[1], (D,), jnp.float32), 0.25, 1.75)
    in_weight = normal_values(splits[2], (D, 3, D), D ** -0.5, 0.1875, ((2, 2),))
    conv_kernel = normal_values(splits[3], (KERNEL, D), KERNEL ** -0.5, 3.5, ((1, 2),))
    out_weight = normal_values(splits[4], (D, D), D ** -0.5, 0.1875, ((0, 2),))
    ffn_gain = jnp.clip(1.0 + 0.15 * jax.random.normal(splits[5], (D,), jnp.float32), 0.25, 1.75)
    gate_weight = normal_values(splits[6], (D, FF), D ** -0.5, 0.1875, ((1, 2),))
    up_weight = normal_values(splits[7], (D, FF), D ** -0.5, 0.1875, ((1, 2),))
    down_weight = normal_values(splits[8], (FF, D), FF ** -0.5, 0.09375, ((0, 2),))
    output_grad = normal_values(splits[9], (TOKENS, D), 1.0, 6.0, ((0, 32),))
    lengths = draw_lengths(jax.random.fold_in(splits[11], 71), 0)
    return dict(block_input=block_input, mixer_gain=mixer_gain, in_weight=in_weight, conv_kernel=conv_kernel, out_weight=out_weight, ffn_gain=ffn_gain, gate_weight=gate_weight, up_weight=up_weight, down_weight=down_weight, output_grad=output_grad, lengths=lengths)


eps = 1e-05

@jax.custom_vjp
def low(v):
    return lax.optimization_barrier(v.astype(jnp.bfloat16)).astype(jnp.float32)

@jax.custom_vjp
def low_back(v):
    return v

def low_keep(v):
    return (low(v), None)

def low_pass(kept, grad):
    return (grad,)

def back_keep(v):
    return (v, None)

def back_low(kept, grad):
    return (low(grad),)
low.defvjp(low_keep, low_pass)
low_back.defvjp(back_keep, back_low)

def matmul(left, right):
    return jnp.dot(left, right, precision=lax.Precision.HIGHEST)

def rms_scale(values, gain_values):
    return values * lax.rsqrt(lax.optimization_barrier(jnp.mean(values * values, axis=-1, keepdims=True)) + eps) * gain_values

def causal_conv(values, kernel_values):
    slot_length = values.shape[1]
    padded = jnp.pad(values, ((0, 0), (KERNEL - 1, 0), (0, 0)))
    summed = jnp.zeros_like(values)
    for offset in range(KERNEL):
        summed = summed + kernel_values[offset] * padded[:, offset:offset + slot_length]
    return summed

def forward(source, params):
    mixer_gain, in_weight, conv_kernel, out_weight, ffn_gain, gate_weight, up_weight, down_weight = params
    normed = low(rms_scale(source, mixer_gain))
    projected = low_back(matmul(normed, in_weight.reshape(D, 3 * D))).reshape(-1, 3, D)
    b_part = projected[:, 0]
    c_part = projected[:, 1]
    x_part = projected[:, 2]
    mixed = (b_part * x_part).reshape(-1, SLOT_LEN, D)
    convolved = causal_conv(mixed, conv_kernel).reshape(-1, D)
    gated = low(c_part * convolved)
    hidden = source + low_back(matmul(gated, out_weight))
    normed_two = low(rms_scale(hidden, ffn_gain))
    gate_value = low_back(matmul(normed_two, gate_weight))
    up_value = low_back(matmul(normed_two, up_weight))
    inner_low = low(jax.nn.silu(gate_value) * up_value)
    return hidden + low_back(matmul(inner_low, down_weight))

def reference(block_input, mixer_gain, in_weight, conv_kernel, out_weight, ffn_gain, gate_weight, up_weight, down_weight, output_grad, lengths):
    params = tuple((weight.astype(jnp.float32) for weight in (mixer_gain, in_weight, conv_kernel, out_weight, ffn_gain, gate_weight, up_weight, down_weight)))
    group_rows = SLOTS_DEV * SLOT_LEN
    input_groups = block_input.reshape(N_DP, group_rows, D)
    grad_groups = output_grad.reshape(N_DP, group_rows, D)
    group_lengths = lengths.reshape(N_DP, SLOTS_DEV)
    position = jnp.arange(SLOT_LEN, dtype=jnp.int32)

    def one_group(totals, pieces):
        group_input, group_grad, slot_lengths = pieces
        token_mask = (position[None, :] < slot_lengths[:, None]).astype(jnp.float32).reshape(group_rows, 1)
        output, pullback = jax.vjp(forward, group_input.astype(jnp.float32), params)
        cotangent = group_grad.astype(jnp.float32) * token_mask
        source_grad, param_grads = pullback(cotangent)
        totals = tuple((running + increment for running, increment in zip(totals, param_grads)))
        return (totals, (output.astype(jnp.bfloat16), source_grad.astype(jnp.bfloat16)))
    initial = tuple((jnp.zeros(weight.shape, jnp.float32) for weight in params))
    totals, (outputs, input_grads) = lax.scan(one_group, initial, (input_groups, grad_groups, group_lengths))
    return (outputs.reshape(N_DP * group_rows, D), input_grads.reshape(N_DP * group_rows, D), totals[0], totals[1], totals[2], totals[3], totals[4], totals[5], totals[6], totals[7])
```

```python
import functools

import jax
import jax.numpy as jnp
from jax import lax
from jax.experimental import pallas as pl
from jax.experimental.pallas import tpu as pltpu
from jax.sharding import PartitionSpec as P

KERNEL = 3


eps = 1e-05


def rms_forward(values, gain_values):
    inverse = lax.rsqrt(jnp.mean(values * values, axis=-1, keepdims=True) + eps)
    return (values * inverse * gain_values, inverse)


def rms_backward(values, inverse, gain_values, upstream):
    weighted = upstream * gain_values
    gain_part = jnp.sum(upstream * values * inverse, axis=0)
    through = inverse * weighted - values * inverse**3 * jnp.mean(
        weighted * values, axis=-1, keepdims=True
    )
    return (through, gain_part)


def local(
    block_input,
    mixer_gain,
    in_weight,
    conv_kernel,
    out_weight,
    ffn_gain,
    gate_weight,
    up_weight,
    down_weight,
    output_grad,
    lengths,
):
    local_rows = block_input.shape[0]
    model_width = block_input.shape[1]
    channels = in_weight.shape[2]
    slot_count = lengths.shape[0]
    source = block_input.astype(jnp.float32)
    normed_one, inverse_one = rms_forward(source, mixer_gain)
    gathered_one = lax.all_gather(normed_one.astype(jnp.bfloat16), "tensor", axis=0, tiled=True)
    group_rows = gathered_one.shape[0]
    slot_length = group_rows // slot_count
    in_flat = in_weight.reshape(model_width, 3 * channels)
    projected = jnp.dot(gathered_one, in_flat, preferred_element_type=jnp.float32).reshape(
        group_rows, 3, channels
    )
    b_part = projected[:, 0]
    c_part = projected[:, 1]
    x_part = projected[:, 2]
    mixed = (b_part * x_part).reshape(slot_count, slot_length, channels)
    kernel_values = conv_kernel.astype(jnp.float32)
    padded = jnp.pad(mixed, ((0, 0), (KERNEL - 1, 0), (0, 0)))
    convolved = jnp.zeros_like(mixed)
    for offset in range(KERNEL):
        convolved = convolved + kernel_values[offset] * padded[:, offset : offset + slot_length]
    convolved = convolved.reshape(group_rows, channels)
    gated = (c_part * convolved).astype(jnp.bfloat16)
    hidden = source + lax.psum_scatter(
        jnp.dot(gated, out_weight, preferred_element_type=jnp.float32).astype(jnp.bfloat16),
        "tensor",
        scatter_dimension=0,
        tiled=True,
    ).astype(jnp.float32)
    normed_two, inverse_two = rms_forward(hidden, ffn_gain)
    gathered_two = lax.all_gather(normed_two.astype(jnp.bfloat16), "tensor", axis=0, tiled=True)
    gate_value = jnp.dot(gathered_two, gate_weight, preferred_element_type=jnp.float32)
    up_value = jnp.dot(gathered_two, up_weight, preferred_element_type=jnp.float32)
    sigmoid_gate = jax.nn.sigmoid(gate_value)
    silu_value = gate_value * sigmoid_gate
    inner_low = (silu_value * up_value).astype(jnp.bfloat16)
    block_output = (
        hidden
        + lax.psum_scatter(
            jnp.dot(inner_low, down_weight, preferred_element_type=jnp.float32).astype(
                jnp.bfloat16
            ),
            "tensor",
            scatter_dimension=0,
            tiled=True,
        ).astype(jnp.float32)
    ).astype(jnp.bfloat16)
    row_index = lax.axis_index("tensor") * local_rows + jnp.arange(local_rows, dtype=jnp.int32)
    slot_of = row_index // slot_length
    position = row_index % slot_length
    matched = (slot_of[:, None] == jnp.arange(slot_count, dtype=jnp.int32)[None, :]) & (
        position[:, None] < lengths[None, :]
    )
    token_mask = jnp.any(matched, axis=1).astype(jnp.float32)
    cotangent = output_grad.astype(jnp.float32) * token_mask[:, None]
    grad_rows = lax.all_gather(cotangent.astype(jnp.bfloat16), "tensor", axis=0, tiled=True)
    inner_grad = jnp.einsum("rd,fd->rf", grad_rows, down_weight, preferred_element_type=jnp.float32)
    down_weight_grad = jnp.einsum(
        "rf,rd->fd", inner_low, grad_rows, preferred_element_type=jnp.float32
    )
    gate_grad = (
        inner_grad * up_value * sigmoid_gate * (1.0 + gate_value * (1.0 - sigmoid_gate))
    ).astype(jnp.bfloat16)
    up_grad = (inner_grad * silu_value).astype(jnp.bfloat16)
    gate_weight_grad = jnp.einsum(
        "rd,rf->df", gathered_two, gate_grad, preferred_element_type=jnp.float32
    )
    up_weight_grad = jnp.einsum(
        "rd,rf->df", gathered_two, up_grad, preferred_element_type=jnp.float32
    )
    from_gate = jnp.einsum("rf,df->rd", gate_grad, gate_weight, preferred_element_type=jnp.float32)
    normed_two_grad = lax.psum_scatter(
        (
            from_gate
            + jnp.einsum("rf,df->rd", up_grad, up_weight, preferred_element_type=jnp.float32)
        ).astype(jnp.bfloat16),
        "tensor",
        scatter_dimension=0,
        tiled=True,
    ).astype(jnp.float32)
    through_two, ffn_gain_part = rms_backward(hidden, inverse_two, ffn_gain, normed_two_grad)
    hidden_grad = cotangent + through_two
    hidden_rows = lax.all_gather(hidden_grad.astype(jnp.bfloat16), "tensor", axis=0, tiled=True)
    gated_grad = jnp.einsum(
        "rd,cd->rc", hidden_rows, out_weight, preferred_element_type=jnp.float32
    )
    out_weight_grad = jnp.einsum(
        "rc,rd->cd", gated, hidden_rows, preferred_element_type=jnp.float32
    )
    c_grad = gated_grad * convolved
    conv_grad = (gated_grad * c_part).reshape(slot_count, slot_length, channels)
    padded_after = jnp.pad(conv_grad, ((0, 0), (0, KERNEL - 1), (0, 0)))
    mixed_grad = jnp.zeros_like(conv_grad)
    kernel_rows = []
    for offset in range(KERNEL):
        shift_start = KERNEL - 1 - offset
        mixed_grad = (
            mixed_grad
            + kernel_values[offset] * padded_after[:, shift_start : shift_start + slot_length]
        )
        kernel_rows.append(
            jnp.sum(conv_grad * padded[:, offset : offset + slot_length], axis=(0, 1))
        )
    conv_kernel_grad = jnp.stack(kernel_rows, axis=0)
    mixed_grad = mixed_grad.reshape(group_rows, channels)
    projected_grad = jnp.stack([mixed_grad * x_part, c_grad, mixed_grad * b_part], axis=1).astype(
        jnp.bfloat16
    )
    in_weight_grad = jnp.einsum(
        "rd,rkc->dkc", gathered_one, projected_grad, preferred_element_type=jnp.float32
    )
    normed_one_grad = lax.psum_scatter(
        jnp.einsum(
            "rkc,dkc->rd", projected_grad, in_weight, preferred_element_type=jnp.float32
        ).astype(jnp.bfloat16),
        "tensor",
        scatter_dimension=0,
        tiled=True,
    ).astype(jnp.float32)
    through_one, mixer_gain_part = rms_backward(source, inverse_one, mixer_gain, normed_one_grad)
    input_grad = (hidden_grad + through_one).astype(jnp.bfloat16)
    (
        in_weight_grad,
        conv_kernel_grad,
        out_weight_grad,
        gate_weight_grad,
        up_weight_grad,
        down_weight_grad,
    ) = (
        lax.psum(in_weight_grad.astype(jnp.bfloat16), "dp").astype(jnp.float32),
        lax.psum(conv_kernel_grad.astype(jnp.bfloat16), "dp").astype(jnp.float32),
        lax.psum(out_weight_grad.astype(jnp.bfloat16), "dp").astype(jnp.float32),
        lax.psum(gate_weight_grad.astype(jnp.bfloat16), "dp").astype(jnp.float32),
        lax.psum(up_weight_grad.astype(jnp.bfloat16), "dp").astype(jnp.float32),
        lax.psum(down_weight_grad.astype(jnp.bfloat16), "dp").astype(jnp.float32),
    )
    mixer_gain_grad, ffn_gain_grad = lax.psum((mixer_gain_part, ffn_gain_part), ("dp", "tensor"))
    return (
        block_output,
        input_grad,
        mixer_gain_grad,
        in_weight_grad,
        conv_kernel_grad,
        out_weight_grad,
        ffn_gain_grad,
        gate_weight_grad,
        up_weight_grad,
        down_weight_grad,
    )


NN = (((1,), (0,)), ((), ()))
NT = (((1,), (1,)), ((), ()))
TN = (((0,), (0,)), ((), ()))
F32 = jnp.float32
BF16 = jnp.bfloat16


def dot(a, b, dims=NN):
    return lax.dot_general(a, b, dims, preferred_element_type=F32)


def ffn_kernel(n2, cot, wg, wu, wd, inner, gg, ug, out, n2g, acc1, acc2, *, rows):
    step = pl.program_id(0)

    @pl.when(step == 0)
    def _():
        acc1[...] = jnp.zeros_like(acc1)
        acc2[...] = jnp.zeros_like(acc2)

    def front(r):
        s = pl.ds(r * rows, rows)
        a, c = n2[s, :], cot[s, :]
        return dot(a, wg[...]), dot(a, wu[...]), dot(c, wd[...], NT)

    count = n2.shape[0] // rows
    held = front(0)
    for r in range(count):
        following = front(r + 1) if r + 1 < count else None
        s = pl.ds(r * rows, rows)
        g, u, ig = held
        sig = jax.nn.sigmoid(g)
        silu = g * sig
        low = (silu * u).astype(BF16)
        gg_low = (ig * u * (sig + silu * (1.0 - sig))).astype(BF16)
        ug_low = (ig * silu).astype(BF16)
        inner[s, :] = low
        gg[s, :] = gg_low
        ug[s, :] = ug_low
        acc1[s, :] += dot(low, wd[...])
        acc2[s, :] += dot(gg_low, wg[...], NT) + dot(ug_low, wu[...], NT)
        held = following

    @pl.when(step == pl.num_programs(0) - 1)
    def _():
        out[...] = acc1[...].astype(out.dtype)
        n2g[...] = acc2[...].astype(n2g.dtype)


def ffn(n2, cot, wg, wu, wd, name):
    rows, width = n2.shape
    hidden = wg.shape[1]
    tile = 256
    full = pl.BlockSpec((rows, width), lambda h: (0, 0), pipeline_mode=pl.Buffered(1))

    def col(n):
        return pl.BlockSpec((n, tile), lambda h: (0, h))

    return pl.pallas_call(
        functools.partial(ffn_kernel, rows=256),
        grid=(hidden // tile,),
        in_specs=[full, full, col(width), col(width), pl.BlockSpec((tile, width), lambda h: (h, 0))],
        out_specs=[col(rows), col(rows), col(rows), full, full],
        out_shape=[jax.ShapeDtypeStruct((rows, hidden), BF16)] * 3
        + [jax.ShapeDtypeStruct((rows, width), BF16)] * 2,
        scratch_shapes=[pltpu.VMEM((rows, width), F32)] * 2,
        name=name,
        cost_estimate=pl.CostEstimate(
            flops=12 * rows * width * hidden,
            bytes_accessed=6 * hidden * width + 6 * rows * hidden + 8 * rows * width,
            transcendentals=rows * hidden,
        ),
        compiler_params=pltpu.CompilerParams(vmem_limit_bytes=48 * 2**20),
    )(n2, cot, wg, wu, wd)


def shift_down(values, amount):
    return jnp.pad(values, ((amount, 0), (0, 0)))[: values.shape[0]]


def shift_up(values, amount):
    return jnp.pad(values, ((0, amount), (0, 0)))[amount:]


def mixer_forward(normed, in_half, kernel_half):
    channels = in_half.shape[2]
    projected = dot(normed, in_half.reshape(in_half.shape[0], 3 * channels))
    b_part = projected[:, :channels]
    c_part = projected[:, channels : 2 * channels]
    x_part = projected[:, 2 * channels :]
    mixed = b_part * x_part
    convolved = jnp.zeros_like(mixed)
    for k in range(KERNEL):
        convolved = convolved + kernel_half[k] * shift_down(mixed, KERNEL - 1 - k)
    gated = (c_part * convolved).astype(BF16)
    return b_part, c_part, x_part, mixed, convolved, gated


def quarter_gather(weight, rows_axis_quarter, dp_index):
    rows = weight.shape[0] // 4
    sliced = lax.dynamic_slice_in_dim(weight, rows_axis_quarter * rows, rows, axis=0)
    first = lax.ppermute(sliced, "tensor", [(0, 1), (1, 0)])
    n_dp = lax.axis_size("dp")
    flip_y = [(i, i ^ 2) for i in range(n_dp)]
    flip_c = [(i, i ^ 1) for i in range(n_dp)]
    from_y = lax.ppermute(first, "dp", flip_y)
    both = jnp.stack([first, from_y])
    from_c = lax.ppermute(both, "dp", flip_c)
    out = jnp.zeros((4, rows) + weight.shape[1:], weight.dtype)
    for piece, which in ((both[0], 0), (both[1], 2), (from_c[0], 1), (from_c[1], 3)):
        out = lax.dynamic_update_slice_in_dim(
            out, piece[None], rows_axis_quarter ^ which, axis=0
        )
    return out.reshape(weight.shape)


def fast(
    block_input,
    mixer_gain,
    in_weight,
    conv_kernel,
    out_weight,
    ffn_gain,
    gate_weight,
    up_weight,
    down_weight,
    output_grad,
    lengths,
):
    rows = block_input.shape[0]
    channels = in_weight.shape[2]
    me = lax.axis_index("tensor")
    dp_index = lax.axis_index("dp")
    swap = [(0, 1), (1, 0)]
    quarter = dp_index % 4

    other_input = lax.ppermute(block_input, "tensor", swap)
    in_other = quarter_gather(in_weight, quarter, dp_index)
    out_other = quarter_gather(out_weight, quarter, dp_index)
    kernel_other = lax.ppermute(conv_kernel, "tensor", swap).astype(F32)
    other_grad = lax.ppermute(output_grad, "tensor", swap)
    kernel_own = conv_kernel.astype(F32)

    position = jnp.arange(rows, dtype=jnp.int32)
    mask_own = (position < lengths[me])[:, None]
    mask_other = (position < lengths[1 - me])[:, None]
    cot_own = jnp.where(mask_own, output_grad, jnp.zeros_like(output_grad))
    cot_other = jnp.where(mask_other, other_grad, jnp.zeros_like(other_grad))

    def forward(source_low):
        source = source_low.astype(F32)
        normed, inverse = rms_forward(source, mixer_gain)
        normed = normed.astype(BF16)
        parts = [
            mixer_forward(normed, w, k)
            for w, k in ((in_weight, kernel_own), (in_other, kernel_other))
        ]
        hidden = source + (dot(parts[0][5], out_weight) + dot(parts[1][5], out_other))
        normed_two, inverse_two = rms_forward(hidden, ffn_gain)
        return source, normed, inverse, parts, hidden, normed_two.astype(BF16), inverse_two

    source, normed_one, inverse_one, parts, hidden, n2_own, inverse_two = forward(block_input)
    n2_other = forward(other_input)[5]

    inner_o, gg_o, ug_o, out_o, n2g_o = ffn(n2_own, cot_own, gate_weight, up_weight, down_weight, "ffn_own")
    inner_p, gg_p, ug_p, out_p, n2g_p = ffn(
        n2_other, cot_other, gate_weight, up_weight, down_weight, "ffn_other"
    )
    n2g_recv = lax.ppermute(n2g_p, "tensor", swap)
    out_recv = lax.ppermute(out_p, "tensor", swap)

    def pair(a_o, a_p, b_o, b_p):
        return dot(
            jnp.concatenate([a_o, a_p], axis=0), jnp.concatenate([b_o, b_p], axis=0), TN
        ).astype(BF16)

    down_grad = pair(inner_o, inner_p, cot_own, cot_other)
    gate_grad = pair(n2_own, n2_other, gg_o, gg_p)
    up_grad = pair(n2_own, n2_other, ug_o, ug_p)

    normed_two_grad = n2g_o.astype(F32) + n2g_recv.astype(F32)
    block_output = (hidden + (out_o.astype(F32) + out_recv.astype(F32))).astype(BF16)
    through_two, ffn_gain_part = rms_backward(hidden, inverse_two, ffn_gain, normed_two_grad)
    hidden_grad = cot_own.astype(F32) + through_two
    hidden_low = hidden_grad.astype(BF16)

    normed_one_grad = 0.0
    in_grads, out_grads, kernel_grads = [], [], []
    for half, w_in, w_out, kernel in (
        (parts[0], in_weight, out_weight, kernel_own),
        (parts[1], in_other, out_other, kernel_other),
    ):
        b_part, c_part, x_part, mixed, convolved, gated = half
        gated_grad = dot(hidden_low, w_out, NT)
        out_grads.append(dot(gated, hidden_low, TN).astype(BF16))
        c_grad = gated_grad * convolved
        conv_grad = gated_grad * c_part
        mixed_grad = jnp.zeros_like(conv_grad)
        kernel_rows = []
        for k in range(KERNEL):
            back = KERNEL - 1 - k
            mixed_grad = mixed_grad + kernel[k] * shift_up(conv_grad, back)
            kernel_rows.append(jnp.sum(conv_grad * shift_down(mixed, back), axis=0))
        kernel_grads.append(jnp.stack(kernel_rows))
        projected_grad = jnp.concatenate(
            [mixed_grad * x_part, c_grad, mixed_grad * b_part], axis=1
        ).astype(BF16)
        w_flat = w_in.reshape(w_in.shape[0], 3 * channels)
        in_grads.append(dot(normed_one, projected_grad, TN).astype(BF16))
        normed_one_grad = normed_one_grad + dot(projected_grad, w_flat, NT)
    through_one, mixer_gain_part = rms_backward(source, inverse_one, mixer_gain, normed_one_grad)
    input_grad = (hidden_grad + through_one).astype(BF16)

    in_grad = in_grads[0] + lax.ppermute(in_grads[1], "tensor", swap)
    out_grad = out_grads[0] + lax.ppermute(out_grads[1], "tensor", swap)

    kernel_first = jnp.where(me == 0, kernel_grads[0], kernel_grads[1])
    kernel_second = jnp.where(me == 0, kernel_grads[1], kernel_grads[0])
    small = jnp.concatenate(
        [
            mixer_gain_part[None],
            ffn_gain_part[None],
            jnp.concatenate([kernel_first, kernel_second], axis=1),
        ],
        axis=0,
    )
    small = lax.psum(small, ("dp", "tensor"))
    conv_kernel_grad = lax.dynamic_slice_in_dim(small[2:], me * channels, channels, axis=1)

    down_grad, gate_grad, up_grad, in_grad, out_grad = [
        lax.psum(g, "dp").astype(F32) for g in (down_grad, gate_grad, up_grad, in_grad, out_grad)
    ]
    return (
        block_output,
        input_grad,
        small[0],
        in_grad.reshape(in_weight.shape),
        conv_kernel_grad,
        out_grad,
        small[1],
        gate_grad,
        up_grad,
        down_grad,
    )


def solution(mesh):
    def step(*args):
        rows, slots = args[0].shape[0], args[10].shape[0]
        whole_slots = mesh.shape["tensor"] == 2 and slots == 2 and mesh.shape["dp"] % 4 == 0 and rows == 1024
        return (fast if whole_slots else local)(*args)

    return jax.shard_map(
        step,
        mesh=mesh,
        in_specs=(
            P(("dp", "tensor"), None),
            P(),
            P(None, None, "tensor"),
            P(None, "tensor"),
            P("tensor", None),
            P(),
            P(None, "tensor"),
            P(None, "tensor"),
            P("tensor", None),
            P(("dp", "tensor"), None),
            P("dp"),
        ),
        out_specs=(
            P(("dp", "tensor"), None),
            P(("dp", "tensor"), None),
            P(),
            P(None, None, "tensor"),
            P(None, "tensor"),
            P("tensor", None),
            P(),
            P(None, "tensor"),
            P(None, "tensor"),
            P("tensor", None),
        ),
        check_vma=False,
    )
```

```python
import functools

import jax
import jax.numpy as jnp
from jax import lax
from jax.experimental import pallas as pl
from jax.experimental.pallas import tpu as pltpu
from jax.sharding import PartitionSpec as P

KERNEL = 3


eps = 1e-05


def rms_forward(values, gain_values):
    inverse = lax.rsqrt(jnp.mean(values * values, axis=-1, keepdims=True) + eps)
    return (values * inverse * gain_values, inverse)


def rms_backward(values, inverse, gain_values, upstream):
    weighted = upstream * gain_values
    gain_part = jnp.sum(upstream * values * inverse, axis=0)
    through = inverse * weighted - values * inverse**3 * jnp.mean(
        weighted * values, axis=-1, keepdims=True
    )
    return (through, gain_part)


def local(
    block_input,
    mixer_gain,
    in_weight,
    conv_kernel,
    out_weight,
    ffn_gain,
    gate_weight,
    up_weight,
    down_weight,
    output_grad,
    lengths,
):
    local_rows = block_input.shape[0]
    model_width = block_input.shape[1]
    channels = in_weight.shape[2]
    slot_count = lengths.shape[0]
    source = block_input.astype(jnp.float32)
    normed_one, inverse_one = rms_forward(source, mixer_gain)
    gathered_one = lax.all_gather(normed_one.astype(jnp.bfloat16), "tensor", axis=0, tiled=True)
    group_rows = gathered_one.shape[0]
    slot_length = group_rows // slot_count
    in_flat = in_weight.reshape(model_width, 3 * channels)
    projected = jnp.dot(gathered_one, in_flat, preferred_element_type=jnp.float32).reshape(
        group_rows, 3, channels
    )
    b_part = projected[:, 0]
    c_part = projected[:, 1]
    x_part = projected[:, 2]
    mixed = (b_part * x_part).reshape(slot_count, slot_length, channels)
    kernel_values = conv_kernel.astype(jnp.float32)
    padded = jnp.pad(mixed, ((0, 0), (KERNEL - 1, 0), (0, 0)))
    convolved = jnp.zeros_like(mixed)
    for offset in range(KERNEL):
        convolved = convolved + kernel_values[offset] * padded[:, offset : offset + slot_length]
    convolved = convolved.reshape(group_rows, channels)
    gated = (c_part * convolved).astype(jnp.bfloat16)
    hidden = source + lax.psum_scatter(
        jnp.dot(gated, out_weight, preferred_element_type=jnp.float32).astype(jnp.bfloat16),
        "tensor",
        scatter_dimension=0,
        tiled=True,
    ).astype(jnp.float32)
    normed_two, inverse_two = rms_forward(hidden, ffn_gain)
    gathered_two = lax.all_gather(normed_two.astype(jnp.bfloat16), "tensor", axis=0, tiled=True)
    gate_value = jnp.dot(gathered_two, gate_weight, preferred_element_type=jnp.float32)
    up_value = jnp.dot(gathered_two, up_weight, preferred_element_type=jnp.float32)
    sigmoid_gate = jax.nn.sigmoid(gate_value)
    silu_value = gate_value * sigmoid_gate
    inner_low = (silu_value * up_value).astype(jnp.bfloat16)
    block_output = (
        hidden
        + lax.psum_scatter(
            jnp.dot(inner_low, down_weight, preferred_element_type=jnp.float32).astype(
                jnp.bfloat16
            ),
            "tensor",
            scatter_dimension=0,
            tiled=True,
        ).astype(jnp.float32)
    ).astype(jnp.bfloat16)
    row_index = lax.axis_index("tensor") * local_rows + jnp.arange(local_rows, dtype=jnp.int32)
    slot_of = row_index // slot_length
    position = row_index % slot_length
    matched = (slot_of[:, None] == jnp.arange(slot_count, dtype=jnp.int32)[None, :]) & (
        position[:, None] < lengths[None, :]
    )
    token_mask = jnp.any(matched, axis=1).astype(jnp.float32)
    cotangent = output_grad.astype(jnp.float32) * token_mask[:, None]
    grad_rows = lax.all_gather(cotangent.astype(jnp.bfloat16), "tensor", axis=0, tiled=True)
    inner_grad = jnp.einsum("rd,fd->rf", grad_rows, down_weight, preferred_element_type=jnp.float32)
    down_weight_grad = jnp.einsum(
        "rf,rd->fd", inner_low, grad_rows, preferred_element_type=jnp.float32
    )
    gate_grad = (
        inner_grad * up_value * sigmoid_gate * (1.0 + gate_value * (1.0 - sigmoid_gate))
    ).astype(jnp.bfloat16)
    up_grad = (inner_grad * silu_value).astype(jnp.bfloat16)
    gate_weight_grad = jnp.einsum(
        "rd,rf->df", gathered_two, gate_grad, preferred_element_type=jnp.float32
    )
    up_weight_grad = jnp.einsum(
        "rd,rf->df", gathered_two, up_grad, preferred_element_type=jnp.float32
    )
    from_gate = jnp.einsum("rf,df->rd", gate_grad, gate_weight, preferred_element_type=jnp.float32)
    normed_two_grad = lax.psum_scatter(
        (
            from_gate
            + jnp.einsum("rf,df->rd", up_grad, up_weight, preferred_element_type=jnp.float32)
        ).astype(jnp.bfloat16),
        "tensor",
        scatter_dimension=0,
        tiled=True,
    ).astype(jnp.float32)
    through_two, ffn_gain_part = rms_backward(hidden, inverse_two, ffn_gain, normed_two_grad)
    hidden_grad = cotangent + through_two
    hidden_rows = lax.all_gather(hidden_grad.astype(jnp.bfloat16), "tensor", axis=0, tiled=True)
    gated_grad = jnp.einsum(
        "rd,cd->rc", hidden_rows, out_weight, preferred_element_type=jnp.float32
    )
    out_weight_grad = jnp.einsum(
        "rc,rd->cd", gated, hidden_rows, preferred_element_type=jnp.float32
    )
    c_grad = gated_grad * convolved
    conv_grad = (gated_grad * c_part).reshape(slot_count, slot_length, channels)
    padded_after = jnp.pad(conv_grad, ((0, 0), (0, KERNEL - 1), (0, 0)))
    mixed_grad = jnp.zeros_like(conv_grad)
    kernel_rows = []
    for offset in range(KERNEL):
        shift_start = KERNEL - 1 - offset
        mixed_grad = (
            mixed_grad
            + kernel_values[offset] * padded_after[:, shift_start : shift_start + slot_length]
        )
        kernel_rows.append(
            jnp.sum(conv_grad * padded[:, offset : offset + slot_length], axis=(0, 1))
        )
    conv_kernel_grad = jnp.stack(kernel_rows, axis=0)
    mixed_grad = mixed_grad.reshape(group_rows, channels)
    projected_grad = jnp.stack([mixed_grad * x_part, c_grad, mixed_grad * b_part], axis=1).astype(
        jnp.bfloat16
    )
    in_weight_grad = jnp.einsum(
        "rd,rkc->dkc", gathered_one, projected_grad, preferred_element_type=jnp.float32
    )
    normed_one_grad = lax.psum_scatter(
        jnp.einsum(
            "rkc,dkc->rd", projected_grad, in_weight, preferred_element_type=jnp.float32
        ).astype(jnp.bfloat16),
        "tensor",
        scatter_dimension=0,
        tiled=True,
    ).astype(jnp.float32)
    through_one, mixer_gain_part = rms_backward(source, inverse_one, mixer_gain, normed_one_grad)
    input_grad = (hidden_grad + through_one).astype(jnp.bfloat16)
    (
        in_weight_grad,
        conv_kernel_grad,
        out_weight_grad,
        gate_weight_grad,
        up_weight_grad,
        down_weight_grad,
    ) = (
        lax.psum(in_weight_grad.astype(jnp.bfloat16), "dp").astype(jnp.float32),
        lax.psum(conv_kernel_grad.astype(jnp.bfloat16), "dp").astype(jnp.float32),
        lax.psum(out_weight_grad.astype(jnp.bfloat16), "dp").astype(jnp.float32),
        lax.psum(gate_weight_grad.astype(jnp.bfloat16), "dp").astype(jnp.float32),
        lax.psum(up_weight_grad.astype(jnp.bfloat16), "dp").astype(jnp.float32),
        lax.psum(down_weight_grad.astype(jnp.bfloat16), "dp").astype(jnp.float32),
    )
    mixer_gain_grad, ffn_gain_grad = lax.psum((mixer_gain_part, ffn_gain_part), ("dp", "tensor"))
    return (
        block_output,
        input_grad,
        mixer_gain_grad,
        in_weight_grad,
        conv_kernel_grad,
        out_weight_grad,
        ffn_gain_grad,
        gate_weight_grad,
        up_weight_grad,
        down_weight_grad,
    )


NN = (((1,), (0,)), ((), ()))
NT = (((1,), (1,)), ((), ()))
TN = (((0,), (0,)), ((), ()))
F32 = jnp.float32
BF16 = jnp.bfloat16


def dot(a, b, dims=NN):
    return lax.dot_general(a, b, dims, preferred_element_type=F32)


def ffn_kernel(n2, cot, wg, wu, wd, inner, gg, ug, out, n2g, acc1, acc2, *, rows):
    step = pl.program_id(0)

    @pl.when(step == 0)
    def _():
        acc1[...] = jnp.zeros_like(acc1)
        acc2[...] = jnp.zeros_like(acc2)

    def front(r):
        s = pl.ds(r * rows, rows)
        a, c = n2[s, :], cot[s, :]
        return dot(a, wg[...]), dot(a, wu[...]), dot(c, wd[...], NT)

    count = n2.shape[0] // rows
    held = front(0)
    for r in range(count):
        following = front(r + 1) if r + 1 < count else None
        s = pl.ds(r * rows, rows)
        g, u, ig = held
        sig = jax.nn.sigmoid(g)
        silu = g * sig
        low = (silu * u).astype(BF16)
        gg_low = (ig * u * (sig + silu * (1.0 - sig))).astype(BF16)
        ug_low = (ig * silu).astype(BF16)
        inner[s, :] = low
        gg[s, :] = gg_low
        ug[s, :] = ug_low
        acc1[s, :] += dot(low, wd[...])
        acc2[s, :] += dot(gg_low, wg[...], NT) + dot(ug_low, wu[...], NT)
        held = following

    @pl.when(step == pl.num_programs(0) - 1)
    def _():
        out[...] = acc1[...].astype(out.dtype)
        n2g[...] = acc2[...].astype(n2g.dtype)


def ffn(n2, cot, wg, wu, wd, name):
    rows, width = n2.shape
    hidden = wg.shape[1]
    tile = 256
    full = pl.BlockSpec((rows, width), lambda h: (0, 0), pipeline_mode=pl.Buffered(1))

    def col(n):
        return pl.BlockSpec((n, tile), lambda h: (0, h))

    return pl.pallas_call(
        functools.partial(ffn_kernel, rows=256),
        grid=(hidden // tile,),
        in_specs=[full, full, col(width), col(width), pl.BlockSpec((tile, width), lambda h: (h, 0))],
        out_specs=[col(rows), col(rows), col(rows), full, full],
        out_shape=[jax.ShapeDtypeStruct((rows, hidden), BF16)] * 3
        + [jax.ShapeDtypeStruct((rows, width), BF16)] * 2,
        scratch_shapes=[pltpu.VMEM((rows, width), F32)] * 2,
        name=name,
        cost_estimate=pl.CostEstimate(
            flops=12 * rows * width * hidden,
            bytes_accessed=6 * hidden * width + 6 * rows * hidden + 8 * rows * width,
            transcendentals=rows * hidden,
        ),
        compiler_params=pltpu.CompilerParams(vmem_limit_bytes=48 * 2**20),
    )(n2, cot, wg, wu, wd)


MESH = pl.DeviceIdType.MESH


class Cube:
    def __init__(self, order, rows):
        me = lax.axis_index("dp")
        self.tensor = lax.axis_index("tensor")
        self.partner, self.size, self.mine, self.theirs = [], [], [], []
        base, size = 0, rows
        for bit in order:
            weight = 1 << bit
            mine = (me // weight) % 2
            self.partner.append(me + weight - 2 * weight * mine)
            size //= 2
            self.size.append(size)
            self.mine.append(pl.multiple_of(base + mine * size, size))
            self.theirs.append(pl.multiple_of(base + (1 - mine) * size, size))
            base = base + mine * size
        self.stages = len(order)

    def scatter(self, s, j, held, received, send, recv):
        return pltpu.make_async_remote_copy(
            src_ref=held.at[j, pl.ds(self.theirs[s], self.size[s])],
            dst_ref=received[s].at[j],
            send_sem=send.at[s, j],
            recv_sem=recv.at[s, j],
            device_id=(self.partner[s], self.tensor),
            device_id_type=MESH,
        )

    def add(self, s, j, held, received):
        rows = pl.ds(self.mine[s], self.size[s])
        held[j, rows, :] = (held[j, rows, :].astype(F32) + received[s][j].astype(F32)).astype(BF16)

    def free(self, s, credit):
        pl.semaphore_signal(
            credit.at[s], inc=1, device_id=(self.partner[s], self.tensor), device_id_type=MESH
        )

    def gather(self, s, j, held, send, recv):
        rows = pl.ds(self.mine[s], self.size[s])
        slot = 2 * self.stages - 1 - s
        return pltpu.make_async_remote_copy(
            src_ref=held.at[j, rows],
            dst_ref=held.at[j, rows],
            send_sem=send.at[slot, j],
            recv_sem=recv.at[slot, j],
            device_id=(self.partner[s], self.tensor),
            device_id_type=MESH,
        )


def enter(devices):
    barrier = pltpu.get_barrier_semaphore()
    for device in devices:
        pl.semaphore_signal(barrier, inc=1, device_id=device, device_id_type=MESH)
    pl.semaphore_wait(barrier, len(devices))


TILE = 256


def grads_kernel(
    n2, cot, inner_o, inner_p, gg_o, gg_p, ug_o, ug_p, n2g, out_p,
    down_out, gate_out, up_out, n2g_recv, out_recv,
    held, rc, ry, ra, rb, operand, staged, load_sem, store_sem, send, recv, x_send, x_recv, credit,
):
    received = (rc, ry, ra, rb)
    width = n2.shape[1]
    rows = inner_o.shape[0]
    per = inner_o.shape[1] // TILE
    total = 3 * per
    cube = Cube((0, 1, 2, 3), TILE)
    other_x = (lax.axis_index("dp"), 1 - lax.axis_index("tensor"))
    enter([(p, cube.tensor) for p in cube.partner] + [other_x])

    def swap(src, dst, k):
        return pltpu.make_async_remote_copy(
            src_ref=src, dst_ref=dst, send_sem=x_send.at[k], recv_sem=x_recv.at[k],
            device_id=other_x, device_id_type=MESH,
        )

    swaps = [swap(n2g, n2g_recv, 0), swap(out_p, out_recv, 1)]
    for one in swaps:
        one.start()

    pairs = ((inner_o, inner_p), (gg_o, gg_p), (ug_o, ug_p))

    def loads(group, i, slot):
        cols = pl.ds(pl.multiple_of(i * TILE, TILE), TILE)
        return [
            pltpu.make_async_copy(
                pairs[group][k].at[:, cols], operand.at[slot, pl.ds(k * rows, rows)], load_sem.at[slot, k]
            )
            for k in range(2)
        ]

    for copy in loads(0, 0, 0):
        copy.start()

    def hand_back(s, j):
        pl.semaphore_wait(credit.at[s], 1)
        cube.gather(s, j, held, send, recv).start()

    def to_y(j):
        cube.scatter(0, j, held, received, send, recv).wait()
        cube.free(0, credit)
        cube.add(0, j, held, received)
        cube.scatter(1, j, held, received, send, recv).start()

    for group in range(3):

        def compute(i, carry, group=group):
            j = group * per + i
            slot = j % 2
            for copy in loads(group, i, slot):
                copy.wait()

            @pl.when(i + 1 < per)
            def _():
                for copy in loads(group, i + 1, 1 - slot):
                    copy.start()

            if group < 2:

                @pl.when(i + 1 == per)
                def _():
                    for copy in loads(group + 1, 0, 1 - slot):
                        copy.start()

            if group == 0:
                held[j] = dot(operand[slot], cot[...], TN).astype(BF16)
            else:
                product = dot(n2[...], operand[slot], TN).astype(BF16)
                for k in range(width // TILE):
                    held[j, :, k * TILE : (k + 1) * TILE] = product[k * TILE : (k + 1) * TILE]
            cube.scatter(0, j, held, received, send, recv).start()

            @pl.when(j > 0)
            def _():
                to_y(j - 1)

            return carry

        lax.fori_loop(0, per, compute, 0)
    to_y(total - 1)

    def reduce_step(tick, carry):
        for lag, s in ((0, 2), (1, 3), (2, 4)):
            j = tick - lag

            @pl.when((j >= 0) & (j < total))
            def _(j=j, s=s):
                cube.scatter(s - 1, j, held, received, send, recv).wait()
                cube.free(s - 1, credit)
                cube.add(s - 1, j, held, received)
                if s < 4:
                    cube.scatter(s, j, held, received, send, recv).start()
                else:
                    hand_back(3, j)

        for lag, s in ((3, 3), (4, 2)):
            j = tick - lag

            @pl.when((j >= 0) & (j < total))
            def _(j=j, s=s):
                cube.gather(s, j, held, send, recv).wait()
                hand_back(s - 1, j)

        return carry

    lax.fori_loop(0, total + 4, reduce_step, 0)

    def stores(group, i, slot):
        at = pl.ds(pl.multiple_of(i * TILE, TILE), TILE)
        if group == 0:
            return [pltpu.make_async_copy(staged.at[slot], down_out.at[at], store_sem.at[slot, 0])]
        out = gate_out if group == 1 else up_out
        return [
            pltpu.make_async_copy(
                staged.at[slot, :, pl.ds(k * TILE, TILE)],
                out.at[pl.ds(k * TILE, TILE), at],
                store_sem.at[slot, k],
            )
            for k in range(width // TILE)
        ]

    cube.gather(1, 0, held, send, recv).wait()
    hand_back(0, 0)
    for group in range(3):

        def finish(i, carry, group=group):
            j = group * per + i
            slot = i % 2

            @pl.when(j + 1 < total)
            def _():
                cube.gather(1, j + 1, held, send, recv).wait()
                hand_back(0, j + 1)

            cube.gather(0, j, held, send, recv).wait()

            @pl.when(i >= 2)
            def _():
                for copy in stores(group, i - 2, slot):
                    copy.wait()

            staged[slot] = held[j].astype(F32)
            for copy in stores(group, i, slot):
                copy.start()
            return carry

        lax.fori_loop(0, per, finish, 0)
        for i in (per - 2, per - 1):
            for copy in stores(group, i, i % 2):
                copy.wait()
    for one in swaps:
        one.wait()


def grads(n2, cot, inner, gg, ug, n2g, out_p):
    width = n2.shape[1]
    rows, hidden = inner[0].shape
    total = 3 * hidden // TILE
    vmem = pl.BlockSpec(memory_space=pltpu.VMEM)
    hbm = pl.BlockSpec(memory_space=pl.ANY)
    sizes = (TILE // 2, TILE // 4, TILE // 8, TILE // 16)
    return pl.pallas_call(
        grads_kernel,
        in_specs=[vmem, vmem] + [hbm] * 8,
        out_specs=[hbm] * 5,
        out_shape=[
            jax.ShapeDtypeStruct((hidden, width), F32),
            jax.ShapeDtypeStruct((width, hidden), F32),
            jax.ShapeDtypeStruct((width, hidden), F32),
            jax.ShapeDtypeStruct((rows, width), BF16),
            jax.ShapeDtypeStruct((rows, width), BF16),
        ],
        scratch_shapes=[pltpu.VMEM((total, TILE, width), BF16)]
        + [pltpu.VMEM((total, size, width), BF16) for size in sizes]
        + [
            pltpu.VMEM((2, 2 * rows, TILE), BF16),
            pltpu.VMEM((2, TILE, width), F32),
            pltpu.SemaphoreType.DMA((2, 2)),
            pltpu.SemaphoreType.DMA((2, width // TILE)),
            pltpu.SemaphoreType.DMA((8, total)),
            pltpu.SemaphoreType.DMA((8, total)),
            pltpu.SemaphoreType.DMA((2,)),
            pltpu.SemaphoreType.DMA((2,)),
            pltpu.SemaphoreType.REGULAR((4,)),
        ],
        name="grads",
        cost_estimate=pl.CostEstimate(
            flops=12 * rows * width * hidden, bytes_accessed=20 * hidden * width, transcendentals=0
        ),
        compiler_params=pltpu.CompilerParams(
            collective_id=1, has_side_effects=True, vmem_limit_bytes=60 * 2**20
        ),
    )(n2, cot, *inner, *gg, *ug, n2g, out_p)


def shift_down(values, amount):
    return jnp.pad(values, ((amount, 0), (0, 0)))[: values.shape[0]]


def shift_up(values, amount):
    return jnp.pad(values, ((0, amount), (0, 0)))[amount:]


def mixer_forward(normed, in_half, kernel_half):
    channels = in_half.shape[1] // 3
    projected = dot(normed, in_half)
    b_part = projected[:, :channels]
    c_part = projected[:, channels : 2 * channels]
    x_part = projected[:, 2 * channels :]
    mixed = b_part * x_part
    convolved = jnp.zeros_like(mixed)
    for k in range(KERNEL):
        convolved = convolved + kernel_half[k] * shift_down(mixed, KERNEL - 1 - k)
    gated = (c_part * convolved).astype(BF16)
    return b_part, c_part, x_part, mixed, convolved, gated


def quarter_gather(weight, rows_axis_quarter, dp_index):
    rows = weight.shape[0] // 4
    sliced = lax.dynamic_slice_in_dim(weight, rows_axis_quarter * rows, rows, axis=0)
    first = lax.ppermute(sliced, "tensor", [(0, 1), (1, 0)])
    n_dp = lax.axis_size("dp")
    flip_y = [(i, i ^ 2) for i in range(n_dp)]
    flip_c = [(i, i ^ 1) for i in range(n_dp)]
    from_y = lax.ppermute(first, "dp", flip_y)
    both = jnp.stack([first, from_y])
    from_c = lax.ppermute(both, "dp", flip_c)
    out = weight
    for piece, which in ((both[0], 0), (both[1], 2), (from_c[0], 1), (from_c[1], 3)):
        out = lax.dynamic_update_slice_in_dim(out, piece, (rows_axis_quarter ^ which) * rows, axis=0)
    return out


def fast(
    block_input,
    mixer_gain,
    in_weight,
    conv_kernel,
    out_weight,
    ffn_gain,
    gate_weight,
    up_weight,
    down_weight,
    output_grad,
    lengths,
):
    rows = block_input.shape[0]
    channels = in_weight.shape[2]
    me = lax.axis_index("tensor")
    dp_index = lax.axis_index("dp")
    swap = [(0, 1), (1, 0)]
    quarter = dp_index % 4

    other_input = lax.ppermute(block_input, "tensor", swap)
    in_shape = in_weight.shape
    in_weight = in_weight.reshape(in_shape[0], 3 * channels)
    in_other = quarter_gather(in_weight, quarter, dp_index)
    out_other = quarter_gather(out_weight, quarter, dp_index)
    kernel_other = lax.ppermute(conv_kernel, "tensor", swap).astype(F32)
    other_grad = lax.ppermute(output_grad, "tensor", swap)
    kernel_own = conv_kernel.astype(F32)

    position = jnp.arange(rows, dtype=jnp.int32)
    mask_own = (position < lengths[me])[:, None]
    mask_other = (position < lengths[1 - me])[:, None]
    cot_own = jnp.where(mask_own, output_grad, jnp.zeros_like(output_grad))
    cot_other = jnp.where(mask_other, other_grad, jnp.zeros_like(other_grad))

    def forward(source_low):
        source = source_low.astype(F32)
        normed, inverse = rms_forward(source, mixer_gain)
        normed = normed.astype(BF16)
        parts = [
            mixer_forward(normed, w, k)
            for w, k in ((in_weight, kernel_own), (in_other, kernel_other))
        ]
        hidden = source + (dot(parts[0][5], out_weight) + dot(parts[1][5], out_other))
        normed_two, inverse_two = rms_forward(hidden, ffn_gain)
        return source, normed, inverse, parts, hidden, normed_two.astype(BF16), inverse_two

    source, normed_one, inverse_one, parts, hidden, n2_own, inverse_two = forward(block_input)
    n2_other = forward(other_input)[5]

    inner_o, gg_o, ug_o, out_o, n2g_o = ffn(n2_own, cot_own, gate_weight, up_weight, down_weight, "ffn_own")
    inner_p, gg_p, ug_p, out_p, n2g_p = ffn(
        n2_other, cot_other, gate_weight, up_weight, down_weight, "ffn_other"
    )
    down_grad, gate_grad, up_grad, n2g_recv, out_recv = grads(
        jnp.concatenate([n2_own, n2_other]),
        jnp.concatenate([cot_own, cot_other]),
        (inner_o, inner_p),
        (gg_o, gg_p),
        (ug_o, ug_p),
        n2g_p,
        out_p,
    )

    normed_two_grad = n2g_o.astype(F32) + n2g_recv.astype(F32)
    block_output = (hidden + (out_o.astype(F32) + out_recv.astype(F32))).astype(BF16)
    through_two, ffn_gain_part = rms_backward(hidden, inverse_two, ffn_gain, normed_two_grad)
    hidden_grad = cot_own.astype(F32) + through_two
    hidden_low = hidden_grad.astype(BF16)

    normed_one_grad = 0.0
    in_grads, out_grads, kernel_grads = [], [], []
    for half, w_in, w_out, kernel in (
        (parts[0], in_weight, out_weight, kernel_own),
        (parts[1], in_other, out_other, kernel_other),
    ):
        b_part, c_part, x_part, mixed, convolved, gated = half
        gated_grad = dot(hidden_low, w_out, NT)
        out_grads.append(dot(gated, hidden_low, TN).astype(BF16))
        c_grad = gated_grad * convolved
        conv_grad = gated_grad * c_part
        mixed_grad = jnp.zeros_like(conv_grad)
        kernel_rows = []
        for k in range(KERNEL):
            back = KERNEL - 1 - k
            mixed_grad = mixed_grad + kernel[k] * shift_up(conv_grad, back)
            kernel_rows.append(jnp.sum(conv_grad * shift_down(mixed, back), axis=0))
        kernel_grads.append(jnp.stack(kernel_rows))
        projected_grad = jnp.concatenate(
            [mixed_grad * x_part, c_grad, mixed_grad * b_part], axis=1
        ).astype(BF16)
        in_grads.append(dot(normed_one, projected_grad, TN).astype(BF16))
        normed_one_grad = normed_one_grad + dot(projected_grad, w_in, NT)
    through_one, mixer_gain_part = rms_backward(source, inverse_one, mixer_gain, normed_one_grad)
    input_grad = (hidden_grad + through_one).astype(BF16)

    in_grad = in_grads[0] + lax.ppermute(in_grads[1], "tensor", swap)
    out_grad = out_grads[0] + lax.ppermute(out_grads[1], "tensor", swap)

    kernel_first = jnp.where(me == 0, kernel_grads[0], kernel_grads[1])
    kernel_second = jnp.where(me == 0, kernel_grads[1], kernel_grads[0])
    small = jnp.concatenate(
        [
            mixer_gain_part[None],
            ffn_gain_part[None],
            jnp.concatenate([kernel_first, kernel_second], axis=1),
        ],
        axis=0,
    )
    small = lax.psum(small, ("dp", "tensor"))
    conv_kernel_grad = lax.dynamic_slice_in_dim(small[2:], me * channels, channels, axis=1)

    in_grad, out_grad = [lax.psum(g, "dp").astype(F32) for g in (in_grad, out_grad)]
    return (
        block_output,
        input_grad,
        small[0],
        in_grad.reshape(in_shape),
        conv_kernel_grad,
        out_grad,
        small[1],
        gate_grad,
        up_grad,
        down_grad,
    )


def solution(mesh):
    def step(*args):
        one_slot_each = mesh.shape["tensor"] == 2 and args[10].shape[0] == 2 and mesh.shape["dp"] == 16
        return (fast if one_slot_each else local)(*args)

    return jax.shard_map(
        step,
        mesh=mesh,
        in_specs=(
            P(("dp", "tensor"), None),
            P(),
            P(None, None, "tensor"),
            P(None, "tensor"),
            P("tensor", None),
            P(),
            P(None, "tensor"),
            P(None, "tensor"),
            P("tensor", None),
            P(("dp", "tensor"), None),
            P("dp"),
        ),
        out_specs=(
            P(("dp", "tensor"), None),
            P(("dp", "tensor"), None),
            P(),
            P(None, None, "tensor"),
            P(None, "tensor"),
            P("tensor", None),
            P(),
            P(None, "tensor"),
            P(None, "tensor"),
            P("tensor", None),
        ),
        check_vma=False,
    )
```

```python
import functools

import jax
import jax.numpy as jnp
from jax import lax
from jax.experimental import pallas as pl
from jax.experimental.pallas import tpu as pltpu
from jax.sharding import PartitionSpec as P

KERNEL = 3


eps = 1e-05


def rms_forward(values, gain_values):
    inverse = lax.rsqrt(jnp.mean(values * values, axis=-1, keepdims=True) + eps)
    return (values * inverse * gain_values, inverse)


def rms_backward(values, inverse, gain_values, upstream):
    weighted = upstream * gain_values
    gain_part = jnp.sum(upstream * values * inverse, axis=0)
    through = inverse * weighted - values * inverse**3 * jnp.mean(
        weighted * values, axis=-1, keepdims=True
    )
    return (through, gain_part)


def local(
    block_input,
    mixer_gain,
    in_weight,
    conv_kernel,
    out_weight,
    ffn_gain,
    gate_weight,
    up_weight,
    down_weight,
    output_grad,
    lengths,
):
    local_rows = block_input.shape[0]
    model_width = block_input.shape[1]
    channels = in_weight.shape[2]
    slot_count = lengths.shape[0]
    source = block_input.astype(jnp.float32)
    normed_one, inverse_one = rms_forward(source, mixer_gain)
    gathered_one = lax.all_gather(normed_one.astype(jnp.bfloat16), "tensor", axis=0, tiled=True)
    group_rows = gathered_one.shape[0]
    slot_length = group_rows // slot_count
    in_flat = in_weight.reshape(model_width, 3 * channels)
    projected = jnp.dot(gathered_one, in_flat, preferred_element_type=jnp.float32).reshape(
        group_rows, 3, channels
    )
    b_part = projected[:, 0]
    c_part = projected[:, 1]
    x_part = projected[:, 2]
    mixed = (b_part * x_part).reshape(slot_count, slot_length, channels)
    kernel_values = conv_kernel.astype(jnp.float32)
    padded = jnp.pad(mixed, ((0, 0), (KERNEL - 1, 0), (0, 0)))
    convolved = jnp.zeros_like(mixed)
    for offset in range(KERNEL):
        convolved = convolved + kernel_values[offset] * padded[:, offset : offset + slot_length]
    convolved = convolved.reshape(group_rows, channels)
    gated = (c_part * convolved).astype(jnp.bfloat16)
    hidden = source + lax.psum_scatter(
        jnp.dot(gated, out_weight, preferred_element_type=jnp.float32).astype(jnp.bfloat16),
        "tensor",
        scatter_dimension=0,
        tiled=True,
    ).astype(jnp.float32)
    normed_two, inverse_two = rms_forward(hidden, ffn_gain)
    gathered_two = lax.all_gather(normed_two.astype(jnp.bfloat16), "tensor", axis=0, tiled=True)
    gate_value = jnp.dot(gathered_two, gate_weight, preferred_element_type=jnp.float32)
    up_value = jnp.dot(gathered_two, up_weight, preferred_element_type=jnp.float32)
    sigmoid_gate = jax.nn.sigmoid(gate_value)
    silu_value = gate_value * sigmoid_gate
    inner_low = (silu_value * up_value).astype(jnp.bfloat16)
    block_output = (
        hidden
        + lax.psum_scatter(
            jnp.dot(inner_low, down_weight, preferred_element_type=jnp.float32).astype(
                jnp.bfloat16
            ),
            "tensor",
            scatter_dimension=0,
            tiled=True,
        ).astype(jnp.float32)
    ).astype(jnp.bfloat16)
    row_index = lax.axis_index("tensor") * local_rows + jnp.arange(local_rows, dtype=jnp.int32)
    slot_of = row_index // slot_length
    position = row_index % slot_length
    matched = (slot_of[:, None] == jnp.arange(slot_count, dtype=jnp.int32)[None, :]) & (
        position[:, None] < lengths[None, :]
    )
    token_mask = jnp.any(matched, axis=1).astype(jnp.float32)
    cotangent = output_grad.astype(jnp.float32) * token_mask[:, None]
    grad_rows = lax.all_gather(cotangent.astype(jnp.bfloat16), "tensor", axis=0, tiled=True)
    inner_grad = jnp.einsum("rd,fd->rf", grad_rows, down_weight, preferred_element_type=jnp.float32)
    down_weight_grad = jnp.einsum(
        "rf,rd->fd", inner_low, grad_rows, preferred_element_type=jnp.float32
    )
    gate_grad = (
        inner_grad * up_value * sigmoid_gate * (1.0 + gate_value * (1.0 - sigmoid_gate))
    ).astype(jnp.bfloat16)
    up_grad = (inner_grad * silu_value).astype(jnp.bfloat16)
    gate_weight_grad = jnp.einsum(
        "rd,rf->df", gathered_two, gate_grad, preferred_element_type=jnp.float32
    )
    up_weight_grad = jnp.einsum(
        "rd,rf->df", gathered_two, up_grad, preferred_element_type=jnp.float32
    )
    from_gate = jnp.einsum("rf,df->rd", gate_grad, gate_weight, preferred_element_type=jnp.float32)
    normed_two_grad = lax.psum_scatter(
        (
            from_gate
            + jnp.einsum("rf,df->rd", up_grad, up_weight, preferred_element_type=jnp.float32)
        ).astype(jnp.bfloat16),
        "tensor",
        scatter_dimension=0,
        tiled=True,
    ).astype(jnp.float32)
    through_two, ffn_gain_part = rms_backward(hidden, inverse_two, ffn_gain, normed_two_grad)
    hidden_grad = cotangent + through_two
    hidden_rows = lax.all_gather(hidden_grad.astype(jnp.bfloat16), "tensor", axis=0, tiled=True)
    gated_grad = jnp.einsum(
        "rd,cd->rc", hidden_rows, out_weight, preferred_element_type=jnp.float32
    )
    out_weight_grad = jnp.einsum(
        "rc,rd->cd", gated, hidden_rows, preferred_element_type=jnp.float32
    )
    c_grad = gated_grad * convolved
    conv_grad = (gated_grad * c_part).reshape(slot_count, slot_length, channels)
    padded_after = jnp.pad(conv_grad, ((0, 0), (0, KERNEL - 1), (0, 0)))
    mixed_grad = jnp.zeros_like(conv_grad)
    kernel_rows = []
    for offset in range(KERNEL):
        shift_start = KERNEL - 1 - offset
        mixed_grad = (
            mixed_grad
            + kernel_values[offset] * padded_after[:, shift_start : shift_start + slot_length]
        )
        kernel_rows.append(
            jnp.sum(conv_grad * padded[:, offset : offset + slot_length], axis=(0, 1))
        )
    conv_kernel_grad = jnp.stack(kernel_rows, axis=0)
    mixed_grad = mixed_grad.reshape(group_rows, channels)
    projected_grad = jnp.stack([mixed_grad * x_part, c_grad, mixed_grad * b_part], axis=1).astype(
        jnp.bfloat16
    )
    in_weight_grad = jnp.einsum(
        "rd,rkc->dkc", gathered_one, projected_grad, preferred_element_type=jnp.float32
    )
    normed_one_grad = lax.psum_scatter(
        jnp.einsum(
            "rkc,dkc->rd", projected_grad, in_weight, preferred_element_type=jnp.float32
        ).astype(jnp.bfloat16),
        "tensor",
        scatter_dimension=0,
        tiled=True,
    ).astype(jnp.float32)
    through_one, mixer_gain_part = rms_backward(source, inverse_one, mixer_gain, normed_one_grad)
    input_grad = (hidden_grad + through_one).astype(jnp.bfloat16)
    (
        in_weight_grad,
        conv_kernel_grad,
        out_weight_grad,
        gate_weight_grad,
        up_weight_grad,
        down_weight_grad,
    ) = (
        lax.psum(in_weight_grad.astype(jnp.bfloat16), "dp").astype(jnp.float32),
        lax.psum(conv_kernel_grad.astype(jnp.bfloat16), "dp").astype(jnp.float32),
        lax.psum(out_weight_grad.astype(jnp.bfloat16), "dp").astype(jnp.float32),
        lax.psum(gate_weight_grad.astype(jnp.bfloat16), "dp").astype(jnp.float32),
        lax.psum(up_weight_grad.astype(jnp.bfloat16), "dp").astype(jnp.float32),
        lax.psum(down_weight_grad.astype(jnp.bfloat16), "dp").astype(jnp.float32),
    )
    mixer_gain_grad, ffn_gain_grad = lax.psum((mixer_gain_part, ffn_gain_part), ("dp", "tensor"))
    return (
        block_output,
        input_grad,
        mixer_gain_grad,
        in_weight_grad,
        conv_kernel_grad,
        out_weight_grad,
        ffn_gain_grad,
        gate_weight_grad,
        up_weight_grad,
        down_weight_grad,
    )


NN = (((1,), (0,)), ((), ()))
NT = (((1,), (1,)), ((), ()))
TN = (((0,), (0,)), ((), ()))
F32 = jnp.float32
BF16 = jnp.bfloat16


def dot(a, b, dims=NN):
    return lax.dot_general(a, b, dims, preferred_element_type=F32)


def ffn_kernel(n2, cot, wg, wu, wd, inner, gg, ug, out, n2g, acc1, acc2, *, rows):
    step = pl.program_id(0)

    @pl.when(step == 0)
    def _():
        acc1[...] = jnp.zeros_like(acc1)
        acc2[...] = jnp.zeros_like(acc2)

    def front(r):
        s = pl.ds(r * rows, rows)
        a, c = n2[s, :], cot[s, :]
        return dot(a, wg[...]), dot(a, wu[...]), dot(c, wd[...], NT)

    count = n2.shape[0] // rows
    held = front(0)
    for r in range(count):
        following = front(r + 1) if r + 1 < count else None
        s = pl.ds(r * rows, rows)
        g, u, ig = held
        sig = jax.nn.sigmoid(g)
        silu = g * sig
        low = (silu * u).astype(BF16)
        gg_low = (ig * u * (sig + silu * (1.0 - sig))).astype(BF16)
        ug_low = (ig * silu).astype(BF16)
        inner[s, :] = low
        gg[s, :] = gg_low
        ug[s, :] = ug_low
        acc1[s, :] += dot(low, wd[...])
        acc2[s, :] += dot(gg_low, wg[...], NT) + dot(ug_low, wu[...], NT)
        held = following

    @pl.when(step == pl.num_programs(0) - 1)
    def _():
        out[...] = acc1[...].astype(out.dtype)
        n2g[...] = acc2[...].astype(n2g.dtype)


def ffn(n2, cot, wg, wu, wd, name):
    rows, width = n2.shape
    hidden = wg.shape[1]
    tile = 256
    full = pl.BlockSpec((rows, width), lambda h: (0, 0), pipeline_mode=pl.Buffered(1))

    def col(n):
        return pl.BlockSpec((n, tile), lambda h: (0, h))

    return pl.pallas_call(
        functools.partial(ffn_kernel, rows=256),
        grid=(hidden // tile,),
        in_specs=[full, full, col(width), col(width), pl.BlockSpec((tile, width), lambda h: (h, 0))],
        out_specs=[col(rows), col(rows), col(rows), full, full],
        out_shape=[jax.ShapeDtypeStruct((rows, hidden), BF16)] * 3
        + [jax.ShapeDtypeStruct((rows, width), BF16)] * 2,
        scratch_shapes=[pltpu.VMEM((rows, width), F32)] * 2,
        name=name,
        cost_estimate=pl.CostEstimate(
            flops=12 * rows * width * hidden,
            bytes_accessed=6 * hidden * width + 6 * rows * hidden + 8 * rows * width,
            transcendentals=rows * hidden,
        ),
        compiler_params=pltpu.CompilerParams(vmem_limit_bytes=48 * 2**20),
    )(n2, cot, wg, wu, wd)


def shift_down(values, amount):
    return jnp.pad(values, ((amount, 0), (0, 0)))[: values.shape[0]]


def mixer_forward(normed, in_half, kernel_half):
    channels = in_half.shape[1] // 3
    projected = dot(normed, in_half)
    b_part = projected[:, :channels]
    c_part = projected[:, channels : 2 * channels]
    x_part = projected[:, 2 * channels :]
    mixed = b_part * x_part
    convolved = jnp.zeros_like(mixed)
    for k in range(KERNEL):
        convolved = convolved + kernel_half[k] * shift_down(mixed, KERNEL - 1 - k)
    gated = (c_part * convolved).astype(BF16)
    return jnp.concatenate([projected.astype(BF16), convolved.astype(BF16)], axis=1), gated


MESH = pl.DeviceIdType.MESH
TILE = 256
RING = 4


def enter(devices):
    barrier = pltpu.get_barrier_semaphore()
    for device in devices:
        pl.semaphore_signal(barrier, inc=1, device_id=device, device_id_type=MESH)
    pl.semaphore_wait(barrier, len(devices))


def widen(values):
    return values.astype(F32)


def back_kernel(
    gains, taps,
    cot_o, cot_p, n2_o, n2_p, inner_o, inner_p, gg_o, gg_p, ug_o, ug_p, n2g_o, n2g_p, out_p,
    hidden, source, parts_o, parts_p, in_o, in_p, out_w_o, out_w_p, n1, gated_o, gated_p,
    summed, input_grad, out_recv, small,
    ring, rc, ry, ra, rb, rx, small_recv, cot, n2, operand, in_w, pg, part, hid, ngo, ngr, src, ig, nxt, kacc,
    load_sem, fixed_sem, tile_sem, send, recv, local_sem, x_send, x_recv, small_send, small_rsem,
):
    width = cot.shape[1]
    rows = inner_o.shape[0]
    channels = gated_o.shape[1]
    ffn_chunks = 3 * inner_o.shape[1] // TILE
    own_chunks = in_o.shape[1] // TILE + channels // TILE
    in_chunks = in_o.shape[1] // TILE
    total = ffn_chunks + own_chunks
    half = width // 2
    sizes = (half, half // 2, half // 4, half // 8)

    me = lax.axis_index("dp")
    tensor = lax.axis_index("tensor")
    bits = [(me // (1 << k)) % 2 for k in range(4)]
    peers = [me + (1 << k) - (2 << k) * bits[k] for k in range(4)]
    enter([(p, tensor) for p in peers] + [(me, 1 - tensor)])

    def peer_copy(src_ref, dst_ref, send_sem, recv_sem, peer):
        return pltpu.make_async_remote_copy(
            src_ref=src_ref, dst_ref=dst_ref, send_sem=send_sem, recv_sem=recv_sem,
            device_id=(peer, tensor), device_id_type=MESH,
        )

    def x_copy(src_ref, dst_ref, k):
        return pltpu.make_async_remote_copy(
            src_ref=src_ref, dst_ref=dst_ref, send_sem=x_send.at[k], recv_sem=x_recv.at[k],
            device_id=(me, 1 - tensor), device_id_type=MESH,
        )

    def stage(j, s):
        if s == 0:
            return peers[0], pl.multiple_of(bits[0] * half, half), pl.multiple_of(half - bits[0] * half, half)
        early = SPLIT_LATE(j)
        first = jnp.where(early, bits[2], bits[1])
        second = jnp.where(early, bits[1], bits[2])
        size = sizes[s]
        if s == 1:
            base, bit, peer = 0, first, jnp.where(early, peers[2], peers[1])
        elif s == 2:
            base, bit, peer = first * sizes[1], second, jnp.where(early, peers[1], peers[2])
        else:
            base, bit, peer = first * sizes[1] + second * sizes[2], bits[3], peers[3]
        return peer, pl.multiple_of(base + bit * size, size), pl.multiple_of(base + size - bit * size, size)

    landing = (None, ry, ra, rb)

    def scatter0(q):
        peer, _, theirs = stage(0, 0)
        return peer_copy(
            ring.at[q % RING, pl.ds(theirs, half)], rc.at[q], send.at[0, q], recv.at[0, q], peer
        )

    def scatter(s, j):
        peer, _, theirs = stage(j, s)
        return peer_copy(
            rc.at[j, pl.ds(theirs, sizes[s])], landing[s].at[j], send.at[s, j], recv.at[s, j], peer
        )

    def add(s, j):
        _, mine, _ = stage(j, s)
        at = pl.ds(mine, sizes[s])
        rc[j, at, :] = (widen(rc[j, at, :]) + widen(landing[s][j])).astype(BF16)

    def region(j, s):
        _, mine, _ = stage(j, s)
        start = mine if s == 0 else mine + bits[0] * half
        return summed.at[
            pl.ds(pl.multiple_of(start, sizes[s]), sizes[s]), pl.ds(pl.multiple_of(j * TILE, TILE), TILE)
        ]

    def gather(s, j):
        peer, mine, _ = stage(j, s)
        src_ref = rc.at[j, pl.ds(mine, sizes[s])] if s == 3 else region(j, s)
        return peer_copy(src_ref, region(j, s), send.at[7 - s, j], recv.at[7 - s, j], peer)

    def keep(j):
        _, mine, _ = stage(j, 3)
        return pltpu.make_async_copy(rc.at[j, pl.ds(mine, sizes[3])], region(j, 3), local_sem.at[j])

    def when(j, what):
        @pl.when((j >= 0) & (j < total))
        def _():
            what()

    def tick(k):
        for lag, s in ((0, 1), (1, 2), (2, 3)):

            def reduce(j=k - lag, s=s):
                scatter(s, j).wait()
                add(s, j)
                if s < 3:
                    scatter(s + 1, j).start()
                else:
                    gather(3, j).start()
                    keep(j).start()

            when(k - lag, reduce)
        for lag, s in ((3, 3), (4, 2)):

            def spread(j=k - lag, s=s):
                gather(s, j).wait()
                if s == 3:
                    keep(j).wait()
                gather(s - 1, j).start()

            when(k - lag, spread)

    def finish(j):
        gather(1, j).wait()
        gather(0, j).start()

        @pl.when(j > 0)
        def _():
            gather(0, j - 1).wait()

    def ticks(low, high):
        def one(k, carry):
            tick(k)
            return carry

        lax.fori_loop(low, high, one, 0)

    def fixed(k, src_ref, dst_ref):
        return pltpu.make_async_copy(src_ref, dst_ref, fixed_sem.at[k])

    first_loads = [fixed(0, cot_o, cot.at[pl.ds(0, rows)]), fixed(1, cot_p, cot.at[pl.ds(rows, rows)])]
    second_loads = [fixed(2, n2_o, n2.at[pl.ds(0, rows)]), fixed(3, n2_p, n2.at[pl.ds(rows, rows)])]
    mixer_loads = [fixed(4, in_o, in_w.at[0]), fixed(5, in_p, in_w.at[1])]
    out_loads = [
        fixed(6, out_w_o, cot.at[pl.ds(rows, channels)]),
        fixed(7, out_w_p, cot.at[pl.ds(rows + channels, channels)]),
    ]
    late_loads = [fixed(8, n1, n2.at[pl.ds(0, rows)])]
    gated_loads = [
        fixed(9, gated_o, n2.at[pl.ds(rows, rows), pl.ds(0, channels)]),
        fixed(10, gated_p, n2.at[pl.ds(rows, rows), pl.ds(channels, channels)]),
    ]

    def start(copies):
        for copy in copies:
            copy.start()

    def wait(copies):
        for copy in copies:
            copy.wait()

    groups = ((inner_o, inner_p), (gg_o, gg_p), (ug_o, ug_p))
    per = ffn_chunks // 3

    def operands(group, i, slot):
        cols = pl.ds(pl.multiple_of(i * TILE, TILE), TILE)
        return [
            pltpu.make_async_copy(
                groups[group][k].at[:, cols], operand.at[slot, pl.ds(k * rows, rows)], load_sem.at[slot, k]
            )
            for k in range(2)
        ]

    start(first_loads)
    start(operands(0, 0, 0))
    start(second_loads)
    start(mixer_loads)

    tiles = rows // TILE

    def n2g_block(i):
        at = pl.ds(pl.multiple_of((tiles - 1 - i) * TILE, TILE), TILE)
        return x_copy(n2g_p.at[at], ngr.at[at], i)

    for i in range(tiles):
        n2g_block(i).start()
    wait(first_loads)

    def from_core(q):
        scatter0(q).wait()
        _, mine, _ = stage(0, 0)
        rc[q] = (widen(ring[q % RING, pl.ds(mine, half), :]) + widen(rc[q])).astype(BF16)

    def to_y(j):
        from_core(j)
        scatter(1, j).start()

    for group in range(3):
        if group == 1:
            wait(second_loads)
            start(out_loads)

        def compute(i, carry, group=group):
            j = group * per + i
            slot = j % 2
            wait(operands(group, i, slot))

            @pl.when(i + 1 < per)
            def _():
                start(operands(group, i + 1, 1 - slot))

            if group < 2:

                @pl.when(i + 1 == per)
                def _():
                    start(operands(group + 1, 0, 1 - slot))

            left = cot if group == 0 else n2
            ring[j % RING] = dot(left[...], operand[slot], TN).astype(BF16)
            scatter0(j).start()

            @pl.when(j > 0)
            def _():
                to_y(j - 1)

            @pl.when((j >= 8) & (j % 2 == 0))
            def _():
                tick((j - 8) // 2)

            return carry

        lax.fori_loop(0, per, compute, 0)
    start(late_loads)
    start(gated_loads)
    to_y(ffn_chunks - 1)
    done = (ffn_chunks - 1 - 8) // 2 + 1

    nxt[...] = jnp.zeros_like(nxt)
    kacc[...] = jnp.zeros_like(kacc)
    small[...] = jnp.zeros_like(small)
    wait(mixer_loads)
    wait(out_loads)

    def mixer(i, carry):
        at = pl.ds(pl.multiple_of((tiles - 1 - i) * TILE, TILE), TILE)
        loads = [
            pltpu.make_async_copy(hidden.at[at], hid, tile_sem.at[0]),
            pltpu.make_async_copy(n2g_o.at[at], ngo, tile_sem.at[1]),
            pltpu.make_async_copy(source.at[at], src, tile_sem.at[2]),
            pltpu.make_async_copy(parts_o.at[at], part.at[0], tile_sem.at[3]),
            pltpu.make_async_copy(parts_p.at[at], part.at[1], tile_sem.at[4]),
        ]
        start(loads)
        n2g_block(i).wait()
        wait(loads)
        upstream = widen(ngo[...]) + widen(ngr[at, :])
        values = hid[...]
        inverse = lax.rsqrt(jnp.mean(values * values, axis=-1, keepdims=True) + eps)
        weighted = upstream * gains[1:2, :]
        scaled = values * inverse
        small[1:2, :] += jnp.sum(upstream * scaled, axis=0, keepdims=True)
        along = jnp.mean(weighted * scaled, axis=-1, keepdims=True)
        grad = widen(cot[at, :]) + inverse * (weighted - scaled * along)
        grad_low = grad.astype(BF16)
        cot[at, :] = grad_low
        row = lax.broadcasted_iota(jnp.int32, (TILE, channels), 0)
        upstream_one = jnp.zeros((TILE, width), F32)
        for h in range(2):
            out_w = cot[pl.ds(rows + h * channels, channels), :]
            gated_grad = dot(grad_low, out_w, NT)
            b_part = widen(part[h, :, 0:channels])
            c_part = widen(part[h, :, channels : 2 * channels])
            x_part = widen(part[h, :, 2 * channels : 3 * channels])
            convolved = widen(part[h, :, 3 * channels : 4 * channels])
            conv_grad = gated_grad * c_part
            one = jnp.where(row == TILE - 1, nxt[h, 0:1, :], pltpu.roll(conv_grad, TILE - 1, 0))
            two = jnp.where(
                row == TILE - 1,
                nxt[h, 1:2, :],
                jnp.where(row == TILE - 2, nxt[h, 0:1, :], pltpu.roll(conv_grad, TILE - 2, 0)),
            )
            nxt[h, 0:2, :] = conv_grad[0:2, :]
            mixed_grad = taps[h, 2:3, :] * conv_grad + taps[h, 1:2, :] * one + taps[h, 0:1, :] * two
            mixed = b_part * x_part
            kacc[h, 0:1, :] += jnp.sum(mixed * two, axis=0, keepdims=True)
            kacc[h, 1:2, :] += jnp.sum(mixed * one, axis=0, keepdims=True)
            kacc[h, 2:3, :] += jnp.sum(mixed * conv_grad, axis=0, keepdims=True)
            low = jnp.concatenate(
                [mixed_grad * x_part, gated_grad * convolved, mixed_grad * b_part], axis=1
            ).astype(BF16)
            pg[h, at, :] = low
            upstream_one = upstream_one + dot(low, in_w[h], NT)
        values_one = widen(src[...])
        inverse_one = lax.rsqrt(jnp.mean(values_one * values_one, axis=-1, keepdims=True) + eps)
        weighted_one = upstream_one * gains[0:1, :]
        scaled_one = values_one * inverse_one
        small[0:1, :] += jnp.sum(upstream_one * scaled_one, axis=0, keepdims=True)
        along_one = jnp.mean(weighted_one * scaled_one, axis=-1, keepdims=True)
        ig[...] = (grad + inverse_one * (weighted_one - scaled_one * along_one)).astype(BF16)
        store = pltpu.make_async_copy(ig, input_grad.at[at], tile_sem.at[5])
        store.start()
        for k in range(3):
            tick(done + 3 * i + k)
        store.wait()
        return carry

    lax.fori_loop(0, tiles, mixer, 0)
    done = done + 3 * tiles
    wait(late_loads)
    wait(gated_loads)

    def piece(h, m_in, m_out):
        if m_in is not None:
            cols = pl.ds(pl.multiple_of(m_in * TILE, TILE), TILE)
            return dot(n2[0:rows, :], pg[h, :, cols], TN)
        cols = pl.ds(pl.multiple_of(h * channels + m_out * TILE, TILE), TILE)
        return dot(cot[0:rows, :], n2[rows : 2 * rows, cols], TN)

    def cross(m):
        return x_copy(rc.at[total + m], rx.at[m], tiles + m)

    def after_core(h, m):
        if h == 1:
            from_core(total + m)
            cross(m).start()
        else:
            from_core(ffn_chunks + m)

    for h in (1, 0):
        base = total if h == 1 else ffn_chunks

        def in_piece(m, carry, h=h, base=base):
            q = base + m
            ring[q % RING] = piece(h, m, None).astype(BF16)
            scatter0(q).start()

            @pl.when(m > 0)
            def _():
                after_core(h, m - 1)

            if h == 0:

                @pl.when(done + m < ffn_chunks)
                def _():
                    tick(done + m)

            return carry

        lax.fori_loop(0, in_chunks, in_piece, 0)
        for m in range(in_chunks, own_chunks):
            ring[(base + m) % RING] = piece(h, None, m - in_chunks).astype(BF16)
            scatter0(base + m).start()
            after_core(h, m - 1)
        after_core(h, own_chunks - 1)
    last_swap = x_copy(out_p, out_recv, tiles + own_chunks)
    last_swap.start()

    for h in range(2):
        cols = pl.ds(pl.multiple_of(channels * (tensor + h - 2 * tensor * h), channels), channels)
        small[2:5, cols] = kacc[h, 0:3, :]

    def small_copy(k):
        device = (peers[k], tensor) if k < 4 else (me, 1 - tensor)
        return pltpu.make_async_remote_copy(
            src_ref=small, dst_ref=small_recv.at[k], send_sem=small_send.at[k], recv_sem=small_rsem.at[k],
            device_id=device, device_id_type=MESH,
        )

    def crossed(m, carry):
        cross(m).wait()
        j = ffn_chunks + m
        rc[j] = (widen(rc[j]) + widen(rx[m])).astype(BF16)
        scatter(1, j).start()
        finish(2 * m)
        finish(2 * m + 1)
        return carry

    lax.fori_loop(0, own_chunks, crossed, 0)
    for k in range(5):
        small_copy(k).start()
        small_copy(k).wait()
        small[...] = small[...] + small_recv[k]

    first = 2 * own_chunks
    lead = 7

    def middle(j, carry):
        finish(j)
        return carry

    lax.fori_loop(first, ffn_chunks - lead, middle, 0)

    def drain(k, carry):
        tick(k)
        finish(k - lead)
        return carry

    lax.fori_loop(ffn_chunks, total + 4, drain, 0)
    lax.fori_loop(total + 4 - lead, total, middle, 0)
    gather(0, total - 1).wait()
    last_swap.wait()


def back(gains, taps, arrays, rows, width, hidden, channels):
    ffn_chunks = 3 * hidden // TILE
    own_chunks = 4 * channels // TILE
    total = ffn_chunks + own_chunks
    half = width // 2
    vmem = pl.BlockSpec(memory_space=pltpu.VMEM)
    hbm = pl.BlockSpec(memory_space=pl.ANY)

    def buffer(count, size):
        return pltpu.VMEM((count, size, TILE), BF16)

    return pl.pallas_call(
        back_kernel,
        in_specs=[vmem, vmem] + [hbm] * len(arrays),
        out_specs=[hbm, hbm, hbm, vmem],
        out_shape=[
            jax.ShapeDtypeStruct((width, total * TILE), BF16),
            jax.ShapeDtypeStruct((rows, width), BF16),
            jax.ShapeDtypeStruct((rows, width), BF16),
            jax.ShapeDtypeStruct((8, width), F32),
        ],
        scratch_shapes=[
            buffer(RING, width),
            buffer(total + own_chunks, half),
            buffer(total, half // 2),
            buffer(total, half // 4),
            buffer(total, half // 8),
            buffer(own_chunks, half),
            pltpu.VMEM((5, 8, width), F32),
            pltpu.VMEM((2 * rows, width), BF16),
            pltpu.VMEM((2 * rows, width), BF16),
            buffer(2, 2 * rows),
            pltpu.VMEM((2, width, 3 * channels), BF16),
            pltpu.VMEM((2, rows, 3 * channels), BF16),
            pltpu.VMEM((2, TILE, 4 * channels), BF16),
            pltpu.VMEM((TILE, width), F32),
            pltpu.VMEM((TILE, width), BF16),
            pltpu.VMEM((rows, width), BF16),
            pltpu.VMEM((TILE, width), BF16),
            pltpu.VMEM((TILE, width), BF16),
            pltpu.VMEM((2, 8, channels), F32),
            pltpu.VMEM((2, 8, channels), F32),
            pltpu.SemaphoreType.DMA((2, 2)),
            pltpu.SemaphoreType.DMA((11,)),
            pltpu.SemaphoreType.DMA((6,)),
            pltpu.SemaphoreType.DMA((8, total + own_chunks)),
            pltpu.SemaphoreType.DMA((8, total + own_chunks)),
            pltpu.SemaphoreType.DMA((total,)),
            pltpu.SemaphoreType.DMA((rows // TILE + own_chunks + 1,)),
            pltpu.SemaphoreType.DMA((rows // TILE + own_chunks + 1,)),
            pltpu.SemaphoreType.DMA((5,)),
            pltpu.SemaphoreType.DMA((5,)),
        ],
        name="back",
        cost_estimate=pl.CostEstimate(
            flops=12 * rows * width * hidden + 32 * rows * width * channels,
            bytes_accessed=20 * hidden * width,
            transcendentals=0,
        ),
        compiler_params=pltpu.CompilerParams(
            collective_id=1, has_side_effects=True, vmem_limit_bytes=63 * 2**20
        ),
    )(gains, taps, *arrays)


def SPLIT_LATE(j):
    return j < 0


def quarter_gather(weight, rows_axis_quarter, dp_index):
    rows = weight.shape[0] // 4
    sliced = lax.dynamic_slice_in_dim(weight, rows_axis_quarter * rows, rows, axis=0)
    first = lax.ppermute(sliced, "tensor", [(0, 1), (1, 0)])
    n_dp = lax.axis_size("dp")
    flip_y = [(i, i ^ 2) for i in range(n_dp)]
    flip_c = [(i, i ^ 1) for i in range(n_dp)]
    from_y = lax.ppermute(first, "dp", flip_y)
    both = jnp.stack([first, from_y])
    from_c = lax.ppermute(both, "dp", flip_c)
    out = weight
    for piece, which in ((both[0], 0), (both[1], 2), (from_c[0], 1), (from_c[1], 3)):
        out = lax.dynamic_update_slice_in_dim(out, piece, (rows_axis_quarter ^ which) * rows, axis=0)
    return out


def fast(
    block_input,
    mixer_gain,
    in_weight,
    conv_kernel,
    out_weight,
    ffn_gain,
    gate_weight,
    up_weight,
    down_weight,
    output_grad,
    lengths,
):
    rows = block_input.shape[0]
    channels = in_weight.shape[2]
    me = lax.axis_index("tensor")
    dp_index = lax.axis_index("dp")
    swap = [(0, 1), (1, 0)]
    quarter = dp_index % 4

    other_input = lax.ppermute(block_input, "tensor", swap)
    in_shape = in_weight.shape
    in_weight = in_weight.reshape(in_shape[0], 3 * channels)
    in_other = quarter_gather(in_weight, quarter, dp_index)
    out_other = quarter_gather(out_weight, quarter, dp_index)
    kernel_other = lax.ppermute(conv_kernel, "tensor", swap).astype(F32)
    other_grad = lax.ppermute(output_grad, "tensor", swap)
    kernel_own = conv_kernel.astype(F32)

    position = jnp.arange(rows, dtype=jnp.int32)
    mask_own = (position < lengths[me])[:, None]
    mask_other = (position < lengths[1 - me])[:, None]
    cot_own = jnp.where(mask_own, output_grad, jnp.zeros_like(output_grad))
    cot_other = jnp.where(mask_other, other_grad, jnp.zeros_like(other_grad))

    def forward(source_low):
        source = source_low.astype(F32)
        normed = rms_forward(source, mixer_gain)[0]
        normed = normed.astype(BF16)
        parts = [
            mixer_forward(normed, w, k)
            for w, k in ((in_weight, kernel_own), (in_other, kernel_other))
        ]
        hidden = source + (dot(parts[0][1], out_weight) + dot(parts[1][1], out_other))
        normed_two = rms_forward(hidden, ffn_gain)[0]
        return normed, parts, hidden, normed_two.astype(BF16)

    normed_one, parts, hidden, n2_own = forward(block_input)
    n2_other = forward(other_input)[3]

    inner_o, gg_o, ug_o, out_o, n2g_o = ffn(n2_own, cot_own, gate_weight, up_weight, down_weight, "ffn_own")
    inner_p, gg_p, ug_p, out_p, n2g_p = ffn(
        n2_other, cot_other, gate_weight, up_weight, down_weight, "ffn_other"
    )
    width, hidden_units = gate_weight.shape
    summed, input_grad, out_recv, small = back(
        jnp.stack([mixer_gain, ffn_gain]),
        jnp.stack([kernel_own, kernel_other]),
        (
            cot_own, cot_other, n2_own, n2_other, inner_o, inner_p, gg_o, gg_p, ug_o, ug_p, n2g_o, n2g_p, out_p,
            hidden, block_input, parts[0][0], parts[1][0], in_weight, in_other, out_weight, out_other,
            normed_one, parts[0][1], parts[1][1],
        ),
        rows,
        width,
        hidden_units,
        channels,
    )
    block_output = (hidden + (widen(out_o) + widen(out_recv))).astype(BF16)
    conv_kernel_grad = lax.dynamic_slice_in_dim(small[2 : 2 + KERNEL], me * channels, channels, axis=1)
    splits = [hidden_units, 2 * hidden_units, 3 * hidden_units, 3 * hidden_units + 3 * channels]
    down_grad, gate_grad, up_grad, in_grad, out_grad = jnp.split(summed, splits, axis=1)
    return (
        block_output,
        input_grad,
        small[0],
        widen(in_grad).reshape(in_shape),
        conv_kernel_grad,
        widen(out_grad.T),
        small[1],
        widen(gate_grad),
        widen(up_grad),
        widen(down_grad.T),
    )


def solution(mesh):
    def step(*args):
        one_slot_each = mesh.shape["tensor"] == 2 and args[10].shape[0] == 2 and mesh.shape["dp"] == 16
        return (fast if one_slot_each else local)(*args)

    return jax.shard_map(
        step,
        mesh=mesh,
        in_specs=(
            P(("dp", "tensor"), None),
            P(),
            P(None, None, "tensor"),
            P(None, "tensor"),
            P("tensor", None),
            P(),
            P(None, "tensor"),
            P(None, "tensor"),
            P("tensor", None),
            P(("dp", "tensor"), None),
            P("dp"),
        ),
        out_specs=(
            P(("dp", "tensor"), None),
            P(("dp", "tensor"), None),
            P(),
            P(None, None, "tensor"),
            P(None, "tensor"),
            P("tensor", None),
            P(),
            P(None, "tensor"),
            P(None, "tensor"),
            P("tensor", None),
        ),
        check_vma=False,
    )
```

```python
import functools

import jax
import jax.numpy as jnp
from jax import lax
from jax.experimental import pallas as pl
from jax.experimental.pallas import tpu as pltpu
from jax.sharding import PartitionSpec as P

KERNEL = 3


eps = 1e-05


def rms_forward(values, gain_values):
    inverse = lax.rsqrt(jnp.mean(values * values, axis=-1, keepdims=True) + eps)
    return (values * inverse * gain_values, inverse)


def rms_backward(values, inverse, gain_values, upstream):
    weighted = upstream * gain_values
    gain_part = jnp.sum(upstream * values * inverse, axis=0)
    through = inverse * weighted - values * inverse**3 * jnp.mean(
        weighted * values, axis=-1, keepdims=True
    )
    return (through, gain_part)


def local(
    block_input,
    mixer_gain,
    in_weight,
    conv_kernel,
    out_weight,
    ffn_gain,
    gate_weight,
    up_weight,
    down_weight,
    output_grad,
    lengths,
):
    local_rows = block_input.shape[0]
    model_width = block_input.shape[1]
    channels = in_weight.shape[2]
    slot_count = lengths.shape[0]
    source = block_input.astype(jnp.float32)
    normed_one, inverse_one = rms_forward(source, mixer_gain)
    gathered_one = lax.all_gather(normed_one.astype(jnp.bfloat16), "tensor", axis=0, tiled=True)
    group_rows = gathered_one.shape[0]
    slot_length = group_rows // slot_count
    in_flat = in_weight.reshape(model_width, 3 * channels)
    projected = jnp.dot(gathered_one, in_flat, preferred_element_type=jnp.float32).reshape(
        group_rows, 3, channels
    )
    b_part = projected[:, 0]
    c_part = projected[:, 1]
    x_part = projected[:, 2]
    mixed = (b_part * x_part).reshape(slot_count, slot_length, channels)
    kernel_values = conv_kernel.astype(jnp.float32)
    padded = jnp.pad(mixed, ((0, 0), (KERNEL - 1, 0), (0, 0)))
    convolved = jnp.zeros_like(mixed)
    for offset in range(KERNEL):
        convolved = convolved + kernel_values[offset] * padded[:, offset : offset + slot_length]
    convolved = convolved.reshape(group_rows, channels)
    gated = (c_part * convolved).astype(jnp.bfloat16)
    hidden = source + lax.psum_scatter(
        jnp.dot(gated, out_weight, preferred_element_type=jnp.float32).astype(jnp.bfloat16),
        "tensor",
        scatter_dimension=0,
        tiled=True,
    ).astype(jnp.float32)
    normed_two, inverse_two = rms_forward(hidden, ffn_gain)
    gathered_two = lax.all_gather(normed_two.astype(jnp.bfloat16), "tensor", axis=0, tiled=True)
    gate_value = jnp.dot(gathered_two, gate_weight, preferred_element_type=jnp.float32)
    up_value = jnp.dot(gathered_two, up_weight, preferred_element_type=jnp.float32)
    sigmoid_gate = jax.nn.sigmoid(gate_value)
    silu_value = gate_value * sigmoid_gate
    inner_low = (silu_value * up_value).astype(jnp.bfloat16)
    block_output = (
        hidden
        + lax.psum_scatter(
            jnp.dot(inner_low, down_weight, preferred_element_type=jnp.float32).astype(
                jnp.bfloat16
            ),
            "tensor",
            scatter_dimension=0,
            tiled=True,
        ).astype(jnp.float32)
    ).astype(jnp.bfloat16)
    row_index = lax.axis_index("tensor") * local_rows + jnp.arange(local_rows, dtype=jnp.int32)
    slot_of = row_index // slot_length
    position = row_index % slot_length
    matched = (slot_of[:, None] == jnp.arange(slot_count, dtype=jnp.int32)[None, :]) & (
        position[:, None] < lengths[None, :]
    )
    token_mask = jnp.any(matched, axis=1).astype(jnp.float32)
    cotangent = output_grad.astype(jnp.float32) * token_mask[:, None]
    grad_rows = lax.all_gather(cotangent.astype(jnp.bfloat16), "tensor", axis=0, tiled=True)
    inner_grad = jnp.einsum("rd,fd->rf", grad_rows, down_weight, preferred_element_type=jnp.float32)
    down_weight_grad = jnp.einsum(
        "rf,rd->fd", inner_low, grad_rows, preferred_element_type=jnp.float32
    )
    gate_grad = (
        inner_grad * up_value * sigmoid_gate * (1.0 + gate_value * (1.0 - sigmoid_gate))
    ).astype(jnp.bfloat16)
    up_grad = (inner_grad * silu_value).astype(jnp.bfloat16)
    gate_weight_grad = jnp.einsum(
        "rd,rf->df", gathered_two, gate_grad, preferred_element_type=jnp.float32
    )
    up_weight_grad = jnp.einsum(
        "rd,rf->df", gathered_two, up_grad, preferred_element_type=jnp.float32
    )
    from_gate = jnp.einsum("rf,df->rd", gate_grad, gate_weight, preferred_element_type=jnp.float32)
    normed_two_grad = lax.psum_scatter(
        (
            from_gate
            + jnp.einsum("rf,df->rd", up_grad, up_weight, preferred_element_type=jnp.float32)
        ).astype(jnp.bfloat16),
        "tensor",
        scatter_dimension=0,
        tiled=True,
    ).astype(jnp.float32)
    through_two, ffn_gain_part = rms_backward(hidden, inverse_two, ffn_gain, normed_two_grad)
    hidden_grad = cotangent + through_two
    hidden_rows = lax.all_gather(hidden_grad.astype(jnp.bfloat16), "tensor", axis=0, tiled=True)
    gated_grad = jnp.einsum(
        "rd,cd->rc", hidden_rows, out_weight, preferred_element_type=jnp.float32
    )
    out_weight_grad = jnp.einsum(
        "rc,rd->cd", gated, hidden_rows, preferred_element_type=jnp.float32
    )
    c_grad = gated_grad * convolved
    conv_grad = (gated_grad * c_part).reshape(slot_count, slot_length, channels)
    padded_after = jnp.pad(conv_grad, ((0, 0), (0, KERNEL - 1), (0, 0)))
    mixed_grad = jnp.zeros_like(conv_grad)
    kernel_rows = []
    for offset in range(KERNEL):
        shift_start = KERNEL - 1 - offset
        mixed_grad = (
            mixed_grad
            + kernel_values[offset] * padded_after[:, shift_start : shift_start + slot_length]
        )
        kernel_rows.append(
            jnp.sum(conv_grad * padded[:, offset : offset + slot_length], axis=(0, 1))
        )
    conv_kernel_grad = jnp.stack(kernel_rows, axis=0)
    mixed_grad = mixed_grad.reshape(group_rows, channels)
    projected_grad = jnp.stack([mixed_grad * x_part, c_grad, mixed_grad * b_part], axis=1).astype(
        jnp.bfloat16
    )
    in_weight_grad = jnp.einsum(
        "rd,rkc->dkc", gathered_one, projected_grad, preferred_element_type=jnp.float32
    )
    normed_one_grad = lax.psum_scatter(
        jnp.einsum(
            "rkc,dkc->rd", projected_grad, in_weight, preferred_element_type=jnp.float32
        ).astype(jnp.bfloat16),
        "tensor",
        scatter_dimension=0,
        tiled=True,
    ).astype(jnp.float32)
    through_one, mixer_gain_part = rms_backward(source, inverse_one, mixer_gain, normed_one_grad)
    input_grad = (hidden_grad + through_one).astype(jnp.bfloat16)
    (
        in_weight_grad,
        conv_kernel_grad,
        out_weight_grad,
        gate_weight_grad,
        up_weight_grad,
        down_weight_grad,
    ) = (
        lax.psum(in_weight_grad.astype(jnp.bfloat16), "dp").astype(jnp.float32),
        lax.psum(conv_kernel_grad.astype(jnp.bfloat16), "dp").astype(jnp.float32),
        lax.psum(out_weight_grad.astype(jnp.bfloat16), "dp").astype(jnp.float32),
        lax.psum(gate_weight_grad.astype(jnp.bfloat16), "dp").astype(jnp.float32),
        lax.psum(up_weight_grad.astype(jnp.bfloat16), "dp").astype(jnp.float32),
        lax.psum(down_weight_grad.astype(jnp.bfloat16), "dp").astype(jnp.float32),
    )
    mixer_gain_grad, ffn_gain_grad = lax.psum((mixer_gain_part, ffn_gain_part), ("dp", "tensor"))
    return (
        block_output,
        input_grad,
        mixer_gain_grad,
        in_weight_grad,
        conv_kernel_grad,
        out_weight_grad,
        ffn_gain_grad,
        gate_weight_grad,
        up_weight_grad,
        down_weight_grad,
    )


NN = (((1,), (0,)), ((), ()))
NT = (((1,), (1,)), ((), ()))
TN = (((0,), (0,)), ((), ()))
F32 = jnp.float32
BF16 = jnp.bfloat16


def dot(a, b, dims=NN):
    return lax.dot_general(a, b, dims, preferred_element_type=F32)


MESH = pl.DeviceIdType.MESH
TILE = 256
RING = 4


def enter(devices):
    barrier = pltpu.get_barrier_semaphore()
    for device in devices:
        pl.semaphore_signal(barrier, inc=1, device_id=device, device_id_type=MESH)
    pl.semaphore_wait(barrier, len(devices))


def widen(values):
    return values.astype(F32)


def inverse_rms(values):
    return lax.rsqrt(jnp.mean(values * values, axis=-1, keepdims=True) + eps)


STEP = 768
PASS = 512


def front_kernel(
    lengths, gains, taps_own, block_input, output_grad, in_own, out_own, gate_w, up_w, down_w,
    taps_out, cot_h, n2_h, inner_h, gg_h, ug_h, n2g_h, out_h, hidden_h, parts_o, parts_p, in_other, out_other, n1_h, gated_h,
    in_w, out_w, src, other, n1, gated, n2, cot, wg, wu, wd, inner, gg, ug, acc1, acc2, part, hid, low1, low2, prev, taps,
    load_sem, w_sem, o_sem, p_sem, h_sem, l_sem, x_send, x_recv, send, recv,
):
    rows, width = src.shape
    channels = out_own.shape[0]
    hidden_units = gate_w.shape[1]
    me = lax.axis_index("dp")
    tensor = lax.axis_index("tensor")
    bits = [(me // (1 << k)) % 2 for k in range(3)]
    peers = [me + (1 << k) - (2 << k) * bits[k] for k in range(3)]
    enter([(p, tensor) for p in peers] + [(me, 1 - tensor)])

    def x_copy(src_ref, dst_ref, k):
        return pltpu.make_async_remote_copy(
            src_ref=src_ref, dst_ref=dst_ref, send_sem=x_send.at[k], recv_sem=x_recv.at[k],
            device_id=(me, 1 - tensor), device_id_type=MESH,
        )

    units = [(in_own.at[k], in_w.at[1, k], width) for k in range(3)] + [(out_own, out_w.at[1], channels)]
    routes = [(1, 2, 0), (2, 1, 0), (2, 1, 0), (1, 2, 0)]

    def span(u, s):
        size = units[u][2]
        first, second, last = routes[u]
        if s == 0:
            start = bits[last] * (size // 2) + bits[second] * (size // 4) + bits[first] * (size // 8)
            return pl.ds(pl.multiple_of(start, size // 8), size // 8)
        if s == 1:
            start = bits[last] * (size // 2) + bits[second] * (size // 4)
            return pl.ds(pl.multiple_of(start, size // 4), size // 4)
        return pl.ds(pl.multiple_of(bits[last] * (size // 2), size // 2), size // 2)

    def cross(u):
        return x_copy(units[u][0].at[span(u, 0)], units[u][1].at[span(u, 0)], u)

    def double(u, s):
        at = span(u, s)
        return pltpu.make_async_remote_copy(
            src_ref=units[u][1].at[at], dst_ref=units[u][1].at[at],
            send_sem=send.at[u, s], recv_sem=recv.at[u, s],
            device_id=(peers[routes[u][s]], tensor), device_id_type=MESH,
        )

    blocks = [pl.ds(k * PASS, PASS) for k in range(rows // PASS)]
    taps_copy = x_copy(taps_own, taps.at[1], 4)
    input_copies = [x_copy(block_input.at[b], other.at[b], 5 + k) for k, b in enumerate(blocks)]
    grad_copies = [
        x_copy(output_grad.at[b], cot.at[pl.ds(rows + k * PASS, PASS)], 5 + len(blocks) + k)
        for k, b in enumerate(blocks)
    ]
    taps_copy.start()
    for u in range(4):
        cross(u).start()
    for copy in input_copies + grad_copies:
        copy.start()

    def load(k, src_ref, dst_ref):
        return pltpu.make_async_copy(src_ref, dst_ref, load_sem.at[k])

    first_load = load(0, block_input, src)
    own_load = load(1, in_own, in_w.at[0])
    out_load = load(2, out_own, out_w.at[0])
    cot_load = load(3, output_grad, cot.at[pl.ds(0, rows)])
    for copy in (first_load, own_load, out_load, cot_load):
        copy.start()

    steps = hidden_units // STEP

    def weights(u):
        at = pl.ds(pl.multiple_of((u % steps) * STEP, STEP), STEP)
        slot = u % 2
        return [
            pltpu.make_async_copy(gate_w.at[:, at], wg.at[slot], w_sem.at[slot, 0]),
            pltpu.make_async_copy(up_w.at[:, at], wu.at[slot], w_sem.at[slot, 1]),
            pltpu.make_async_copy(down_w.at[at], wd.at[slot], w_sem.at[slot, 2]),
        ]

    for copy in weights(0):
        copy.start()
    taps[0] = taps_own[...]
    first_load.wait()

    tiles = rows // TILE

    def tile_at(i, base=0):
        return pl.ds(pl.multiple_of(base + i * TILE, TILE), TILE)

    def normalize(i, carry):
        values = widen(src[tile_at(i), :])
        n1[tile_at(i), :] = (values * inverse_rms(values) * gains[0:1, :]).astype(BF16)
        return carry

    lax.fori_loop(0, tiles, normalize, 0)
    n1_store = load(4, n1, n1_h)
    n1_store.start()
    own_load.wait()

    row = lax.broadcasted_iota(jnp.int32, (TILE, channels), 0)

    def mix(normed, h):
        b_part, c_part, x_part = [dot(normed, in_w[h, k]) for k in range(3)]
        mixed = b_part * x_part
        last, before = prev[h, 7:8, :], prev[h, 6:7, :]
        one = jnp.where(row == 0, last, pltpu.roll(mixed, 1, 0))
        two = jnp.where(row == 0, before, jnp.where(row == 1, last, pltpu.roll(mixed, 2, 0)))
        prev[h, :, :] = mixed[TILE - 8 :, :]
        convolved = taps[h, 2:3, :] * mixed + taps[h, 1:2, :] * one + taps[h, 0:1, :] * two
        return b_part, c_part, x_part, convolved, c_part * convolved

    def part_store(h, i):
        out = parts_o if h == 0 else parts_p
        return pltpu.make_async_copy(part.at[i % 2], out.at[tile_at(i)], p_sem.at[i % 2])

    def own_half(i, h):
        pieces = mix(n1[tile_at(i), :], h)
        for k in range(4):
            part[i % 2, :, k * channels : (k + 1) * channels] = pieces[k].astype(BF16)
        gated[tile_at(i), h * channels : (h + 1) * channels] = pieces[4].astype(BF16)
        part_store(h, i).start()

    prev[...] = jnp.zeros_like(prev)
    for i in range(tiles):
        if i >= 2:
            part_store(0, i - 2).wait()
        own_half(i, 0)
        cross(i).wait()
        double(i, 0).start()
        if i >= 2:
            double(i - 2, 0).wait()
            double(i - 2, 1).start()
    for u in (2, 3):
        part_store(0, u).wait()
        double(u, 0).wait()
        double(u, 1).start()
    taps_copy.wait()
    for u in range(4):
        double(u, 1).wait()
        double(u, 2).start()

    def masked(base, length):
        def one(i, carry):
            at = tile_at(i, base)
            position = lax.broadcasted_iota(jnp.int32, (TILE, width), 0) + i * TILE
            values = widen(cot[at, :])
            cot[at, :] = jnp.where(position < length, values, jnp.zeros_like(values)).astype(BF16)
            return carry

        return one

    own_length = jnp.where(tensor == 0, lengths[0], lengths[1])
    other_length = jnp.where(tensor == 0, lengths[1], lengths[0])
    cot_load.wait()
    lax.fori_loop(0, tiles, masked(0, own_length), 0)
    cot_store = load(5, cot.at[pl.ds(0, rows)], cot_h.at[pl.ds(0, rows)])
    cot_store.start()
    out_load.wait()
    for u in range(4):
        double(u, 2).wait()
    other_stores = [load(6, in_w.at[1], in_other), load(7, out_w.at[1], out_other)]
    for copy in other_stores:
        copy.start()

    def leave_mixer(values, gated_low, at):
        hidden = values + (dot(gated_low[0], out_w[0]) + dot(gated_low[1], out_w[1]))
        n2[at, :] = (hidden * inverse_rms(hidden) * gains[1:2, :]).astype(BF16)
        return hidden

    def hid_store(i):
        return pltpu.make_async_copy(hid.at[i % 2], hidden_h.at[tile_at(i)], h_sem.at[i % 2])

    def second_half(i, carry):
        @pl.when(i >= 2)
        def _():
            part_store(1, i - 2).wait()
            hid_store(i - 2).wait()

        own_half(i, 1)
        at = tile_at(i)
        both = [gated[at, h * channels : (h + 1) * channels] for h in range(2)]
        hid[i % 2] = leave_mixer(widen(src[at, :]), both, at)
        hid_store(i).start()
        return carry

    lax.fori_loop(0, tiles, second_half, 0)
    for i in (tiles - 2, tiles - 1):
        part_store(1, i).wait()
        hid_store(i).wait()
    gated_store = load(8, gated, gated_h)
    gated_store.start()
    n2_store = load(9, n2.at[pl.ds(0, rows)], n2_h.at[pl.ds(0, rows)])
    n2_store.start()

    def stores(p, step, slot):
        at = pl.ds(pl.multiple_of(p * PASS, PASS), PASS)
        cols = pl.ds(pl.multiple_of(step * STEP, STEP), STEP)
        return [
            pltpu.make_async_copy(buf.at[slot], out.at[at, cols], o_sem.at[slot, k])
            for k, (buf, out) in enumerate(((inner, inner_h), (gg, gg_h), (ug, ug_h)))
        ]

    def low_stores(p):
        at = pl.ds(pl.multiple_of(p * PASS, PASS), PASS)
        return [
            pltpu.make_async_copy(low1, out_h.at[at], l_sem.at[0]),
            pltpu.make_async_copy(low2, n2g_h.at[at], l_sem.at[1]),
        ]

    passes = 2 * rows // PASS

    def ffn_pass(p, carry):
        acc1[...] = jnp.zeros_like(acc1)
        acc2[...] = jnp.zeros_like(acc2)

        def ffn_step(step, carry):
            u = p * steps + step
            slot = u % 2
            for copy in weights(u):
                copy.wait()

            @pl.when(u + 1 < passes * steps)
            def _():
                for copy in weights(u + 1):
                    copy.start()

            @pl.when(u >= 2)
            def _():
                for copy in stores(p, step, slot):
                    copy.wait()

            def front(r):
                at = tile_at(r, p * PASS)
                a, c = n2[at, :], cot[at, :]
                return dot(a, wg[slot]), dot(a, wu[slot]), dot(c, wd[slot], NT)

            count = PASS // TILE
            held = front(0)
            for r in range(count):
                following = front(r + 1) if r + 1 < count else None
                s = pl.ds(r * TILE, TILE)
                g, v, ig = held
                sig = jax.nn.sigmoid(g)
                silu = g * sig
                low = (silu * v).astype(BF16)
                gg_low = (ig * v * (sig + silu * (1.0 - sig))).astype(BF16)
                ug_low = (ig * silu).astype(BF16)
                inner[slot, s, :] = low
                gg[slot, s, :] = gg_low
                ug[slot, s, :] = ug_low
                acc1[s, :] += dot(low, wd[slot])
                acc2[s, :] += dot(gg_low, wg[slot], NT) + dot(ug_low, wu[slot], NT)
                held = following
            for copy in stores(p, step, slot):
                copy.start()
            return carry

        lax.fori_loop(0, steps, ffn_step, 0)

        @pl.when(p > 0)
        def _():
            for copy in low_stores(p):
                copy.wait()

        low1[...] = acc1[...].astype(BF16)
        low2[...] = acc2[...].astype(BF16)
        for copy in low_stores(p):
            copy.start()
        return carry

    lax.fori_loop(0, passes // 2, ffn_pass, 0)

    prev[...] = jnp.zeros_like(prev)
    for copy in input_copies:
        copy.wait()

    def other_tile(i, carry):
        values = widen(other[tile_at(i), :])
        normed = (values * inverse_rms(values) * gains[0:1, :]).astype(BF16)
        both = [mix(normed, h)[4].astype(BF16) for h in range(2)]
        leave_mixer(values, both, tile_at(i, rows))
        return carry

    lax.fori_loop(0, tiles, other_tile, 0)
    n2_other = load(10, n2.at[pl.ds(rows, rows)], n2_h.at[pl.ds(rows, rows)])
    n2_other.start()
    per_block = PASS // TILE
    for k, copy in enumerate(grad_copies):
        copy.wait()
        lax.fori_loop(k * per_block, (k + 1) * per_block, masked(rows, other_length), 0)
        lax.fori_loop(passes // 2 + k, passes // 2 + k + 1, ffn_pass, 0)
    cot_other = load(11, cot.at[pl.ds(rows, rows)], cot_h.at[pl.ds(rows, rows)])
    cot_other.start()
    for slot in range(2):
        for copy in stores(0, 0, slot):
            copy.wait()
    for copy in low_stores(0):
        copy.wait()
    taps_out[...] = taps[...]
    for copy in [n1_store, cot_store, gated_store, n2_store, n2_other, cot_other] + other_stores:
        copy.wait()


def front(lengths, gains, taps_own, block_input, output_grad, in_own, out_own, gate_w, up_w, down_w):
    rows, width = block_input.shape
    channels = out_own.shape[0]
    hidden_units = gate_w.shape[1]
    vmem = pl.BlockSpec(memory_space=pltpu.VMEM)
    hbm = pl.BlockSpec(memory_space=pl.ANY)

    def shaped(*shape, kind=BF16):
        return jax.ShapeDtypeStruct(shape, kind)

    both = 2 * rows
    outs = [
        shaped(2, KERNEL, channels, kind=F32),
        shaped(both, width),
        shaped(both, width),
        shaped(both, hidden_units),
        shaped(both, hidden_units),
        shaped(both, hidden_units),
        shaped(both, width),
        shaped(both, width),
        shaped(rows, width, kind=F32),
        shaped(rows, 4 * channels),
        shaped(rows, 4 * channels),
        shaped(KERNEL, width, channels),
        shaped(channels, width),
        shaped(rows, width),
        shaped(rows, 2 * channels),
    ]
    x_count = 5 + 2 * (rows // PASS)
    dma = pltpu.SemaphoreType.DMA
    return pl.pallas_call(
        front_kernel,
        in_specs=[pl.BlockSpec(memory_space=pltpu.SMEM), vmem, vmem] + [hbm] * 7,
        out_specs=[vmem] + [hbm] * 14,
        out_shape=outs,
        scratch_shapes=[
            pltpu.VMEM((2, KERNEL, width, channels), BF16),
            pltpu.VMEM((2, channels, width), BF16),
            pltpu.VMEM((rows, width), BF16),
            pltpu.VMEM((rows, width), BF16),
            pltpu.VMEM((rows, width), BF16),
            pltpu.VMEM((rows, 2 * channels), BF16),
            pltpu.VMEM((both, width), BF16),
            pltpu.VMEM((both, width), BF16),
            pltpu.VMEM((2, width, STEP), BF16),
            pltpu.VMEM((2, width, STEP), BF16),
            pltpu.VMEM((2, STEP, width), BF16),
            pltpu.VMEM((2, PASS, STEP), BF16),
            pltpu.VMEM((2, PASS, STEP), BF16),
            pltpu.VMEM((2, PASS, STEP), BF16),
            pltpu.VMEM((PASS, width), F32),
            pltpu.VMEM((PASS, width), F32),
            pltpu.VMEM((2, TILE, 4 * channels), BF16),
            pltpu.VMEM((2, TILE, width), F32),
            pltpu.VMEM((PASS, width), BF16),
            pltpu.VMEM((PASS, width), BF16),
            pltpu.VMEM((2, 8, channels), F32),
            pltpu.VMEM((2, KERNEL, channels), F32),
            dma((12,)),
            dma((2, 3)),
            dma((2, 3)),
            dma((2,)),
            dma((2,)),
            dma((2,)),
            dma((x_count,)),
            dma((x_count,)),
            dma((4, 3)),
            dma((4, 3)),
        ],
        name="front",
        cost_estimate=pl.CostEstimate(
            flops=24 * rows * width * hidden_units, bytes_accessed=40 * hidden_units * width, transcendentals=0
        ),
        compiler_params=pltpu.CompilerParams(
            collective_id=2, has_side_effects=True, vmem_limit_bytes=63 * 2**20
        ),
    )(lengths, gains, taps_own, block_input, output_grad, in_own, out_own, gate_w, up_w, down_w)


def back_kernel(
    gains, taps,
    cot_h, n2_h, inner_h, gg_h, ug_h, n2g_h, out_h,
    hidden, source, parts_o, parts_p, in_o, in_p, out_w_o, out_w_p, n1, gated,
    summed, input_grad, block_out, out_recv, small,
    ring, rc, ry, ra, rb, rx, small_recv, cot, n2, operand, in_w, pg, part, hid, ngo, ngr, src, ig, nxt, kacc,
    load_sem, fixed_sem, tile_sem, send, recv, local_sem, x_send, x_recv, small_send, small_rsem,
):
    width = cot.shape[1]
    rows = n1.shape[0]
    channels = out_w_o.shape[0]
    ffn_chunks = 3 * inner_h.shape[1] // TILE
    in_chunks = 3 * channels // TILE
    own_chunks = in_chunks + channels // TILE
    total = ffn_chunks + own_chunks
    half = width // 2
    sizes = (half, half // 2, half // 4, half // 8)

    me = lax.axis_index("dp")
    tensor = lax.axis_index("tensor")
    bits = [(me // (1 << k)) % 2 for k in range(4)]
    peers = [me + (1 << k) - (2 << k) * bits[k] for k in range(4)]
    enter([(p, tensor) for p in peers] + [(me, 1 - tensor)])

    def peer_copy(src_ref, dst_ref, send_sem, recv_sem, peer):
        return pltpu.make_async_remote_copy(
            src_ref=src_ref, dst_ref=dst_ref, send_sem=send_sem, recv_sem=recv_sem,
            device_id=(peer, tensor), device_id_type=MESH,
        )

    def x_copy(src_ref, dst_ref, k):
        return pltpu.make_async_remote_copy(
            src_ref=src_ref, dst_ref=dst_ref, send_sem=x_send.at[k], recv_sem=x_recv.at[k],
            device_id=(me, 1 - tensor), device_id_type=MESH,
        )

    def stage(j, s):
        if s == 0:
            return peers[0], pl.multiple_of(bits[0] * half, half), pl.multiple_of(half - bits[0] * half, half)
        early = SPLIT_LATE(j)
        first = jnp.where(early, bits[2], bits[1])
        second = jnp.where(early, bits[1], bits[2])
        size = sizes[s]
        if s == 1:
            base, bit, peer = 0, first, jnp.where(early, peers[2], peers[1])
        elif s == 2:
            base, bit, peer = first * sizes[1], second, jnp.where(early, peers[1], peers[2])
        else:
            base, bit, peer = first * sizes[1] + second * sizes[2], bits[3], peers[3]
        return peer, pl.multiple_of(base + bit * size, size), pl.multiple_of(base + size - bit * size, size)

    landing = (None, ry, ra, rb)

    def scatter0(q):
        peer, _, theirs = stage(0, 0)
        return peer_copy(
            ring.at[q % RING, pl.ds(theirs, half)], rc.at[q], send.at[0, q], recv.at[0, q], peer
        )

    def scatter(s, j):
        peer, _, theirs = stage(j, s)
        return peer_copy(
            rc.at[j, pl.ds(theirs, sizes[s])], landing[s].at[j], send.at[s, j], recv.at[s, j], peer
        )

    def add(s, j):
        _, mine, _ = stage(j, s)
        at = pl.ds(mine, sizes[s])
        rc[j, at, :] = (widen(rc[j, at, :]) + widen(landing[s][j])).astype(BF16)

    def region(j, s):
        _, mine, _ = stage(j, s)
        start = mine if s == 0 else mine + bits[0] * half
        return summed.at[
            pl.ds(pl.multiple_of(start, sizes[s]), sizes[s]), pl.ds(pl.multiple_of(j * TILE, TILE), TILE)
        ]

    def gather(s, j):
        peer, mine, _ = stage(j, s)
        src_ref = rc.at[j, pl.ds(mine, sizes[s])] if s == 3 else region(j, s)
        return peer_copy(src_ref, region(j, s), send.at[7 - s, j], recv.at[7 - s, j], peer)

    def keep(j):
        _, mine, _ = stage(j, 3)
        return pltpu.make_async_copy(rc.at[j, pl.ds(mine, sizes[3])], region(j, 3), local_sem.at[j])

    def when(j, what):
        @pl.when((j >= 0) & (j < total))
        def _():
            what()

    def tick(k):
        for lag, s in ((0, 1), (1, 2), (2, 3)):

            def reduce(j=k - lag, s=s):
                scatter(s, j).wait()
                add(s, j)
                if s < 3:
                    scatter(s + 1, j).start()
                else:
                    gather(3, j).start()
                    keep(j).start()

            when(k - lag, reduce)
        for lag, s in ((3, 3), (4, 2)):

            def spread(j=k - lag, s=s):
                gather(s, j).wait()
                if s == 3:
                    keep(j).wait()
                gather(s - 1, j).start()

            when(k - lag, spread)

    def finish(j):
        gather(1, j).wait()
        gather(0, j).start()

        @pl.when(j > 0)
        def _():
            gather(0, j - 1).wait()

    def ticks(low, high):
        def one(k, carry):
            tick(k)
            return carry

        lax.fori_loop(low, high, one, 0)

    def fixed(k, src_ref, dst_ref):
        return pltpu.make_async_copy(src_ref, dst_ref, fixed_sem.at[k])

    first_loads = [fixed(0, cot_h, cot)]
    second_loads = [fixed(1, n2_h, n2)]
    mixer_loads = [fixed(2, in_o, in_w.at[0]), fixed(3, in_p, in_w.at[1])]
    out_loads = [
        fixed(4, out_w_o, cot.at[pl.ds(rows, channels)]),
        fixed(5, out_w_p, cot.at[pl.ds(rows + channels, channels)]),
    ]
    late_loads = [fixed(6, n1, n2.at[pl.ds(0, rows)]), fixed(7, gated, n2.at[pl.ds(rows, rows)])]

    def start(copies):
        for copy in copies:
            copy.start()

    def wait(copies):
        for copy in copies:
            copy.wait()

    groups = (inner_h, gg_h, ug_h)
    per = ffn_chunks // 3

    def operands(group, i, slot):
        cols = pl.ds(pl.multiple_of(i * TILE, TILE), TILE)
        return [pltpu.make_async_copy(groups[group].at[:, cols], operand.at[slot], load_sem.at[slot])]

    start(first_loads)
    start(operands(0, 0, 0))
    start(second_loads)
    start(mixer_loads)

    tiles = rows // TILE

    def n2g_block(i):
        at = (tiles - 1 - i) * TILE
        return x_copy(
            n2g_h.at[pl.ds(pl.multiple_of(rows + at, TILE), TILE)],
            ngr.at[pl.ds(pl.multiple_of(at, TILE), TILE)],
            i,
        )

    for i in range(tiles):
        n2g_block(i).start()
    wait(first_loads)

    def from_core(q):
        scatter0(q).wait()
        _, mine, _ = stage(0, 0)
        rc[q] = (widen(ring[q % RING, pl.ds(mine, half), :]) + widen(rc[q])).astype(BF16)

    def to_y(j):
        from_core(j)
        scatter(1, j).start()

    for group in range(3):
        if group == 1:
            wait(second_loads)
            start(out_loads)

        def compute(i, carry, group=group):
            j = group * per + i
            slot = j % 2
            wait(operands(group, i, slot))

            @pl.when(i + 1 < per)
            def _():
                start(operands(group, i + 1, 1 - slot))

            if group < 2:

                @pl.when(i + 1 == per)
                def _():
                    start(operands(group + 1, 0, 1 - slot))

            left = cot if group == 0 else n2
            ring[j % RING] = dot(left[...], operand[slot], TN).astype(BF16)
            scatter0(j).start()

            @pl.when(j > 0)
            def _():
                to_y(j - 1)

            @pl.when((j >= 8) & (j % 2 == 0))
            def _():
                tick((j - 8) // 2)

            return carry

        lax.fori_loop(0, per, compute, 0)
    start(late_loads)
    to_y(ffn_chunks - 1)
    done = (ffn_chunks - 1 - 8) // 2 + 1

    nxt[...] = jnp.zeros_like(nxt)
    kacc[...] = jnp.zeros_like(kacc)
    small[...] = jnp.zeros_like(small)
    wait(mixer_loads)
    wait(out_loads)

    def mixer(i, carry):
        at = pl.ds(pl.multiple_of((tiles - 1 - i) * TILE, TILE), TILE)
        loads = [
            pltpu.make_async_copy(hidden.at[at], hid, tile_sem.at[0]),
            pltpu.make_async_copy(n2g_h.at[at], ngo, tile_sem.at[1]),
            pltpu.make_async_copy(source.at[at], src, tile_sem.at[2]),
            pltpu.make_async_copy(parts_o.at[at], part.at[0], tile_sem.at[3]),
            pltpu.make_async_copy(parts_p.at[at], part.at[1], tile_sem.at[4]),
        ]
        start(loads)
        n2g_block(i).wait()
        wait(loads)
        upstream = widen(ngo[...]) + widen(ngr[at, :])
        values = hid[...]
        inverse = lax.rsqrt(jnp.mean(values * values, axis=-1, keepdims=True) + eps)
        weighted = upstream * gains[1:2, :]
        scaled = values * inverse
        small[1:2, :] += jnp.sum(upstream * scaled, axis=0, keepdims=True)
        along = jnp.mean(weighted * scaled, axis=-1, keepdims=True)
        grad = widen(cot[at, :]) + inverse * (weighted - scaled * along)
        grad_low = grad.astype(BF16)
        cot[at, :] = grad_low
        row = lax.broadcasted_iota(jnp.int32, (TILE, channels), 0)
        upstream_one = jnp.zeros((TILE, width), F32)
        for h in range(2):
            out_w = cot[pl.ds(rows + h * channels, channels), :]
            gated_grad = dot(grad_low, out_w, NT)
            b_part = widen(part[h, :, 0:channels])
            c_part = widen(part[h, :, channels : 2 * channels])
            x_part = widen(part[h, :, 2 * channels : 3 * channels])
            convolved = widen(part[h, :, 3 * channels : 4 * channels])
            conv_grad = gated_grad * c_part
            one = jnp.where(row == TILE - 1, nxt[h, 0:1, :], pltpu.roll(conv_grad, TILE - 1, 0))
            two = jnp.where(
                row == TILE - 1,
                nxt[h, 1:2, :],
                jnp.where(row == TILE - 2, nxt[h, 0:1, :], pltpu.roll(conv_grad, TILE - 2, 0)),
            )
            nxt[h, 0:2, :] = conv_grad[0:2, :]
            mixed_grad = taps[h, 2:3, :] * conv_grad + taps[h, 1:2, :] * one + taps[h, 0:1, :] * two
            mixed = b_part * x_part
            kacc[h, 0:1, :] += jnp.sum(mixed * two, axis=0, keepdims=True)
            kacc[h, 1:2, :] += jnp.sum(mixed * one, axis=0, keepdims=True)
            kacc[h, 2:3, :] += jnp.sum(mixed * conv_grad, axis=0, keepdims=True)
            for k, piece_grad in enumerate((mixed_grad * x_part, gated_grad * convolved, mixed_grad * b_part)):
                low = piece_grad.astype(BF16)
                pg[h, at, k * channels : (k + 1) * channels] = low
                upstream_one = upstream_one + dot(low, in_w[h, k], NT)
        values_one = widen(src[...])
        inverse_one = lax.rsqrt(jnp.mean(values_one * values_one, axis=-1, keepdims=True) + eps)
        weighted_one = upstream_one * gains[0:1, :]
        scaled_one = values_one * inverse_one
        small[0:1, :] += jnp.sum(upstream_one * scaled_one, axis=0, keepdims=True)
        along_one = jnp.mean(weighted_one * scaled_one, axis=-1, keepdims=True)
        ig[...] = (grad + inverse_one * (weighted_one - scaled_one * along_one)).astype(BF16)
        store = pltpu.make_async_copy(ig, input_grad.at[at], tile_sem.at[5])
        store.start()
        for k in range(3):
            tick(done + 3 * i + k)
        store.wait()
        return carry

    lax.fori_loop(0, tiles, mixer, 0)
    done = done + 3 * tiles
    wait(late_loads)

    def piece(h, m_in, m_out):
        if m_in is not None:
            cols = pl.ds(pl.multiple_of(m_in * TILE, TILE), TILE)
            return dot(n2[0:rows, :], pg[h, :, cols], TN)
        cols = pl.ds(pl.multiple_of(h * channels + m_out * TILE, TILE), TILE)
        return dot(cot[0:rows, :], n2[rows : 2 * rows, cols], TN)

    def cross(m):
        return x_copy(rc.at[total + m], rx.at[m], tiles + m)

    def after_core(h, m):
        if h == 1:
            from_core(total + m)
            cross(m).start()
        else:
            from_core(ffn_chunks + m)

    for h in (1, 0):
        base = total if h == 1 else ffn_chunks

        def in_piece(m, carry, h=h, base=base):
            q = base + m
            ring[q % RING] = piece(h, m, None).astype(BF16)
            scatter0(q).start()

            @pl.when(m > 0)
            def _():
                after_core(h, m - 1)

            if h == 0:

                @pl.when(done + m < ffn_chunks)
                def _():
                    tick(done + m)

            return carry

        lax.fori_loop(0, in_chunks, in_piece, 0)
        for m in range(in_chunks, own_chunks):
            ring[(base + m) % RING] = piece(h, None, m - in_chunks).astype(BF16)
            scatter0(base + m).start()
            after_core(h, m - 1)
        after_core(h, own_chunks - 1)
    last_swap = x_copy(out_h.at[pl.ds(rows, rows)], out_recv, tiles + own_chunks)
    last_swap.start()

    for h in range(2):
        cols = pl.ds(pl.multiple_of(channels * (tensor + h - 2 * tensor * h), channels), channels)
        small[2:5, cols] = kacc[h, 0:3, :]

    def small_copy(k):
        device = (peers[k], tensor) if k < 4 else (me, 1 - tensor)
        return pltpu.make_async_remote_copy(
            src_ref=small, dst_ref=small_recv.at[k], send_sem=small_send.at[k], recv_sem=small_rsem.at[k],
            device_id=device, device_id_type=MESH,
        )

    def crossed(m, carry):
        cross(m).wait()
        j = ffn_chunks + m
        rc[j] = (widen(rc[j]) + widen(rx[m])).astype(BF16)
        scatter(1, j).start()
        finish(2 * m)
        finish(2 * m + 1)
        return carry

    lax.fori_loop(0, own_chunks, crossed, 0)
    for k in range(5):
        small_copy(k).start()
        small_copy(k).wait()
        small[...] = small[...] + small_recv[k]

    first = 2 * own_chunks
    lead = 7

    def middle(j, carry):
        finish(j)
        return carry

    lax.fori_loop(first, ffn_chunks - lead, middle, 0)

    last_swap.wait()

    def leave(i, carry):
        at = pl.ds(pl.multiple_of(i * TILE, TILE), TILE)
        loads = [
            pltpu.make_async_copy(hidden.at[at], hid, tile_sem.at[0]),
            pltpu.make_async_copy(out_h.at[at], ngo, tile_sem.at[1]),
            pltpu.make_async_copy(out_recv.at[at], src, tile_sem.at[2]),
        ]
        start(loads)
        wait(loads)
        ig[...] = (hid[...] + (widen(ngo[...]) + widen(src[...]))).astype(BF16)
        store = pltpu.make_async_copy(ig, block_out.at[at], tile_sem.at[5])
        store.start()
        store.wait()
        return carry

    lax.fori_loop(0, tiles, leave, 0)

    def drain(k, carry):
        tick(k)
        finish(k - lead)
        return carry

    lax.fori_loop(ffn_chunks, total + 4, drain, 0)
    lax.fori_loop(total + 4 - lead, total, middle, 0)
    gather(0, total - 1).wait()


def back(gains, taps, arrays, rows, width, hidden, channels):
    ffn_chunks = 3 * hidden // TILE
    own_chunks = 4 * channels // TILE
    total = ffn_chunks + own_chunks
    half = width // 2
    vmem = pl.BlockSpec(memory_space=pltpu.VMEM)
    hbm = pl.BlockSpec(memory_space=pl.ANY)

    def buffer(count, size):
        return pltpu.VMEM((count, size, TILE), BF16)

    return pl.pallas_call(
        back_kernel,
        in_specs=[vmem, vmem] + [hbm] * len(arrays),
        out_specs=[hbm, hbm, hbm, hbm, vmem],
        out_shape=[
            jax.ShapeDtypeStruct((width, total * TILE), BF16),
            jax.ShapeDtypeStruct((rows, width), BF16),
            jax.ShapeDtypeStruct((rows, width), BF16),
            jax.ShapeDtypeStruct((rows, width), BF16),
            jax.ShapeDtypeStruct((8, width), F32),
        ],
        scratch_shapes=[
            buffer(RING, width),
            buffer(total + own_chunks, half),
            buffer(total, half // 2),
            buffer(total, half // 4),
            buffer(total, half // 8),
            buffer(own_chunks, half),
            pltpu.VMEM((5, 8, width), F32),
            pltpu.VMEM((2 * rows, width), BF16),
            pltpu.VMEM((2 * rows, width), BF16),
            buffer(2, 2 * rows),
            pltpu.VMEM((2, 3, width, channels), BF16),
            pltpu.VMEM((2, rows, 3 * channels), BF16),
            pltpu.VMEM((2, TILE, 4 * channels), BF16),
            pltpu.VMEM((TILE, width), F32),
            pltpu.VMEM((TILE, width), BF16),
            pltpu.VMEM((rows, width), BF16),
            pltpu.VMEM((TILE, width), BF16),
            pltpu.VMEM((TILE, width), BF16),
            pltpu.VMEM((2, 8, channels), F32),
            pltpu.VMEM((2, 8, channels), F32),
            pltpu.SemaphoreType.DMA((2,)),
            pltpu.SemaphoreType.DMA((8,)),
            pltpu.SemaphoreType.DMA((6,)),
            pltpu.SemaphoreType.DMA((8, total + own_chunks)),
            pltpu.SemaphoreType.DMA((8, total + own_chunks)),
            pltpu.SemaphoreType.DMA((total,)),
            pltpu.SemaphoreType.DMA((rows // TILE + own_chunks + 1,)),
            pltpu.SemaphoreType.DMA((rows // TILE + own_chunks + 1,)),
            pltpu.SemaphoreType.DMA((5,)),
            pltpu.SemaphoreType.DMA((5,)),
        ],
        name="back",
        cost_estimate=pl.CostEstimate(
            flops=12 * rows * width * hidden + 32 * rows * width * channels,
            bytes_accessed=20 * hidden * width,
            transcendentals=0,
        ),
        compiler_params=pltpu.CompilerParams(
            collective_id=1, has_side_effects=True, vmem_limit_bytes=63 * 2**20
        ),
    )(gains, taps, *arrays)


def SPLIT_LATE(j):
    return j < 0


def finish_kernel(summed, down, gate, up, in_grad, out, *, per, in_count):
    j = pl.program_id(0)
    values = widen(summed[...])

    @pl.when(j < per)
    def _():
        down[...] = values.T

    @pl.when((j >= per) & (j < 2 * per))
    def _():
        gate[...] = values

    @pl.when((j >= 2 * per) & (j < 3 * per))
    def _():
        up[...] = values

    @pl.when((j >= 3 * per) & (j < 3 * per + in_count))
    def _():
        in_grad[0] = values

    @pl.when(j >= 3 * per + in_count)
    def _():
        out[...] = values.T


def finish_grads(summed, hidden_units, channels):
    width, columns = summed.shape
    per, halves = hidden_units // TILE, channels // TILE
    in_count = KERNEL * halves

    def clamp(j, low, count):
        return jnp.minimum(jnp.maximum(j - low, 0), count - 1)

    def in_map(j):
        m = clamp(j, 3 * per, in_count)
        return (m // halves, 0, m % halves)

    return pl.pallas_call(
        functools.partial(finish_kernel, per=per, in_count=in_count),
        grid=(columns // TILE,),
        in_specs=[pl.BlockSpec((width, TILE), lambda j: (0, j))],
        out_specs=[
            pl.BlockSpec((TILE, width), lambda j: (clamp(j, 0, per), 0)),
            pl.BlockSpec((width, TILE), lambda j: (0, clamp(j, per, per))),
            pl.BlockSpec((width, TILE), lambda j: (0, clamp(j, 2 * per, per))),
            pl.BlockSpec((1, width, TILE), in_map),
            pl.BlockSpec((TILE, width), lambda j: (clamp(j, 3 * per + in_count, halves), 0)),
        ],
        out_shape=[
            jax.ShapeDtypeStruct((hidden_units, width), F32),
            jax.ShapeDtypeStruct((width, hidden_units), F32),
            jax.ShapeDtypeStruct((width, hidden_units), F32),
            jax.ShapeDtypeStruct((KERNEL, width, channels), F32),
            jax.ShapeDtypeStruct((channels, width), F32),
        ],
        name="finish_grads",
        compiler_params=pltpu.CompilerParams(vmem_limit_bytes=48 * 2**20),
    )(summed)


def fast(
    block_input,
    mixer_gain,
    in_weight,
    conv_kernel,
    out_weight,
    ffn_gain,
    gate_weight,
    up_weight,
    down_weight,
    output_grad,
    lengths,
):
    rows, width = block_input.shape
    channels, hidden_units = out_weight.shape[0], gate_weight.shape[1]
    me = lax.axis_index("tensor")
    gains = jnp.stack([mixer_gain, ffn_gain])
    in_parts = jnp.transpose(in_weight, (1, 0, 2))
    taps, cot, n2, inner, gg, ug, n2g, out, hidden, parts_o, parts_p, in_other, out_other, n1, gated = front(
        lengths,
        gains,
        conv_kernel.astype(F32),
        block_input,
        output_grad,
        in_parts,
        out_weight,
        gate_weight,
        up_weight,
        down_weight,
    )
    arrays = (cot, n2, inner, gg, ug, n2g, out, hidden, block_input, parts_o, parts_p)
    arrays += (in_parts, in_other, out_weight, out_other, n1, gated)
    summed, input_grad, block_output, _, small = back(gains, taps, arrays, rows, width, hidden_units, channels)
    down_grad, gate_grad, up_grad, in_grad, out_grad = finish_grads(summed, hidden_units, channels)
    conv_kernel_grad = lax.dynamic_slice_in_dim(small[2 : 2 + KERNEL], me * channels, channels, axis=1)
    return (
        block_output,
        input_grad,
        small[0],
        jnp.transpose(in_grad, (1, 0, 2)),
        conv_kernel_grad,
        out_grad,
        small[1],
        gate_grad,
        up_grad,
        down_grad,
    )


def solution(mesh):
    def step(*args):
        rows, slots = args[0].shape[0], args[10].shape[0]
        one_slot_each = mesh.shape["tensor"] == 2 and mesh.shape["dp"] == 16 and slots == 2 and rows == 4 * TILE
        return (fast if one_slot_each else local)(*args)

    return jax.shard_map(
        step,
        mesh=mesh,
        in_specs=(
            P(("dp", "tensor"), None),
            P(),
            P(None, None, "tensor"),
            P(None, "tensor"),
            P("tensor", None),
            P(),
            P(None, "tensor"),
            P(None, "tensor"),
            P("tensor", None),
            P(("dp", "tensor"), None),
            P("dp"),
        ),
        out_specs=(
            P(("dp", "tensor"), None),
            P(("dp", "tensor"), None),
            P(),
            P(None, None, "tensor"),
            P(None, "tensor"),
            P("tensor", None),
            P(),
            P(None, "tensor"),
            P(None, "tensor"),
            P("tensor", None),
        ),
        check_vma=False,
    )
```

```python
import functools

import jax
import jax.numpy as jnp
from jax import lax
from jax.experimental import pallas as pl
from jax.experimental.pallas import tpu as pltpu
from jax.sharding import PartitionSpec as P

KERNEL = 3


eps = 1e-05


def rms_forward(values, gain_values):
    inverse = lax.rsqrt(jnp.mean(values * values, axis=-1, keepdims=True) + eps)
    return (values * inverse * gain_values, inverse)


def rms_backward(values, inverse, gain_values, upstream):
    weighted = upstream * gain_values
    gain_part = jnp.sum(upstream * values * inverse, axis=0)
    through = inverse * weighted - values * inverse**3 * jnp.mean(
        weighted * values, axis=-1, keepdims=True
    )
    return (through, gain_part)


def local(
    block_input,
    mixer_gain,
    in_weight,
    conv_kernel,
    out_weight,
    ffn_gain,
    gate_weight,
    up_weight,
    down_weight,
    output_grad,
    lengths,
):
    local_rows = block_input.shape[0]
    model_width = block_input.shape[1]
    channels = in_weight.shape[2]
    slot_count = lengths.shape[0]
    source = block_input.astype(jnp.float32)
    normed_one, inverse_one = rms_forward(source, mixer_gain)
    gathered_one = lax.all_gather(normed_one.astype(jnp.bfloat16), "tensor", axis=0, tiled=True)
    group_rows = gathered_one.shape[0]
    slot_length = group_rows // slot_count
    in_flat = in_weight.reshape(model_width, 3 * channels)
    projected = jnp.dot(gathered_one, in_flat, preferred_element_type=jnp.float32).reshape(
        group_rows, 3, channels
    )
    b_part = projected[:, 0]
    c_part = projected[:, 1]
    x_part = projected[:, 2]
    mixed = (b_part * x_part).reshape(slot_count, slot_length, channels)
    kernel_values = conv_kernel.astype(jnp.float32)
    padded = jnp.pad(mixed, ((0, 0), (KERNEL - 1, 0), (0, 0)))
    convolved = jnp.zeros_like(mixed)
    for offset in range(KERNEL):
        convolved = convolved + kernel_values[offset] * padded[:, offset : offset + slot_length]
    convolved = convolved.reshape(group_rows, channels)
    gated = (c_part * convolved).astype(jnp.bfloat16)
    hidden = source + lax.psum_scatter(
        jnp.dot(gated, out_weight, preferred_element_type=jnp.float32).astype(jnp.bfloat16),
        "tensor",
        scatter_dimension=0,
        tiled=True,
    ).astype(jnp.float32)
    normed_two, inverse_two = rms_forward(hidden, ffn_gain)
    gathered_two = lax.all_gather(normed_two.astype(jnp.bfloat16), "tensor", axis=0, tiled=True)
    gate_value = jnp.dot(gathered_two, gate_weight, preferred_element_type=jnp.float32)
    up_value = jnp.dot(gathered_two, up_weight, preferred_element_type=jnp.float32)
    sigmoid_gate = jax.nn.sigmoid(gate_value)
    silu_value = gate_value * sigmoid_gate
    inner_low = (silu_value * up_value).astype(jnp.bfloat16)
    block_output = (
        hidden
        + lax.psum_scatter(
            jnp.dot(inner_low, down_weight, preferred_element_type=jnp.float32).astype(
                jnp.bfloat16
            ),
            "tensor",
            scatter_dimension=0,
            tiled=True,
        ).astype(jnp.float32)
    ).astype(jnp.bfloat16)
    row_index = lax.axis_index("tensor") * local_rows + jnp.arange(local_rows, dtype=jnp.int32)
    slot_of = row_index // slot_length
    position = row_index % slot_length
    matched = (slot_of[:, None] == jnp.arange(slot_count, dtype=jnp.int32)[None, :]) & (
        position[:, None] < lengths[None, :]
    )
    token_mask = jnp.any(matched, axis=1).astype(jnp.float32)
    cotangent = output_grad.astype(jnp.float32) * token_mask[:, None]
    grad_rows = lax.all_gather(cotangent.astype(jnp.bfloat16), "tensor", axis=0, tiled=True)
    inner_grad = jnp.einsum("rd,fd->rf", grad_rows, down_weight, preferred_element_type=jnp.float32)
    down_weight_grad = jnp.einsum(
        "rf,rd->fd", inner_low, grad_rows, preferred_element_type=jnp.float32
    )
    gate_grad = (
        inner_grad * up_value * sigmoid_gate * (1.0 + gate_value * (1.0 - sigmoid_gate))
    ).astype(jnp.bfloat16)
    up_grad = (inner_grad * silu_value).astype(jnp.bfloat16)
    gate_weight_grad = jnp.einsum(
        "rd,rf->df", gathered_two, gate_grad, preferred_element_type=jnp.float32
    )
    up_weight_grad = jnp.einsum(
        "rd,rf->df", gathered_two, up_grad, preferred_element_type=jnp.float32
    )
    from_gate = jnp.einsum("rf,df->rd", gate_grad, gate_weight, preferred_element_type=jnp.float32)
    normed_two_grad = lax.psum_scatter(
        (
            from_gate
            + jnp.einsum("rf,df->rd", up_grad, up_weight, preferred_element_type=jnp.float32)
        ).astype(jnp.bfloat16),
        "tensor",
        scatter_dimension=0,
        tiled=True,
    ).astype(jnp.float32)
    through_two, ffn_gain_part = rms_backward(hidden, inverse_two, ffn_gain, normed_two_grad)
    hidden_grad = cotangent + through_two
    hidden_rows = lax.all_gather(hidden_grad.astype(jnp.bfloat16), "tensor", axis=0, tiled=True)
    gated_grad = jnp.einsum(
        "rd,cd->rc", hidden_rows, out_weight, preferred_element_type=jnp.float32
    )
    out_weight_grad = jnp.einsum(
        "rc,rd->cd", gated, hidden_rows, preferred_element_type=jnp.float32
    )
    c_grad = gated_grad * convolved
    conv_grad = (gated_grad * c_part).reshape(slot_count, slot_length, channels)
    padded_after = jnp.pad(conv_grad, ((0, 0), (0, KERNEL - 1), (0, 0)))
    mixed_grad = jnp.zeros_like(conv_grad)
    kernel_rows = []
    for offset in range(KERNEL):
        shift_start = KERNEL - 1 - offset
        mixed_grad = (
            mixed_grad
            + kernel_values[offset] * padded_after[:, shift_start : shift_start + slot_length]
        )
        kernel_rows.append(
            jnp.sum(conv_grad * padded[:, offset : offset + slot_length], axis=(0, 1))
        )
    conv_kernel_grad = jnp.stack(kernel_rows, axis=0)
    mixed_grad = mixed_grad.reshape(group_rows, channels)
    projected_grad = jnp.stack([mixed_grad * x_part, c_grad, mixed_grad * b_part], axis=1).astype(
        jnp.bfloat16
    )
    in_weight_grad = jnp.einsum(
        "rd,rkc->dkc", gathered_one, projected_grad, preferred_element_type=jnp.float32
    )
    normed_one_grad = lax.psum_scatter(
        jnp.einsum(
            "rkc,dkc->rd", projected_grad, in_weight, preferred_element_type=jnp.float32
        ).astype(jnp.bfloat16),
        "tensor",
        scatter_dimension=0,
        tiled=True,
    ).astype(jnp.float32)
    through_one, mixer_gain_part = rms_backward(source, inverse_one, mixer_gain, normed_one_grad)
    input_grad = (hidden_grad + through_one).astype(jnp.bfloat16)
    (
        in_weight_grad,
        conv_kernel_grad,
        out_weight_grad,
        gate_weight_grad,
        up_weight_grad,
        down_weight_grad,
    ) = (
        lax.psum(in_weight_grad.astype(jnp.bfloat16), "dp").astype(jnp.float32),
        lax.psum(conv_kernel_grad.astype(jnp.bfloat16), "dp").astype(jnp.float32),
        lax.psum(out_weight_grad.astype(jnp.bfloat16), "dp").astype(jnp.float32),
        lax.psum(gate_weight_grad.astype(jnp.bfloat16), "dp").astype(jnp.float32),
        lax.psum(up_weight_grad.astype(jnp.bfloat16), "dp").astype(jnp.float32),
        lax.psum(down_weight_grad.astype(jnp.bfloat16), "dp").astype(jnp.float32),
    )
    mixer_gain_grad, ffn_gain_grad = lax.psum((mixer_gain_part, ffn_gain_part), ("dp", "tensor"))
    return (
        block_output,
        input_grad,
        mixer_gain_grad,
        in_weight_grad,
        conv_kernel_grad,
        out_weight_grad,
        ffn_gain_grad,
        gate_weight_grad,
        up_weight_grad,
        down_weight_grad,
    )


NN = (((1,), (0,)), ((), ()))
NT = (((1,), (1,)), ((), ()))
TN = (((0,), (0,)), ((), ()))
F32 = jnp.float32
BF16 = jnp.bfloat16


def dot(a, b, dims=NN):
    return lax.dot_general(a, b, dims, preferred_element_type=F32)


MESH = pl.DeviceIdType.MESH
TILE = 256
RING = 4
LAG = 2
LAGS = (2, 3, 5, 6)


def enter(devices):
    barrier = pltpu.get_barrier_semaphore()
    for device in devices:
        pl.semaphore_signal(barrier, inc=1, device_id=device, device_id_type=MESH)
    pl.semaphore_wait(barrier, len(devices))


def widen(values):
    return values.astype(F32)


def inverse_rms(values):
    return lax.rsqrt(jnp.mean(values * values, axis=-1, keepdims=True) + eps)


STEP = 768
PASS = 512


def front_kernel(
    lengths, gain_one, gain_two, taps_own, block_input, output_grad, in_own, out_own, gate_w, up_w, down_w,
    taps_out, cot_h, n2_h, inner_h, gg_h, ug_h, n2g_h, out_h, hidden_h, parts_o, parts_p, in_other, out_other, n1_h, gated_h,
    in_w, out_w, src, other, n1, gated, n2, cot, wg, wu, wd, inner, gg, ug, acc1, acc2, part, hid, low1, low2, prev, taps, taps_low,
    load_sem, w_sem, o_sem, p_sem, h_sem, l_sem, x_send, x_recv, send, recv,
):
    rows, width = src.shape
    channels = out_own.shape[0]
    hidden_units = gate_w.shape[1]
    me = lax.axis_index("dp")
    tensor = lax.axis_index("tensor")
    bits = [(me // (1 << k)) % 2 for k in range(3)]
    peers = [me + (1 << k) - (2 << k) * bits[k] for k in range(3)]
    enter([(p, tensor) for p in peers] + [(me, 1 - tensor)])

    def x_copy(src_ref, dst_ref, k):
        return pltpu.make_async_remote_copy(
            src_ref=src_ref, dst_ref=dst_ref, send_sem=x_send.at[k], recv_sem=x_recv.at[k],
            device_id=(me, 1 - tensor), device_id_type=MESH,
        )

    units = [(in_own.at[k], in_w.at[1, k], width) for k in range(3)] + [(out_own, out_w.at[1], channels)]
    routes = [(1, 2, 0), (2, 1, 0), (2, 1, 0), (1, 2, 0)]

    def span(u, s):
        size = units[u][2]
        first, second, last = routes[u]
        if s == 0:
            start = bits[last] * (size // 2) + bits[second] * (size // 4) + bits[first] * (size // 8)
            return pl.ds(pl.multiple_of(start, size // 8), size // 8)
        if s == 1:
            start = bits[last] * (size // 2) + bits[second] * (size // 4)
            return pl.ds(pl.multiple_of(start, size // 4), size // 4)
        return pl.ds(pl.multiple_of(bits[last] * (size // 2), size // 2), size // 2)

    def cross(u):
        return x_copy(units[u][0].at[span(u, 0)], units[u][1].at[span(u, 0)], u)

    def double(u, s):
        at = span(u, s)
        return pltpu.make_async_remote_copy(
            src_ref=units[u][1].at[at], dst_ref=units[u][1].at[at],
            send_sem=send.at[u, s], recv_sem=recv.at[u, s],
            device_id=(peers[routes[u][s]], tensor), device_id_type=MESH,
        )

    blocks = [pl.ds(k * PASS, PASS) for k in range(rows // PASS)]
    taps_copy = x_copy(taps_own, taps_low, 4)
    input_copies = [x_copy(block_input.at[b], other.at[b], 5 + k) for k, b in enumerate(blocks)]
    grad_copies = [
        x_copy(output_grad.at[b], cot.at[pl.ds(rows + k * PASS, PASS)], 5 + len(blocks) + k)
        for k, b in enumerate(blocks)
    ]
    taps_copy.start()
    for u in range(4):
        cross(u).start()
    for copy in input_copies + grad_copies:
        copy.start()

    def load(k, src_ref, dst_ref):
        return pltpu.make_async_copy(src_ref, dst_ref, load_sem.at[k])

    first_load = load(0, block_input, src)
    own_load = load(1, in_own, in_w.at[0])
    out_load = load(2, out_own, out_w.at[0])
    cot_load = load(3, output_grad, cot.at[pl.ds(0, rows)])
    for copy in (first_load, own_load, out_load, cot_load):
        copy.start()

    steps = hidden_units // STEP

    def weights(u):
        at = pl.ds(pl.multiple_of((u % steps) * STEP, STEP), STEP)
        slot = u % 2
        return [
            pltpu.make_async_copy(gate_w.at[:, at], wg.at[slot], w_sem.at[slot, 0]),
            pltpu.make_async_copy(up_w.at[:, at], wu.at[slot], w_sem.at[slot, 1]),
            pltpu.make_async_copy(down_w.at[at], wd.at[slot], w_sem.at[slot, 2]),
        ]

    for copy in weights(0):
        copy.start()
    taps[0] = widen(taps_own[...])
    first_load.wait()

    tiles = rows // TILE

    def tile_at(i, base=0):
        return pl.ds(pl.multiple_of(base + i * TILE, TILE), TILE)

    def normalize(i, carry):
        values = widen(src[tile_at(i), :])
        n1[tile_at(i), :] = (values * inverse_rms(values) * gain_one[...]).astype(BF16)
        return carry

    lax.fori_loop(0, tiles, normalize, 0)
    n1_store = load(4, n1, n1_h)
    n1_store.start()
    own_load.wait()

    row = lax.broadcasted_iota(jnp.int32, (TILE, channels), 0)

    def mix(normed, h):
        b_part, c_part, x_part = [dot(normed, in_w[h, k]) for k in range(3)]
        mixed = b_part * x_part
        last, before = prev[h, 7:8, :], prev[h, 6:7, :]
        one = jnp.where(row == 0, last, pltpu.roll(mixed, 1, 0))
        two = jnp.where(row == 0, before, jnp.where(row == 1, last, pltpu.roll(mixed, 2, 0)))
        prev[h, :, :] = mixed[TILE - 8 :, :]
        convolved = taps[h, 2:3, :] * mixed + taps[h, 1:2, :] * one + taps[h, 0:1, :] * two
        return b_part, c_part, x_part, convolved, c_part * convolved

    def part_store(h, i):
        out = parts_o if h == 0 else parts_p
        return pltpu.make_async_copy(part.at[i % 2], out.at[tile_at(i)], p_sem.at[i % 2])

    def own_half(i, h):
        pieces = mix(n1[tile_at(i), :], h)
        for k in range(4):
            part[i % 2, :, k * channels : (k + 1) * channels] = pieces[k].astype(BF16)
        gated[tile_at(i), h * channels : (h + 1) * channels] = pieces[4].astype(BF16)
        part_store(h, i).start()

    prev[...] = jnp.zeros_like(prev)
    for i in range(tiles):
        if i >= 2:
            part_store(0, i - 2).wait()
        own_half(i, 0)
        cross(i).wait()
        double(i, 0).start()
        if i >= 2:
            double(i - 2, 0).wait()
            double(i - 2, 1).start()
    for u in (2, 3):
        part_store(0, u).wait()
        double(u, 0).wait()
        double(u, 1).start()
    taps_copy.wait()
    taps[1] = widen(taps_low[...])
    for u in range(4):
        double(u, 1).wait()
        double(u, 2).start()

    def masked(base, length):
        def one(i, carry):
            at = tile_at(i, base)
            position = lax.broadcasted_iota(jnp.int32, (TILE, width), 0) + i * TILE
            values = widen(cot[at, :])
            cot[at, :] = jnp.where(position < length, values, jnp.zeros_like(values)).astype(BF16)
            return carry

        return one

    own_length = jnp.where(tensor == 0, lengths[0], lengths[1])
    other_length = jnp.where(tensor == 0, lengths[1], lengths[0])
    cot_load.wait()
    lax.fori_loop(0, tiles, masked(0, own_length), 0)
    cot_store = load(5, cot.at[pl.ds(0, rows)], cot_h.at[pl.ds(0, rows)])
    cot_store.start()
    out_load.wait()
    for u in range(4):
        double(u, 2).wait()
    other_stores = [load(6, in_w.at[1], in_other), load(7, out_w.at[1], out_other)]
    for copy in other_stores:
        copy.start()

    def leave_mixer(values, gated_low, at):
        hidden = values + (dot(gated_low[0], out_w[0]) + dot(gated_low[1], out_w[1]))
        n2[at, :] = (hidden * inverse_rms(hidden) * gain_two[...]).astype(BF16)
        return hidden

    def hid_store(i):
        return pltpu.make_async_copy(hid.at[i % 2], hidden_h.at[tile_at(i)], h_sem.at[i % 2])

    def second_half(i, carry):
        @pl.when(i >= 2)
        def _():
            part_store(1, i - 2).wait()
            hid_store(i - 2).wait()

        own_half(i, 1)
        at = tile_at(i)
        both = [gated[at, h * channels : (h + 1) * channels] for h in range(2)]
        hid[i % 2] = leave_mixer(widen(src[at, :]), both, at)
        hid_store(i).start()
        return carry

    lax.fori_loop(0, tiles, second_half, 0)
    for i in (tiles - 2, tiles - 1):
        part_store(1, i).wait()
        hid_store(i).wait()
    gated_store = load(8, gated, gated_h)
    gated_store.start()
    n2_store = load(9, n2.at[pl.ds(0, rows)], n2_h.at[pl.ds(0, rows)])
    n2_store.start()

    def stores(p, step, slot):
        at = pl.ds(pl.multiple_of(p * PASS, PASS), PASS)
        cols = pl.ds(pl.multiple_of(step * STEP, STEP), STEP)
        return [
            pltpu.make_async_copy(buf.at[slot], out.at[at, cols], o_sem.at[slot, k])
            for k, (buf, out) in enumerate(((inner, inner_h), (gg, gg_h), (ug, ug_h)))
        ]

    def low_stores(p):
        at = pl.ds(pl.multiple_of(p * PASS, PASS), PASS)
        return [
            pltpu.make_async_copy(low1, out_h.at[at], l_sem.at[0]),
            pltpu.make_async_copy(low2, n2g_h.at[at], l_sem.at[1]),
        ]

    passes = 2 * rows // PASS

    def ffn_pass(p, carry):
        acc1[...] = jnp.zeros_like(acc1)
        acc2[...] = jnp.zeros_like(acc2)

        def ffn_step(step, carry):
            u = p * steps + step
            slot = u % 2
            for copy in weights(u):
                copy.wait()

            @pl.when(u + 1 < passes * steps)
            def _():
                for copy in weights(u + 1):
                    copy.start()

            @pl.when(u >= 2)
            def _():
                for copy in stores(p, step, slot):
                    copy.wait()

            def front(r):
                at = tile_at(r, p * PASS)
                a, c = n2[at, :], cot[at, :]
                return dot(a, wg[slot]), dot(a, wu[slot]), dot(c, wd[slot], NT)

            count = PASS // TILE
            held = front(0)
            for r in range(count):
                following = front(r + 1) if r + 1 < count else None
                s = pl.ds(r * TILE, TILE)
                g, v, ig = held
                sig = jax.nn.sigmoid(g)
                silu = g * sig
                low = (silu * v).astype(BF16)
                gg_low = (ig * v * (sig + silu * (1.0 - sig))).astype(BF16)
                ug_low = (ig * silu).astype(BF16)
                inner[slot, s, :] = low
                gg[slot, s, :] = gg_low
                ug[slot, s, :] = ug_low
                acc1[s, :] += dot(low, wd[slot])
                acc2[s, :] += dot(gg_low, wg[slot], NT) + dot(ug_low, wu[slot], NT)
                held = following
            for copy in stores(p, step, slot):
                copy.start()
            return carry

        lax.fori_loop(0, steps, ffn_step, 0)

        @pl.when(p > 0)
        def _():
            for copy in low_stores(p):
                copy.wait()

        low1[...] = acc1[...].astype(BF16)
        low2[...] = acc2[...].astype(BF16)
        for copy in low_stores(p):
            copy.start()
        return carry

    lax.fori_loop(0, passes // 2, ffn_pass, 0)

    prev[...] = jnp.zeros_like(prev)
    for copy in input_copies:
        copy.wait()

    def other_tile(i, carry):
        values = widen(other[tile_at(i), :])
        normed = (values * inverse_rms(values) * gain_one[...]).astype(BF16)
        both = [mix(normed, h)[4].astype(BF16) for h in range(2)]
        leave_mixer(values, both, tile_at(i, rows))
        return carry

    lax.fori_loop(0, tiles, other_tile, 0)
    n2_other = load(10, n2.at[pl.ds(rows, rows)], n2_h.at[pl.ds(rows, rows)])
    n2_other.start()
    per_block = PASS // TILE
    for k, copy in enumerate(grad_copies):
        copy.wait()
        lax.fori_loop(k * per_block, (k + 1) * per_block, masked(rows, other_length), 0)
        lax.fori_loop(passes // 2 + k, passes // 2 + k + 1, ffn_pass, 0)
    cot_other = load(11, cot.at[pl.ds(rows, rows)], cot_h.at[pl.ds(rows, rows)])
    cot_other.start()
    for slot in range(2):
        for copy in stores(0, 0, slot):
            copy.wait()
    for copy in low_stores(0):
        copy.wait()
    taps_out[...] = taps[...]
    for copy in [n1_store, cot_store, gated_store, n2_store, n2_other, cot_other] + other_stores:
        copy.wait()


def front(lengths, gains, taps_own, block_input, output_grad, in_own, out_own, gate_w, up_w, down_w):
    rows, width = block_input.shape
    channels = out_own.shape[0]
    hidden_units = gate_w.shape[1]
    vmem = pl.BlockSpec(memory_space=pltpu.VMEM)
    hbm = pl.BlockSpec(memory_space=pl.ANY)

    def shaped(*shape, kind=BF16):
        return jax.ShapeDtypeStruct(shape, kind)

    both = 2 * rows
    outs = [
        shaped(2, KERNEL, channels, kind=F32),
        shaped(both, width),
        shaped(both, width),
        shaped(both, hidden_units),
        shaped(both, hidden_units),
        shaped(both, hidden_units),
        shaped(both, width),
        shaped(both, width),
        shaped(rows, width, kind=F32),
        shaped(rows, 4 * channels),
        shaped(rows, 4 * channels),
        shaped(KERNEL, width, channels),
        shaped(channels, width),
        shaped(rows, width),
        shaped(rows, 2 * channels),
    ]
    x_count = 5 + 2 * (rows // PASS)
    dma = pltpu.SemaphoreType.DMA
    return pl.pallas_call(
        front_kernel,
        in_specs=[pl.BlockSpec(memory_space=pltpu.SMEM), vmem, vmem, vmem] + [hbm] * 7,
        out_specs=[vmem] + [hbm] * 14,
        out_shape=outs,
        scratch_shapes=[
            pltpu.VMEM((2, KERNEL, width, channels), BF16),
            pltpu.VMEM((2, channels, width), BF16),
            pltpu.VMEM((rows, width), BF16),
            pltpu.VMEM((rows, width), BF16),
            pltpu.VMEM((rows, width), BF16),
            pltpu.VMEM((rows, 2 * channels), BF16),
            pltpu.VMEM((both, width), BF16),
            pltpu.VMEM((both, width), BF16),
            pltpu.VMEM((2, width, STEP), BF16),
            pltpu.VMEM((2, width, STEP), BF16),
            pltpu.VMEM((2, STEP, width), BF16),
            pltpu.VMEM((2, PASS, STEP), BF16),
            pltpu.VMEM((2, PASS, STEP), BF16),
            pltpu.VMEM((2, PASS, STEP), BF16),
            pltpu.VMEM((PASS, width), F32),
            pltpu.VMEM((PASS, width), F32),
            pltpu.VMEM((2, TILE, 4 * channels), BF16),
            pltpu.VMEM((2, TILE, width), F32),
            pltpu.VMEM((PASS, width), BF16),
            pltpu.VMEM((PASS, width), BF16),
            pltpu.VMEM((2, 8, channels), F32),
            pltpu.VMEM((2, KERNEL, channels), F32),
            pltpu.VMEM((KERNEL, channels), BF16),
            dma((12,)),
            dma((2, 3)),
            dma((2, 3)),
            dma((2,)),
            dma((2,)),
            dma((2,)),
            dma((x_count,)),
            dma((x_count,)),
            dma((4, 3)),
            dma((4, 3)),
        ],
        name="front",
        cost_estimate=pl.CostEstimate(
            flops=24 * rows * width * hidden_units, bytes_accessed=40 * hidden_units * width, transcendentals=0
        ),
        compiler_params=pltpu.CompilerParams(
            collective_id=2, has_side_effects=True, vmem_limit_bytes=63 * 2**20
        ),
    )(lengths, *gains, taps_own, block_input, output_grad, in_own, out_own, gate_w, up_w, down_w)


def back_kernel(
    gain_one, gain_two, taps,
    cot_h, n2_h, inner_h, gg_h, ug_h, n2g_h, out_h,
    hidden, source, parts_o, parts_p, in_o, in_p, out_w_o, out_w_p, n1, gated,
    summed, input_grad, block_out, out_recv, small,
    ring, rc, ry, ra, rb, rx, small_recv, cot, n2, operand, in_w, pg, part, hid, ngo, ngr, src, ig, nxt, kacc,
    load_sem, fixed_sem, tile_sem, send, recv, local_sem, x_send, x_recv, small_send, small_rsem,
):
    width = cot.shape[1]
    rows = n1.shape[0]
    channels = out_w_o.shape[0]
    ffn_chunks = 3 * inner_h.shape[1] // TILE
    in_chunks = 3 * channels // TILE
    own_chunks = in_chunks + channels // TILE
    total = ffn_chunks + own_chunks
    half = width // 2

    me = lax.axis_index("dp")
    tensor = lax.axis_index("tensor")
    bits = [(me // (1 << k)) % 2 for k in range(4)]
    peers = [me + (1 << k) - (2 << k) * bits[k] for k in range(4)]
    z = me // 4
    mirror = me + 4 * (3 - 2 * z)
    inner_z = (z == 1) | (z == 2)
    outer_z = (z == 0) | (z == 3)
    enter([(p, tensor) for p in peers] + [(mirror, tensor), (me, 1 - tensor)])

    def peer_copy(src_ref, dst_ref, slot, j, peer):
        return pltpu.make_async_remote_copy(
            src_ref=src_ref, dst_ref=dst_ref, send_sem=send.at[slot, j], recv_sem=recv.at[slot, j],
            device_id=(peer, tensor), device_id_type=MESH,
        )

    def x_copy(src_ref, dst_ref, k):
        return pltpu.make_async_remote_copy(
            src_ref=src_ref, dst_ref=dst_ref, send_sem=x_send.at[k], recv_sem=x_recv.at[k],
            device_id=(me, 1 - tensor), device_id_type=MESH,
        )

    def rows_at(start, size):
        return pl.ds(pl.multiple_of(start, size), size)

    quarter, eighth = half // 2, half // 4
    core_at = rows_at(bits[0] * half, half)
    core_away = rows_at((1 - bits[0]) * half, half)
    y_at = rows_at(bits[1] * quarter, quarter)
    y_away = rows_at((1 - bits[1]) * quarter, quarter)
    z_at = rows_at(bits[1] * quarter + bits[3] * eighth, eighth)
    z_away = rows_at(bits[1] * quarter + (1 - bits[3]) * eighth, eighth)

    def result(j, start, size):
        return summed.at[rows_at(start, size), rows_at(j * TILE, TILE)]

    def result_y(j):
        return result(j, bits[0] * half + bits[1] * quarter, quarter)

    def result_z(j, side):
        return result(j, bits[0] * half + bits[1] * quarter + side * eighth, eighth)

    def scatter0(q):
        return peer_copy(ring.at[q % RING, core_away], rc.at[q], 0, q, peers[0])

    def scatter_y(j):
        return peer_copy(rc.at[j, y_away], ry.at[j], 1, j, peers[1])

    def up(j):
        return peer_copy(rc.at[j, y_at], ra.at[j], 2, j, peers[2])

    def across(j):
        return peer_copy(rc.at[j, z_away], rb.at[j], 3, j, mirror)

    def keep(j):
        return pltpu.make_async_copy(rc.at[j, z_at], result_z(j, bits[3]), local_sem.at[j])

    def gather_across(j):
        return peer_copy(rc.at[j, z_at], result_z(j, bits[3]), 4, j, mirror)

    def down_own(j):
        return peer_copy(rc.at[j, z_at], result_z(j, bits[3]), 5, j, peers[2])

    def down_other(j):
        return peer_copy(result_z(j, 1 - bits[3]), result_z(j, 1 - bits[3]), 6, j, peers[2])

    def gather_y(j):
        return peer_copy(result_y(j), result_y(j), 7, j, peers[1])

    def gather_core(j):
        at = result(j, bits[0] * half, half)
        return peer_copy(at, at, 8, j, peers[0])

    def add(j, at, landed):
        rc[j, at, :] = (widen(rc[j, at, :]) + widen(landed[j])).astype(BF16)

    def when(j, also, what):
        inside = (j >= 0) & (j < total)

        @pl.when(inside if also is None else inside & also)
        def _():
            what(j)

    def tick(k):
        def from_y(j):
            scatter_y(j).wait()
            add(j, y_at, ry)

            @pl.when(outer_z)
            def _():
                up(j).start()

        def from_outer(j):
            up(j).wait_recv()
            add(j, y_at, ra)
            across(j).start()

        def from_inner(j):
            across(j).wait()
            add(j, z_at, rb)
            gather_across(j).start()
            down_own(j).start()
            keep(j).start()

        def to_outer(j):
            gather_across(j).wait()
            keep(j).wait()
            down_other(j).start()

        def to_y_again(j):
            @pl.when(inner_z)
            def _():
                down_own(j).wait_send()

            @pl.when(outer_z)
            def _():
                up(j).wait_send()
                down_own(j).wait_recv()
                down_other(j).wait_recv()

            gather_y(j).start()

        when(k, None, from_y)
        when(k - LAGS[0], inner_z, from_outer)
        when(k - LAGS[1], inner_z, from_inner)
        when(k - LAGS[2], inner_z, to_outer)
        when(k - LAGS[3], None, to_y_again)

    def finish(j):
        gather_y(j).wait()
        gather_core(j).start()

    def ticks(low, high):
        def one(k, carry):
            tick(k)
            return carry

        lax.fori_loop(low, high, one, 0)

    def fixed(k, src_ref, dst_ref):
        return pltpu.make_async_copy(src_ref, dst_ref, fixed_sem.at[k])

    first_loads = [fixed(0, cot_h, cot)]
    second_loads = [fixed(1, n2_h, n2)]
    mixer_loads = [fixed(2, in_o, in_w.at[0]), fixed(3, in_p, in_w.at[1])]
    out_loads = [
        fixed(4, out_w_o, cot.at[pl.ds(rows, channels)]),
        fixed(5, out_w_p, cot.at[pl.ds(rows + channels, channels)]),
    ]
    late_loads = [fixed(6, n1, n2.at[pl.ds(0, rows)]), fixed(7, gated, n2.at[pl.ds(rows, rows)])]

    def start(copies):
        for copy in copies:
            copy.start()

    def wait(copies):
        for copy in copies:
            copy.wait()

    groups = (inner_h, gg_h, ug_h)
    per = ffn_chunks // 3

    def operands(group, i, slot):
        cols = pl.ds(pl.multiple_of(i * TILE, TILE), TILE)
        return [pltpu.make_async_copy(groups[group].at[:, cols], operand.at[slot], load_sem.at[slot])]

    start(first_loads)
    start(operands(0, 0, 0))
    start(second_loads)
    start(mixer_loads)

    tiles = rows // TILE

    def n2g_block(i):
        at = (tiles - 1 - i) * TILE
        return x_copy(
            n2g_h.at[pl.ds(pl.multiple_of(rows + at, TILE), TILE)],
            ngr.at[pl.ds(pl.multiple_of(at, TILE), TILE)],
            i,
        )

    for i in range(tiles):
        n2g_block(i).start()
    last_swap = x_copy(out_h.at[pl.ds(rows, rows)], out_recv, tiles + own_chunks)
    last_swap.start()
    wait(first_loads)

    def from_core(q):
        scatter0(q).wait()
        rc[q] = (widen(ring[q % RING, core_at, :]) + widen(rc[q])).astype(BF16)

    def to_y(j):
        from_core(j)
        scatter_y(j).start()

    for group in range(3):
        if group == 1:
            wait(second_loads)
            start(out_loads)

        def compute(i, carry, group=group):
            j = group * per + i
            slot = j % 2
            wait(operands(group, i, slot))

            @pl.when(i + 1 < per)
            def _():
                start(operands(group, i + 1, 1 - slot))

            if group < 2:

                @pl.when(i + 1 == per)
                def _():
                    start(operands(group + 1, 0, 1 - slot))

            left = cot if group == 0 else n2
            ring[j % RING] = dot(left[...], operand[slot], TN).astype(BF16)
            scatter0(j).start()

            @pl.when(j >= LAG)
            def _():
                to_y(j - LAG)

            @pl.when(j >= 10)
            def _():
                tick(j - 10)

            return carry

        lax.fori_loop(0, per, compute, 0)
    start(late_loads)
    for j in range(ffn_chunks - LAG, ffn_chunks):
        to_y(j)
    done = ffn_chunks - 10

    nxt[...] = jnp.zeros_like(nxt)
    kacc[...] = jnp.zeros_like(kacc)
    small[...] = jnp.zeros_like(small)
    wait(mixer_loads)
    wait(out_loads)

    def mixer(i, carry):
        at = pl.ds(pl.multiple_of((tiles - 1 - i) * TILE, TILE), TILE)
        loads = [
            pltpu.make_async_copy(hidden.at[at], hid, tile_sem.at[0]),
            pltpu.make_async_copy(n2g_h.at[at], ngo, tile_sem.at[1]),
            pltpu.make_async_copy(source.at[at], src, tile_sem.at[2]),
            pltpu.make_async_copy(parts_o.at[at], part.at[0], tile_sem.at[3]),
            pltpu.make_async_copy(parts_p.at[at], part.at[1], tile_sem.at[4]),
        ]
        start(loads)
        n2g_block(i).wait()
        wait(loads)
        upstream = widen(ngo[...]) + widen(ngr[at, :])
        values = hid[...]
        inverse = lax.rsqrt(jnp.mean(values * values, axis=-1, keepdims=True) + eps)
        weighted = upstream * gain_two[...]
        scaled = values * inverse
        small[1:2, :] += jnp.sum(upstream * scaled, axis=0, keepdims=True)
        along = jnp.mean(weighted * scaled, axis=-1, keepdims=True)
        grad = widen(cot[at, :]) + inverse * (weighted - scaled * along)
        grad_low = grad.astype(BF16)
        cot[at, :] = grad_low
        row = lax.broadcasted_iota(jnp.int32, (TILE, channels), 0)
        upstream_one = jnp.zeros((TILE, width), F32)
        for h in range(2):
            out_w = cot[pl.ds(rows + h * channels, channels), :]
            gated_grad = dot(grad_low, out_w, NT)
            b_part = widen(part[h, :, 0:channels])
            c_part = widen(part[h, :, channels : 2 * channels])
            x_part = widen(part[h, :, 2 * channels : 3 * channels])
            convolved = widen(part[h, :, 3 * channels : 4 * channels])
            conv_grad = gated_grad * c_part
            one = jnp.where(row == TILE - 1, nxt[h, 0:1, :], pltpu.roll(conv_grad, TILE - 1, 0))
            two = jnp.where(
                row == TILE - 1,
                nxt[h, 1:2, :],
                jnp.where(row == TILE - 2, nxt[h, 0:1, :], pltpu.roll(conv_grad, TILE - 2, 0)),
            )
            nxt[h, 0:2, :] = conv_grad[0:2, :]
            mixed_grad = taps[h, 2:3, :] * conv_grad + taps[h, 1:2, :] * one + taps[h, 0:1, :] * two
            mixed = b_part * x_part
            kacc[h, 0:1, :] += jnp.sum(mixed * two, axis=0, keepdims=True)
            kacc[h, 1:2, :] += jnp.sum(mixed * one, axis=0, keepdims=True)
            kacc[h, 2:3, :] += jnp.sum(mixed * conv_grad, axis=0, keepdims=True)
            for k, piece_grad in enumerate((mixed_grad * x_part, gated_grad * convolved, mixed_grad * b_part)):
                low = piece_grad.astype(BF16)
                pg[h, at, k * channels : (k + 1) * channels] = low
                upstream_one = upstream_one + dot(low, in_w[h, k], NT)
        values_one = widen(src[...])
        inverse_one = lax.rsqrt(jnp.mean(values_one * values_one, axis=-1, keepdims=True) + eps)
        weighted_one = upstream_one * gain_one[...]
        scaled_one = values_one * inverse_one
        small[0:1, :] += jnp.sum(upstream_one * scaled_one, axis=0, keepdims=True)
        along_one = jnp.mean(weighted_one * scaled_one, axis=-1, keepdims=True)
        ig[...] = (grad + inverse_one * (weighted_one - scaled_one * along_one)).astype(BF16)
        store = pltpu.make_async_copy(ig, input_grad.at[at], tile_sem.at[5])
        store.start()
        store.wait()
        return carry

    lax.fori_loop(0, tiles, mixer, 0)
    wait(late_loads)

    def piece(h, m_in, m_out):
        if m_in is not None:
            cols = pl.ds(pl.multiple_of(m_in * TILE, TILE), TILE)
            return dot(n2[0:rows, :], pg[h, :, cols], TN)
        cols = pl.ds(pl.multiple_of(h * channels + m_out * TILE, TILE), TILE)
        return dot(cot[0:rows, :], n2[rows : 2 * rows, cols], TN)

    def cross(m):
        return x_copy(rc.at[total + m], rx.at[m], tiles + m)

    def after_core(h, m):
        if h == 1:
            from_core(total + m)
            cross(m).start()
        else:
            from_core(ffn_chunks + m)

    for h in (1, 0):
        base = total if h == 1 else ffn_chunks

        def in_piece(m, carry, h=h, base=base):
            q = base + m
            ring[q % RING] = piece(h, m, None).astype(BF16)
            scatter0(q).start()

            @pl.when(m >= LAG)
            def _():
                after_core(h, m - LAG)

            k = done + m + (in_chunks if h == 0 else 0)

            @pl.when(k < ffn_chunks)
            def _():
                tick(k)

            return carry

        lax.fori_loop(0, in_chunks, in_piece, 0)
        for m in range(in_chunks, own_chunks):
            ring[(base + m) % RING] = piece(h, None, m - in_chunks).astype(BF16)
            scatter0(base + m).start()
            after_core(h, m - LAG)
        for m in range(own_chunks - LAG, own_chunks):
            after_core(h, m)
    for h in range(2):
        cols = pl.ds(pl.multiple_of(channels * (tensor + h - 2 * tensor * h), channels), channels)
        small[2:5, cols] = kacc[h, 0:3, :]

    def small_copy(k):
        device = (peers[k], tensor) if k < 4 else (me, 1 - tensor)
        return pltpu.make_async_remote_copy(
            src_ref=small, dst_ref=small_recv.at[k], send_sem=small_send.at[k], recv_sem=small_rsem.at[k],
            device_id=device, device_id_type=MESH,
        )

    def crossed(m, carry):
        cross(m).wait()
        j = ffn_chunks + m
        rc[j] = (widen(rc[j]) + widen(rx[m])).astype(BF16)
        scatter_y(j).start()
        finish(m)
        return carry

    lax.fori_loop(0, own_chunks, crossed, 0)
    for k in range(5):
        small_copy(k).start()
        small_copy(k).wait()
        small[...] = small[...] + small_recv[k]

    last_tick = total + LAGS[3]
    turn = 2 * ffn_chunks - own_chunks - LAGS[3] - 3

    def drain_two(k, carry):
        tick(k)
        finish(own_chunks + 2 * (k - ffn_chunks))
        finish(own_chunks + 2 * (k - ffn_chunks) + 1)
        return carry

    def drain_one(k, carry):
        tick(k)
        finish(k - LAGS[3] - 3)
        return carry

    def drain(j, carry):
        finish(j)
        return carry

    lax.fori_loop(ffn_chunks, turn, drain_two, 0)
    lax.fori_loop(turn, last_tick, drain_one, 0)
    lax.fori_loop(last_tick - LAGS[3] - 3, total, drain, 0)

    last_swap.wait()

    def leave(i, carry):
        at = pl.ds(pl.multiple_of(i * TILE, TILE), TILE)
        loads = [
            pltpu.make_async_copy(hidden.at[at], hid, tile_sem.at[0]),
            pltpu.make_async_copy(out_h.at[at], ngo, tile_sem.at[1]),
            pltpu.make_async_copy(out_recv.at[at], src, tile_sem.at[2]),
        ]
        start(loads)
        wait(loads)
        ig[...] = (hid[...] + (widen(ngo[...]) + widen(src[...]))).astype(BF16)
        store = pltpu.make_async_copy(ig, block_out.at[at], tile_sem.at[5])
        store.start()
        store.wait()
        return carry

    lax.fori_loop(0, tiles, leave, 0)

    def arrive(j, carry):
        gather_core(j).wait()

        @pl.when(inner_z)
        def _():
            down_other(j).wait_send()

        return carry

    lax.fori_loop(0, total, arrive, 0)


def back(gains, taps, arrays, rows, width, hidden, channels):
    ffn_chunks = 3 * hidden // TILE
    own_chunks = 4 * channels // TILE
    total = ffn_chunks + own_chunks
    half = width // 2
    vmem = pl.BlockSpec(memory_space=pltpu.VMEM)
    hbm = pl.BlockSpec(memory_space=pl.ANY)

    def buffer(count, size):
        return pltpu.VMEM((count, size, TILE), BF16)

    return pl.pallas_call(
        back_kernel,
        in_specs=[vmem, vmem, vmem] + [hbm] * len(arrays),
        out_specs=[hbm, hbm, hbm, hbm, vmem],
        out_shape=[
            jax.ShapeDtypeStruct((width, total * TILE), BF16),
            jax.ShapeDtypeStruct((rows, width), BF16),
            jax.ShapeDtypeStruct((rows, width), BF16),
            jax.ShapeDtypeStruct((rows, width), BF16),
            jax.ShapeDtypeStruct((8, width), F32),
        ],
        scratch_shapes=[
            buffer(RING, width),
            buffer(total + own_chunks, half),
            buffer(total, half // 2),
            buffer(total, half // 2),
            buffer(total, half // 4),
            buffer(own_chunks, half),
            pltpu.VMEM((5, 8, width), F32),
            pltpu.VMEM((2 * rows, width), BF16),
            pltpu.VMEM((2 * rows, width), BF16),
            buffer(2, 2 * rows),
            pltpu.VMEM((2, 3, width, channels), BF16),
            pltpu.VMEM((2, rows, 3 * channels), BF16),
            pltpu.VMEM((2, TILE, 4 * channels), BF16),
            pltpu.VMEM((TILE, width), F32),
            pltpu.VMEM((TILE, width), BF16),
            pltpu.VMEM((rows, width), BF16),
            pltpu.VMEM((TILE, width), BF16),
            pltpu.VMEM((TILE, width), BF16),
            pltpu.VMEM((2, 8, channels), F32),
            pltpu.VMEM((2, 8, channels), F32),
            pltpu.SemaphoreType.DMA((2,)),
            pltpu.SemaphoreType.DMA((8,)),
            pltpu.SemaphoreType.DMA((6,)),
            pltpu.SemaphoreType.DMA((9, total + own_chunks)),
            pltpu.SemaphoreType.DMA((9, total + own_chunks)),
            pltpu.SemaphoreType.DMA((total,)),
            pltpu.SemaphoreType.DMA((rows // TILE + own_chunks + 1,)),
            pltpu.SemaphoreType.DMA((rows // TILE + own_chunks + 1,)),
            pltpu.SemaphoreType.DMA((5,)),
            pltpu.SemaphoreType.DMA((5,)),
        ],
        name="back",
        cost_estimate=pl.CostEstimate(
            flops=12 * rows * width * hidden + 32 * rows * width * channels,
            bytes_accessed=20 * hidden * width,
            transcendentals=0,
        ),
        compiler_params=pltpu.CompilerParams(
            collective_id=1, has_side_effects=True, vmem_limit_bytes=63 * 2**20
        ),
    )(*gains, taps, *arrays)


def finish_kernel(
    summed, block_in, grad_in, down, gate, up, in_grad, out, block_out, grad_out, buf, wide, turned, sem_in, sem_out, sem_keep
):
    width = summed.shape[0]
    step = buf.shape[2]
    hidden_units, channels = down.shape[0], out.shape[0]
    keeps = [
        pltpu.make_async_copy(block_in, block_out, sem_keep.at[0]),
        pltpu.make_async_copy(grad_in, grad_out, sem_keep.at[1]),
    ]
    jobs = []
    for group, target in ((1, gate), (0, down), (2, up)):
        for i in range(hidden_units // step):
            at = pl.ds(i * step, step)
            place = target.at[at] if group == 0 else target.at[:, at]
            jobs.append((group * hidden_units + i * step, step, group == 0, place))
    base = 3 * hidden_units
    jobs.append((base + KERNEL * channels, channels, True, out))
    for k in range(KERNEL):
        jobs.append((base + k * channels, channels, False, in_grad.at[k]))

    def load(n):
        first, size = jobs[n][0], jobs[n][1]
        return pltpu.make_async_copy(
            summed.at[:, pl.ds(first, size)], buf.at[n % 2, :, pl.ds(0, size)], sem_in.at[n % 2]
        )

    def store(n):
        _, size, turn, place = jobs[n]
        source = turned.at[n % 2, pl.ds(0, size)] if turn else wide.at[n % 2, :, pl.ds(0, size)]
        return pltpu.make_async_copy(source, place, sem_out.at[n % 2])

    load(0).start()
    load(1).start()
    for n, (_, size, turn, _) in enumerate(jobs):
        load(n).wait()
        if n >= 2:
            store(n - 2).wait()
        slot = n % 2
        for r in range(0, size if turn else width, TILE):
            if turn:
                turned[slot, r : r + TILE, :] = widen(buf[slot, :, r : r + TILE]).T
            else:
                wide[slot, r : r + TILE, 0:size] = widen(buf[slot, r : r + TILE, 0:size])
        store(n).start()
        if n + 2 < len(jobs):
            load(n + 2).start()
        if n == 1:
            for copy in keeps:
                copy.start()
    for n in (len(jobs) - 2, len(jobs) - 1):
        store(n).wait()
    for copy in keeps:
        copy.wait()


def finish_grads(summed, block_output, input_grad, hidden_units, channels):
    width = summed.shape[0]
    hbm = pl.BlockSpec(memory_space=pl.ANY)
    low = jax.ShapeDtypeStruct(block_output.shape, BF16)
    return pl.pallas_call(
        finish_kernel,
        in_specs=[hbm] * 3,
        out_specs=[hbm] * 7,
        out_shape=[
            jax.ShapeDtypeStruct((hidden_units, width), F32),
            jax.ShapeDtypeStruct((width, hidden_units), F32),
            jax.ShapeDtypeStruct((width, hidden_units), F32),
            jax.ShapeDtypeStruct((KERNEL, width, channels), F32),
            jax.ShapeDtypeStruct((channels, width), F32),
            low,
            low,
        ],
        scratch_shapes=[
            pltpu.VMEM((2, width, STEP), BF16),
            pltpu.VMEM((2, width, STEP), F32),
            pltpu.VMEM((2, STEP, width), F32),
            pltpu.SemaphoreType.DMA((2,)),
            pltpu.SemaphoreType.DMA((2,)),
            pltpu.SemaphoreType.DMA((2,)),
        ],
        name="finish_grads",
        compiler_params=pltpu.CompilerParams(vmem_limit_bytes=48 * 2**20),
    )(summed, block_output, input_grad)


def fast(
    block_input,
    mixer_gain,
    in_weight,
    conv_kernel,
    out_weight,
    ffn_gain,
    gate_weight,
    up_weight,
    down_weight,
    output_grad,
    lengths,
):
    rows, width = block_input.shape
    channels, hidden_units = out_weight.shape[0], gate_weight.shape[1]
    me = lax.axis_index("tensor")
    gains = (mixer_gain[None], ffn_gain[None])
    in_parts = jnp.transpose(in_weight, (1, 0, 2))
    taps, cot, n2, inner, gg, ug, n2g, out, hidden, parts_o, parts_p, in_other, out_other, n1, gated = front(
        lengths,
        gains,
        conv_kernel,
        block_input,
        output_grad,
        in_parts,
        out_weight,
        gate_weight,
        up_weight,
        down_weight,
    )
    arrays = (cot, n2, inner, gg, ug, n2g, out, hidden, block_input, parts_o, parts_p)
    arrays += (in_parts, in_other, out_weight, out_other, n1, gated)
    summed, input_grad, block_output, _, small = back(gains, taps, arrays, rows, width, hidden_units, channels)
    down_grad, gate_grad, up_grad, in_grad, out_grad, block_output, input_grad = finish_grads(
        summed, block_output, input_grad, hidden_units, channels
    )
    conv_kernel_grad = lax.dynamic_slice_in_dim(small[2 : 2 + KERNEL], me * channels, channels, axis=1)
    return (
        block_output,
        input_grad,
        small[0],
        jnp.transpose(in_grad, (1, 0, 2)),
        conv_kernel_grad,
        out_grad,
        small[1],
        gate_grad,
        up_grad,
        down_grad,
    )


def solution(mesh):
    def step(*args):
        rows, slots = args[0].shape[0], args[10].shape[0]
        one_slot_each = mesh.shape["tensor"] == 2 and mesh.shape["dp"] == 16 and slots == 2 and rows == 4 * TILE
        return (fast if one_slot_each else local)(*args)

    return jax.shard_map(
        step,
        mesh=mesh,
        in_specs=(
            P(("dp", "tensor"), None),
            P(),
            P(None, None, "tensor"),
            P(None, "tensor"),
            P("tensor", None),
            P(),
            P(None, "tensor"),
            P(None, "tensor"),
            P("tensor", None),
            P(("dp", "tensor"), None),
            P("dp"),
        ),
        out_specs=(
            P(("dp", "tensor"), None),
            P(("dp", "tensor"), None),
            P(),
            P(None, None, "tensor"),
            P(None, "tensor"),
            P("tensor", None),
            P(),
            P(None, "tensor"),
            P(None, "tensor"),
            P("tensor", None),
        ),
        check_vma=False,
    )
```

```python
import functools

import jax
import jax.numpy as jnp
from jax import lax
from jax.experimental import pallas as pl
from jax.experimental.pallas import tpu as pltpu
from jax.sharding import PartitionSpec as P

KERNEL = 3


eps = 1e-05


def rms_forward(values, gain_values):
    inverse = lax.rsqrt(jnp.mean(values * values, axis=-1, keepdims=True) + eps)
    return (values * inverse * gain_values, inverse)


def rms_backward(values, inverse, gain_values, upstream):
    weighted = upstream * gain_values
    gain_part = jnp.sum(upstream * values * inverse, axis=0)
    through = inverse * weighted - values * inverse**3 * jnp.mean(
        weighted * values, axis=-1, keepdims=True
    )
    return (through, gain_part)


def local(
    block_input,
    mixer_gain,
    in_weight,
    conv_kernel,
    out_weight,
    ffn_gain,
    gate_weight,
    up_weight,
    down_weight,
    output_grad,
    lengths,
):
    local_rows = block_input.shape[0]
    model_width = block_input.shape[1]
    channels = in_weight.shape[2]
    slot_count = lengths.shape[0]
    source = block_input.astype(jnp.float32)
    normed_one, inverse_one = rms_forward(source, mixer_gain)
    gathered_one = lax.all_gather(normed_one.astype(jnp.bfloat16), "tensor", axis=0, tiled=True)
    group_rows = gathered_one.shape[0]
    slot_length = group_rows // slot_count
    in_flat = in_weight.reshape(model_width, 3 * channels)
    projected = jnp.dot(gathered_one, in_flat, preferred_element_type=jnp.float32).reshape(
        group_rows, 3, channels
    )
    b_part = projected[:, 0]
    c_part = projected[:, 1]
    x_part = projected[:, 2]
    mixed = (b_part * x_part).reshape(slot_count, slot_length, channels)
    kernel_values = conv_kernel.astype(jnp.float32)
    padded = jnp.pad(mixed, ((0, 0), (KERNEL - 1, 0), (0, 0)))
    convolved = jnp.zeros_like(mixed)
    for offset in range(KERNEL):
        convolved = convolved + kernel_values[offset] * padded[:, offset : offset + slot_length]
    convolved = convolved.reshape(group_rows, channels)
    gated = (c_part * convolved).astype(jnp.bfloat16)
    hidden = source + lax.psum_scatter(
        jnp.dot(gated, out_weight, preferred_element_type=jnp.float32).astype(jnp.bfloat16),
        "tensor",
        scatter_dimension=0,
        tiled=True,
    ).astype(jnp.float32)
    normed_two, inverse_two = rms_forward(hidden, ffn_gain)
    gathered_two = lax.all_gather(normed_two.astype(jnp.bfloat16), "tensor", axis=0, tiled=True)
    gate_value = jnp.dot(gathered_two, gate_weight, preferred_element_type=jnp.float32)
    up_value = jnp.dot(gathered_two, up_weight, preferred_element_type=jnp.float32)
    sigmoid_gate = jax.nn.sigmoid(gate_value)
    silu_value = gate_value * sigmoid_gate
    inner_low = (silu_value * up_value).astype(jnp.bfloat16)
    block_output = (
        hidden
        + lax.psum_scatter(
            jnp.dot(inner_low, down_weight, preferred_element_type=jnp.float32).astype(
                jnp.bfloat16
            ),
            "tensor",
            scatter_dimension=0,
            tiled=True,
        ).astype(jnp.float32)
    ).astype(jnp.bfloat16)
    row_index = lax.axis_index("tensor") * local_rows + jnp.arange(local_rows, dtype=jnp.int32)
    slot_of = row_index // slot_length
    position = row_index % slot_length
    matched = (slot_of[:, None] == jnp.arange(slot_count, dtype=jnp.int32)[None, :]) & (
        position[:, None] < lengths[None, :]
    )
    token_mask = jnp.any(matched, axis=1).astype(jnp.float32)
    cotangent = output_grad.astype(jnp.float32) * token_mask[:, None]
    grad_rows = lax.all_gather(cotangent.astype(jnp.bfloat16), "tensor", axis=0, tiled=True)
    inner_grad = jnp.einsum("rd,fd->rf", grad_rows, down_weight, preferred_element_type=jnp.float32)
    down_weight_grad = jnp.einsum(
        "rf,rd->fd", inner_low, grad_rows, preferred_element_type=jnp.float32
    )
    gate_grad = (
        inner_grad * up_value * sigmoid_gate * (1.0 + gate_value * (1.0 - sigmoid_gate))
    ).astype(jnp.bfloat16)
    up_grad = (inner_grad * silu_value).astype(jnp.bfloat16)
    gate_weight_grad = jnp.einsum(
        "rd,rf->df", gathered_two, gate_grad, preferred_element_type=jnp.float32
    )
    up_weight_grad = jnp.einsum(
        "rd,rf->df", gathered_two, up_grad, preferred_element_type=jnp.float32
    )
    from_gate = jnp.einsum("rf,df->rd", gate_grad, gate_weight, preferred_element_type=jnp.float32)
    normed_two_grad = lax.psum_scatter(
        (
            from_gate
            + jnp.einsum("rf,df->rd", up_grad, up_weight, preferred_element_type=jnp.float32)
        ).astype(jnp.bfloat16),
        "tensor",
        scatter_dimension=0,
        tiled=True,
    ).astype(jnp.float32)
    through_two, ffn_gain_part = rms_backward(hidden, inverse_two, ffn_gain, normed_two_grad)
    hidden_grad = cotangent + through_two
    hidden_rows = lax.all_gather(hidden_grad.astype(jnp.bfloat16), "tensor", axis=0, tiled=True)
    gated_grad = jnp.einsum(
        "rd,cd->rc", hidden_rows, out_weight, preferred_element_type=jnp.float32
    )
    out_weight_grad = jnp.einsum(
        "rc,rd->cd", gated, hidden_rows, preferred_element_type=jnp.float32
    )
    c_grad = gated_grad * convolved
    conv_grad = (gated_grad * c_part).reshape(slot_count, slot_length, channels)
    padded_after = jnp.pad(conv_grad, ((0, 0), (0, KERNEL - 1), (0, 0)))
    mixed_grad = jnp.zeros_like(conv_grad)
    kernel_rows = []
    for offset in range(KERNEL):
        shift_start = KERNEL - 1 - offset
        mixed_grad = (
            mixed_grad
            + kernel_values[offset] * padded_after[:, shift_start : shift_start + slot_length]
        )
        kernel_rows.append(
            jnp.sum(conv_grad * padded[:, offset : offset + slot_length], axis=(0, 1))
        )
    conv_kernel_grad = jnp.stack(kernel_rows, axis=0)
    mixed_grad = mixed_grad.reshape(group_rows, channels)
    projected_grad = jnp.stack([mixed_grad * x_part, c_grad, mixed_grad * b_part], axis=1).astype(
        jnp.bfloat16
    )
    in_weight_grad = jnp.einsum(
        "rd,rkc->dkc", gathered_one, projected_grad, preferred_element_type=jnp.float32
    )
    normed_one_grad = lax.psum_scatter(
        jnp.einsum(
            "rkc,dkc->rd", projected_grad, in_weight, preferred_element_type=jnp.float32
        ).astype(jnp.bfloat16),
        "tensor",
        scatter_dimension=0,
        tiled=True,
    ).astype(jnp.float32)
    through_one, mixer_gain_part = rms_backward(source, inverse_one, mixer_gain, normed_one_grad)
    input_grad = (hidden_grad + through_one).astype(jnp.bfloat16)
    (
        in_weight_grad,
        conv_kernel_grad,
        out_weight_grad,
        gate_weight_grad,
        up_weight_grad,
        down_weight_grad,
    ) = (
        lax.psum(in_weight_grad.astype(jnp.bfloat16), "dp").astype(jnp.float32),
        lax.psum(conv_kernel_grad.astype(jnp.bfloat16), "dp").astype(jnp.float32),
        lax.psum(out_weight_grad.astype(jnp.bfloat16), "dp").astype(jnp.float32),
        lax.psum(gate_weight_grad.astype(jnp.bfloat16), "dp").astype(jnp.float32),
        lax.psum(up_weight_grad.astype(jnp.bfloat16), "dp").astype(jnp.float32),
        lax.psum(down_weight_grad.astype(jnp.bfloat16), "dp").astype(jnp.float32),
    )
    mixer_gain_grad, ffn_gain_grad = lax.psum((mixer_gain_part, ffn_gain_part), ("dp", "tensor"))
    return (
        block_output,
        input_grad,
        mixer_gain_grad,
        in_weight_grad,
        conv_kernel_grad,
        out_weight_grad,
        ffn_gain_grad,
        gate_weight_grad,
        up_weight_grad,
        down_weight_grad,
    )


NN = (((1,), (0,)), ((), ()))
NT = (((1,), (1,)), ((), ()))
TN = (((0,), (0,)), ((), ()))
F32 = jnp.float32
BF16 = jnp.bfloat16


def dot(a, b, dims=NN):
    return lax.dot_general(a, b, dims, preferred_element_type=F32)


MESH = pl.DeviceIdType.MESH
TILE = 256
RING = 4
LAG = 2
LAGS = (2, 3, 5, 6)


def enter(devices):
    barrier = pltpu.get_barrier_semaphore()
    for device in devices:
        pl.semaphore_signal(barrier, inc=1, device_id=device, device_id_type=MESH)
    pl.semaphore_wait(barrier, len(devices))


def widen(values):
    return values.astype(F32)


def inverse_rms(values):
    return lax.rsqrt(jnp.mean(values * values, axis=-1, keepdims=True) + eps)


STEP = 768
PASS = 512


def front_kernel(
    lengths, gain_one, gain_two, taps_own, block_input, output_grad, in_own, out_own, gate_w, up_w, down_w,
    taps_out, cot_h, n2_h, inner_h, gg_h, ug_h, n2g_h, out_h, hidden_h, parts_o, parts_p, in_other, out_other, n1_h, gated_h,
    in_w, out_w, src, other, n1, gated, n2, cot, wg, wu, wd, inner, gg, ug, acc1, acc2, part, hid, low1, low2, prev, taps, taps_low,
    load_sem, w_sem, o_sem, p_sem, h_sem, l_sem, x_send, x_recv, send, recv,
):
    rows, width = src.shape
    channels = out_own.shape[0]
    hidden_units = gate_w.shape[1]
    me = lax.axis_index("dp")
    tensor = lax.axis_index("tensor")
    bits = [(me // (1 << k)) % 2 for k in range(3)]
    peers = [me + (1 << k) - (2 << k) * bits[k] for k in range(3)]
    enter([(p, tensor) for p in peers] + [(me, 1 - tensor)])

    def x_copy(src_ref, dst_ref, k):
        return pltpu.make_async_remote_copy(
            src_ref=src_ref, dst_ref=dst_ref, send_sem=x_send.at[k], recv_sem=x_recv.at[k],
            device_id=(me, 1 - tensor), device_id_type=MESH,
        )

    units = [(in_own.at[k], in_w.at[1, k], width) for k in range(3)] + [(out_own, out_w.at[1], channels)]
    routes = [(1, 2, 0), (2, 1, 0), (2, 1, 0), (1, 2, 0)]

    def span(u, s):
        size = units[u][2]
        first, second, last = routes[u]
        if s == 0:
            start = bits[last] * (size // 2) + bits[second] * (size // 4) + bits[first] * (size // 8)
            return pl.ds(pl.multiple_of(start, size // 8), size // 8)
        if s == 1:
            start = bits[last] * (size // 2) + bits[second] * (size // 4)
            return pl.ds(pl.multiple_of(start, size // 4), size // 4)
        return pl.ds(pl.multiple_of(bits[last] * (size // 2), size // 2), size // 2)

    def cross(u):
        return x_copy(units[u][0].at[span(u, 0)], units[u][1].at[span(u, 0)], u)

    def double(u, s):
        at = span(u, s)
        return pltpu.make_async_remote_copy(
            src_ref=units[u][1].at[at], dst_ref=units[u][1].at[at],
            send_sem=send.at[u, s], recv_sem=recv.at[u, s],
            device_id=(peers[routes[u][s]], tensor), device_id_type=MESH,
        )

    blocks = [pl.ds(k * PASS, PASS) for k in range(rows // PASS)]
    taps_copy = x_copy(taps_own, taps_low, 4)
    input_copies = [x_copy(block_input.at[b], other.at[b], 5 + k) for k, b in enumerate(blocks)]
    grad_copies = [
        x_copy(output_grad.at[b], cot.at[pl.ds(rows + k * PASS, PASS)], 5 + len(blocks) + k)
        for k, b in enumerate(blocks)
    ]
    taps_copy.start()
    for u in range(4):
        cross(u).start()
    for copy in input_copies + grad_copies:
        copy.start()

    def load(k, src_ref, dst_ref):
        return pltpu.make_async_copy(src_ref, dst_ref, load_sem.at[k])

    first_load = load(0, block_input, src)
    own_load = load(1, in_own, in_w.at[0])
    out_load = load(2, out_own, out_w.at[0])
    cot_load = load(3, output_grad, cot.at[pl.ds(0, rows)])
    for copy in (first_load, own_load, out_load, cot_load):
        copy.start()

    steps = hidden_units // STEP

    def weights(u):
        at = pl.ds(pl.multiple_of((u % steps) * STEP, STEP), STEP)
        slot = u % 2
        return [
            pltpu.make_async_copy(gate_w.at[:, at], wg.at[slot], w_sem.at[slot, 0]),
            pltpu.make_async_copy(up_w.at[:, at], wu.at[slot], w_sem.at[slot, 1]),
            pltpu.make_async_copy(down_w.at[at], wd.at[slot], w_sem.at[slot, 2]),
        ]

    for copy in weights(0):
        copy.start()
    taps[0] = widen(taps_own[...])
    first_load.wait()

    tiles = rows // TILE

    def tile_at(i, base=0):
        return pl.ds(pl.multiple_of(base + i * TILE, TILE), TILE)

    def normalize(i, carry):
        values = widen(src[tile_at(i), :])
        n1[tile_at(i), :] = (values * inverse_rms(values) * gain_one[...]).astype(BF16)
        return carry

    lax.fori_loop(0, tiles, normalize, 0)
    n1_store = load(4, n1, n1_h)
    n1_store.start()
    own_load.wait()

    row = lax.broadcasted_iota(jnp.int32, (TILE, channels), 0)

    def mix(normed, h):
        b_part, c_part, x_part = [dot(normed, in_w[h, k]) for k in range(3)]
        mixed = b_part * x_part
        last, before = prev[h, 7:8, :], prev[h, 6:7, :]
        one = jnp.where(row == 0, last, pltpu.roll(mixed, 1, 0))
        two = jnp.where(row == 0, before, jnp.where(row == 1, last, pltpu.roll(mixed, 2, 0)))
        prev[h, :, :] = mixed[TILE - 8 :, :]
        convolved = taps[h, 2:3, :] * mixed + taps[h, 1:2, :] * one + taps[h, 0:1, :] * two
        return b_part, c_part, x_part, convolved, c_part * convolved

    def part_store(h, i):
        out = parts_o if h == 0 else parts_p
        return pltpu.make_async_copy(part.at[i % 2], out.at[tile_at(i)], p_sem.at[i % 2])

    def own_half(i, h):
        pieces = mix(n1[tile_at(i), :], h)
        for k in range(4):
            part[i % 2, :, k * channels : (k + 1) * channels] = pieces[k].astype(BF16)
        gated[tile_at(i), h * channels : (h + 1) * channels] = pieces[4].astype(BF16)
        part_store(h, i).start()

    prev[...] = jnp.zeros_like(prev)

    def first_half(i, carry):
        @pl.when(i >= 2)
        def _():
            part_store(0, i - 2).wait()

        own_half(i, 0)
        for u in range(tiles):

            @pl.when(i == u)
            def _(u=u):
                cross(u).wait()
                double(u, 0).start()
                if u >= 2:
                    double(u - 2, 0).wait()
                    double(u - 2, 1).start()

        return carry

    lax.fori_loop(0, tiles, first_half, 0)
    for u in (2, 3):
        part_store(0, u).wait()
        double(u, 0).wait()
        double(u, 1).start()
    taps_copy.wait()
    taps[1] = widen(taps_low[...])
    for u in range(4):
        double(u, 1).wait()
        double(u, 2).start()

    def masked(base, length):
        def one(i, carry):
            at = tile_at(i, base)
            position = lax.broadcasted_iota(jnp.int32, (TILE, width), 0) + i * TILE
            values = widen(cot[at, :])
            cot[at, :] = jnp.where(position < length, values, jnp.zeros_like(values)).astype(BF16)
            return carry

        return one

    own_length = jnp.where(tensor == 0, lengths[0], lengths[1])
    other_length = jnp.where(tensor == 0, lengths[1], lengths[0])
    cot_load.wait()
    lax.fori_loop(0, tiles, masked(0, own_length), 0)
    cot_store = load(5, cot.at[pl.ds(0, rows)], cot_h.at[pl.ds(0, rows)])
    cot_store.start()
    out_load.wait()
    for u in range(4):
        double(u, 2).wait()
    other_stores = [load(6, in_w.at[1], in_other), load(7, out_w.at[1], out_other)]
    for copy in other_stores:
        copy.start()

    def leave_mixer(values, gated_low, at):
        hidden = values + (dot(gated_low[0], out_w[0]) + dot(gated_low[1], out_w[1]))
        n2[at, :] = (hidden * inverse_rms(hidden) * gain_two[...]).astype(BF16)
        return hidden

    def hid_store(i):
        return pltpu.make_async_copy(hid.at[i % 2], hidden_h.at[tile_at(i)], h_sem.at[i % 2])

    def second_half(i, carry):
        @pl.when(i >= 2)
        def _():
            part_store(1, i - 2).wait()
            hid_store(i - 2).wait()

        own_half(i, 1)
        at = tile_at(i)
        both = [gated[at, h * channels : (h + 1) * channels] for h in range(2)]
        hid[i % 2] = leave_mixer(widen(src[at, :]), both, at)
        hid_store(i).start()
        return carry

    lax.fori_loop(0, tiles, second_half, 0)
    for i in (tiles - 2, tiles - 1):
        part_store(1, i).wait()
        hid_store(i).wait()
    gated_store = load(8, gated, gated_h)
    gated_store.start()
    n2_store = load(9, n2.at[pl.ds(0, rows)], n2_h.at[pl.ds(0, rows)])
    n2_store.start()

    def stores(p, step, slot):
        at = pl.ds(pl.multiple_of(p * PASS, PASS), PASS)
        cols = pl.ds(pl.multiple_of(step * STEP, STEP), STEP)
        return [
            pltpu.make_async_copy(buf.at[slot], out.at[at, cols], o_sem.at[slot, k])
            for k, (buf, out) in enumerate(((inner, inner_h), (gg, gg_h), (ug, ug_h)))
        ]

    def low_stores(p):
        at = pl.ds(pl.multiple_of(p * PASS, PASS), PASS)
        return [
            pltpu.make_async_copy(low1, out_h.at[at], l_sem.at[0]),
            pltpu.make_async_copy(low2, n2g_h.at[at], l_sem.at[1]),
        ]

    passes = 2 * rows // PASS

    def ffn_pass(p, carry):
        acc1[...] = jnp.zeros_like(acc1)
        acc2[...] = jnp.zeros_like(acc2)

        def ffn_step(step, carry):
            u = p * steps + step
            slot = u % 2
            for copy in weights(u):
                copy.wait()

            @pl.when(u + 1 < passes * steps)
            def _():
                for copy in weights(u + 1):
                    copy.start()

            @pl.when(u >= 2)
            def _():
                for copy in stores(p, step, slot):
                    copy.wait()

            def front(r):
                at = tile_at(r, p * PASS)
                a, c = n2[at, :], cot[at, :]
                return dot(a, wg[slot]), dot(a, wu[slot]), dot(c, wd[slot], NT)

            count = PASS // TILE
            held = front(0)
            for r in range(count):
                following = front(r + 1) if r + 1 < count else None
                s = pl.ds(r * TILE, TILE)
                g, v, ig = held
                sig = jax.nn.sigmoid(g)
                silu = g * sig
                low = (silu * v).astype(BF16)
                gg_low = (ig * v * (sig + silu * (1.0 - sig))).astype(BF16)
                ug_low = (ig * silu).astype(BF16)
                inner[slot, s, :] = low
                gg[slot, s, :] = gg_low
                ug[slot, s, :] = ug_low
                acc1[s, :] += dot(low, wd[slot])
                acc2[s, :] += dot(gg_low, wg[slot], NT) + dot(ug_low, wu[slot], NT)
                held = following
            for copy in stores(p, step, slot):
                copy.start()
            return carry

        lax.fori_loop(0, steps, ffn_step, 0)

        @pl.when(p > 0)
        def _():
            for copy in low_stores(p):
                copy.wait()

        low1[...] = acc1[...].astype(BF16)
        low2[...] = acc2[...].astype(BF16)
        for copy in low_stores(p):
            copy.start()
        return carry

    n2_other = load(10, n2.at[pl.ds(rows, rows)], n2_h.at[pl.ds(rows, rows)])

    def other_tile(i, carry):
        values = widen(other[tile_at(i), :])
        normed = (values * inverse_rms(values) * gain_one[...]).astype(BF16)
        both = [mix(normed, h)[4].astype(BF16) for h in range(2)]
        leave_mixer(values, both, tile_at(i, rows))
        return carry

    def arrived(p):
        @pl.when(p == passes // 2)
        def _():
            prev[...] = jnp.zeros_like(prev)
            for copy in input_copies:
                copy.wait()
            lax.fori_loop(0, tiles, other_tile, 0)
            n2_other.start()

        per_block = PASS // TILE
        for k, copy in enumerate(grad_copies):

            @pl.when(p == passes // 2 + k)
            def _(k=k, copy=copy):
                copy.wait()
                lax.fori_loop(k * per_block, (k + 1) * per_block, masked(rows, other_length), 0)

    def whole_pass(p, carry):
        arrived(p)
        return ffn_pass(p, carry)

    lax.fori_loop(0, passes, whole_pass, 0)
    cot_other = load(11, cot.at[pl.ds(rows, rows)], cot_h.at[pl.ds(rows, rows)])
    cot_other.start()
    for slot in range(2):
        for copy in stores(0, 0, slot):
            copy.wait()
    for copy in low_stores(0):
        copy.wait()
    taps_out[...] = taps[...]
    for copy in [n1_store, cot_store, gated_store, n2_store, n2_other, cot_other] + other_stores:
        copy.wait()


def front(lengths, gains, taps_own, block_input, output_grad, in_own, out_own, gate_w, up_w, down_w):
    rows, width = block_input.shape
    channels = out_own.shape[0]
    hidden_units = gate_w.shape[1]
    vmem = pl.BlockSpec(memory_space=pltpu.VMEM)
    hbm = pl.BlockSpec(memory_space=pl.ANY)

    def shaped(*shape, kind=BF16):
        return jax.ShapeDtypeStruct(shape, kind)

    both = 2 * rows
    outs = [
        shaped(2, KERNEL, channels, kind=F32),
        shaped(both, width),
        shaped(both, width),
        shaped(both, hidden_units),
        shaped(both, hidden_units),
        shaped(both, hidden_units),
        shaped(both, width),
        shaped(both, width),
        shaped(rows, width, kind=F32),
        shaped(rows, 4 * channels),
        shaped(rows, 4 * channels),
        shaped(KERNEL, width, channels),
        shaped(channels, width),
        shaped(rows, width),
        shaped(rows, 2 * channels),
    ]
    x_count = 5 + 2 * (rows // PASS)
    dma = pltpu.SemaphoreType.DMA
    return pl.pallas_call(
        front_kernel,
        in_specs=[pl.BlockSpec(memory_space=pltpu.SMEM), vmem, vmem, vmem] + [hbm] * 7,
        out_specs=[vmem] + [hbm] * 14,
        out_shape=outs,
        scratch_shapes=[
            pltpu.VMEM((2, KERNEL, width, channels), BF16),
            pltpu.VMEM((2, channels, width), BF16),
            pltpu.VMEM((rows, width), BF16),
            pltpu.VMEM((rows, width), BF16),
            pltpu.VMEM((rows, width), BF16),
            pltpu.VMEM((rows, 2 * channels), BF16),
            pltpu.VMEM((both, width), BF16),
            pltpu.VMEM((both, width), BF16),
            pltpu.VMEM((2, width, STEP), BF16),
            pltpu.VMEM((2, width, STEP), BF16),
            pltpu.VMEM((2, STEP, width), BF16),
            pltpu.VMEM((2, PASS, STEP), BF16),
            pltpu.VMEM((2, PASS, STEP), BF16),
            pltpu.VMEM((2, PASS, STEP), BF16),
            pltpu.VMEM((PASS, width), F32),
            pltpu.VMEM((PASS, width), F32),
            pltpu.VMEM((2, TILE, 4 * channels), BF16),
            pltpu.VMEM((2, TILE, width), F32),
            pltpu.VMEM((PASS, width), BF16),
            pltpu.VMEM((PASS, width), BF16),
            pltpu.VMEM((2, 8, channels), F32),
            pltpu.VMEM((2, KERNEL, channels), F32),
            pltpu.VMEM((KERNEL, channels), BF16),
            dma((12,)),
            dma((2, 3)),
            dma((2, 3)),
            dma((2,)),
            dma((2,)),
            dma((2,)),
            dma((x_count,)),
            dma((x_count,)),
            dma((4, 3)),
            dma((4, 3)),
        ],
        name="front",
        cost_estimate=pl.CostEstimate(
            flops=24 * rows * width * hidden_units, bytes_accessed=40 * hidden_units * width, transcendentals=0
        ),
        compiler_params=pltpu.CompilerParams(
            collective_id=2, has_side_effects=True, vmem_limit_bytes=63 * 2**20
        ),
    )(lengths, *gains, taps_own, block_input, output_grad, in_own, out_own, gate_w, up_w, down_w)


def back_kernel(
    gain_one, gain_two, taps,
    cot_h, n2_h, inner_h, gg_h, ug_h, n2g_h, out_h,
    hidden, source, parts_o, parts_p, in_o, in_p, out_w_o, out_w_p, n1, gated,
    summed, input_grad, block_out, out_recv, small,
    ring, rc, ry, ra, rb, rx, small_recv, cot, n2, operand, in_w, pg, part, hid, ngo, ngr, src, ig, nxt, kacc,
    load_sem, fixed_sem, tile_sem, send, recv, local_sem, x_send, x_recv, small_send, small_rsem,
):
    width = cot.shape[1]
    rows = n1.shape[0]
    channels = out_w_o.shape[0]
    ffn_chunks = 3 * inner_h.shape[1] // TILE
    in_chunks = 3 * channels // TILE
    own_chunks = in_chunks + channels // TILE
    total = ffn_chunks + own_chunks
    half = width // 2

    me = lax.axis_index("dp")
    tensor = lax.axis_index("tensor")
    bits = [(me // (1 << k)) % 2 for k in range(4)]
    peers = [me + (1 << k) - (2 << k) * bits[k] for k in range(4)]
    z = me // 4
    mirror = me + 4 * (3 - 2 * z)
    inner_z = (z == 1) | (z == 2)
    outer_z = (z == 0) | (z == 3)
    enter([(p, tensor) for p in peers] + [(mirror, tensor), (me, 1 - tensor)])

    def peer_copy(src_ref, dst_ref, slot, j, peer):
        return pltpu.make_async_remote_copy(
            src_ref=src_ref, dst_ref=dst_ref, send_sem=send.at[slot, j], recv_sem=recv.at[slot, j],
            device_id=(peer, tensor), device_id_type=MESH,
        )

    def x_copy(src_ref, dst_ref, k):
        return pltpu.make_async_remote_copy(
            src_ref=src_ref, dst_ref=dst_ref, send_sem=x_send.at[k], recv_sem=x_recv.at[k],
            device_id=(me, 1 - tensor), device_id_type=MESH,
        )

    def rows_at(start, size):
        return pl.ds(pl.multiple_of(start, size), size)

    quarter, eighth = half // 2, half // 4
    core_at = rows_at(bits[0] * half, half)
    core_away = rows_at((1 - bits[0]) * half, half)
    y_at = rows_at(bits[1] * quarter, quarter)
    y_away = rows_at((1 - bits[1]) * quarter, quarter)
    z_at = rows_at(bits[1] * quarter + bits[3] * eighth, eighth)
    z_away = rows_at(bits[1] * quarter + (1 - bits[3]) * eighth, eighth)

    def result(j, start, size):
        return summed.at[j, rows_at(start, size)]

    def result_y(j):
        return result(j, bits[0] * half + bits[1] * quarter, quarter)

    def result_z(j, side):
        return result(j, bits[0] * half + bits[1] * quarter + side * eighth, eighth)

    def scatter0(q):
        return peer_copy(ring.at[q % RING, core_away], rc.at[q], 0, q, peers[0])

    def scatter_y(j):
        return peer_copy(rc.at[j, y_away], ry.at[j], 1, j, peers[1])

    def up(j):
        return peer_copy(rc.at[j, y_at], ra.at[j], 2, j, peers[2])

    def across(j):
        return peer_copy(rc.at[j, z_away], rb.at[j], 3, j, mirror)

    def keep(j):
        return pltpu.make_async_copy(rc.at[j, z_at], result_z(j, bits[3]), local_sem.at[j])

    def gather_across(j):
        return peer_copy(rc.at[j, z_at], result_z(j, bits[3]), 4, j, mirror)

    def down_own(j):
        return peer_copy(rc.at[j, z_at], result_z(j, bits[3]), 5, j, peers[2])

    def down_other(j):
        return peer_copy(result_z(j, 1 - bits[3]), result_z(j, 1 - bits[3]), 6, j, peers[2])

    def gather_y(j):
        return peer_copy(result_y(j), result_y(j), 7, j, peers[1])

    def gather_core(j):
        at = result(j, bits[0] * half, half)
        return peer_copy(at, at, 8, j, peers[0])

    def add(j, at, landed):
        rc[j, at, :] = (widen(rc[j, at, :]) + widen(landed[j])).astype(BF16)

    def when(j, also, what):
        inside = (j >= 0) & (j < total)

        @pl.when(inside if also is None else inside & also)
        def _():
            what(j)

    def tick(k):
        def from_y(j):
            scatter_y(j).wait()
            add(j, y_at, ry)

            @pl.when(outer_z)
            def _():
                up(j).start()

        def from_outer(j):
            up(j).wait_recv()
            add(j, y_at, ra)
            across(j).start()

        def from_inner(j):
            across(j).wait()
            add(j, z_at, rb)
            gather_across(j).start()
            down_own(j).start()
            keep(j).start()

        def to_outer(j):
            gather_across(j).wait()
            keep(j).wait()
            down_other(j).start()

        def to_y_again(j):
            @pl.when(inner_z)
            def _():
                down_own(j).wait_send()

            @pl.when(outer_z)
            def _():
                up(j).wait_send()
                down_own(j).wait_recv()
                down_other(j).wait_recv()

            gather_y(j).start()

        when(k, None, from_y)
        when(k - LAGS[0], inner_z, from_outer)
        when(k - LAGS[1], inner_z, from_inner)
        when(k - LAGS[2], inner_z, to_outer)
        when(k - LAGS[3], None, to_y_again)

    def finish(j):
        gather_y(j).wait()
        gather_core(j).start()

    def ticks(low, high):
        def one(k, carry):
            tick(k)
            return carry

        lax.fori_loop(low, high, one, 0)

    def fixed(k, src_ref, dst_ref):
        return pltpu.make_async_copy(src_ref, dst_ref, fixed_sem.at[k])

    first_loads = [fixed(0, cot_h, cot)]
    second_loads = [fixed(1, n2_h, n2)]
    mixer_loads = [fixed(2, in_o, in_w.at[0]), fixed(3, in_p, in_w.at[1])]
    out_loads = [
        fixed(4, out_w_o, cot.at[pl.ds(rows, channels)]),
        fixed(5, out_w_p, cot.at[pl.ds(rows + channels, channels)]),
    ]
    late_loads = [fixed(6, n1, n2.at[pl.ds(0, rows)]), fixed(7, gated, n2.at[pl.ds(rows, rows)])]

    def start(copies):
        for copy in copies:
            copy.start()

    def wait(copies):
        for copy in copies:
            copy.wait()

    groups = (inner_h, gg_h, ug_h)
    per = ffn_chunks // 3

    def operands(group, i, slot):
        cols = pl.ds(pl.multiple_of(i * TILE, TILE), TILE)
        return [pltpu.make_async_copy(groups[group].at[:, cols], operand.at[slot], load_sem.at[slot])]

    start(first_loads)
    start(operands(0, 0, 0))
    start(second_loads)
    start(mixer_loads)

    tiles = rows // TILE

    def n2g_block(i):
        at = (tiles - 1 - i) * TILE
        return x_copy(
            n2g_h.at[pl.ds(pl.multiple_of(rows + at, TILE), TILE)],
            ngr.at[pl.ds(pl.multiple_of(at, TILE), TILE)],
            i,
        )

    for i in range(tiles):
        n2g_block(i).start()
    last_swap = x_copy(out_h.at[pl.ds(rows, rows)], out_recv, tiles + own_chunks)
    last_swap.start()
    wait(first_loads)

    def from_core(q):
        scatter0(q).wait()
        rc[q] = (widen(ring[q % RING, core_at, :]) + widen(rc[q])).astype(BF16)

    def to_y(j):
        from_core(j)
        scatter_y(j).start()

    for group in range(3):
        if group == 1:
            wait(second_loads)
            start(out_loads)

        def compute(i, carry, group=group):
            j = group * per + i
            slot = j % 2
            wait(operands(group, i, slot))

            @pl.when(i + 1 < per)
            def _():
                start(operands(group, i + 1, 1 - slot))

            if group < 2:

                @pl.when(i + 1 == per)
                def _():
                    start(operands(group + 1, 0, 1 - slot))

            left = cot if group == 0 else n2
            ring[j % RING] = dot(left[...], operand[slot], TN).astype(BF16)
            scatter0(j).start()

            @pl.when(j >= LAG)
            def _():
                to_y(j - LAG)

            @pl.when(j >= 10)
            def _():
                tick(j - 10)

            return carry

        lax.fori_loop(0, per, compute, 0)
    start(late_loads)
    for j in range(ffn_chunks - LAG, ffn_chunks):
        to_y(j)
    done = ffn_chunks - 10

    nxt[...] = jnp.zeros_like(nxt)
    kacc[...] = jnp.zeros_like(kacc)
    small[...] = jnp.zeros_like(small)
    wait(mixer_loads)
    wait(out_loads)

    def mixer(i, carry):
        at = pl.ds(pl.multiple_of((tiles - 1 - i) * TILE, TILE), TILE)
        loads = [
            pltpu.make_async_copy(hidden.at[at], hid, tile_sem.at[0]),
            pltpu.make_async_copy(n2g_h.at[at], ngo, tile_sem.at[1]),
            pltpu.make_async_copy(source.at[at], src, tile_sem.at[2]),
            pltpu.make_async_copy(parts_o.at[at], part.at[0], tile_sem.at[3]),
            pltpu.make_async_copy(parts_p.at[at], part.at[1], tile_sem.at[4]),
        ]
        start(loads)
        n2g_block(i).wait()
        wait(loads)
        upstream = widen(ngo[...]) + widen(ngr[at, :])
        values = hid[...]
        inverse = lax.rsqrt(jnp.mean(values * values, axis=-1, keepdims=True) + eps)
        weighted = upstream * gain_two[...]
        scaled = values * inverse
        small[1:2, :] += jnp.sum(upstream * scaled, axis=0, keepdims=True)
        along = jnp.mean(weighted * scaled, axis=-1, keepdims=True)
        grad = widen(cot[at, :]) + inverse * (weighted - scaled * along)
        grad_low = grad.astype(BF16)
        cot[at, :] = grad_low
        row = lax.broadcasted_iota(jnp.int32, (TILE, channels), 0)
        upstream_one = jnp.zeros((TILE, width), F32)
        for h in range(2):
            out_w = cot[pl.ds(rows + h * channels, channels), :]
            gated_grad = dot(grad_low, out_w, NT)
            b_part = widen(part[h, :, 0:channels])
            c_part = widen(part[h, :, channels : 2 * channels])
            x_part = widen(part[h, :, 2 * channels : 3 * channels])
            convolved = widen(part[h, :, 3 * channels : 4 * channels])
            conv_grad = gated_grad * c_part
            one = jnp.where(row == TILE - 1, nxt[h, 0:1, :], pltpu.roll(conv_grad, TILE - 1, 0))
            two = jnp.where(
                row == TILE - 1,
                nxt[h, 1:2, :],
                jnp.where(row == TILE - 2, nxt[h, 0:1, :], pltpu.roll(conv_grad, TILE - 2, 0)),
            )
            nxt[h, 0:2, :] = conv_grad[0:2, :]
            mixed_grad = taps[h, 2:3, :] * conv_grad + taps[h, 1:2, :] * one + taps[h, 0:1, :] * two
            mixed = b_part * x_part
            kacc[h, 0:1, :] += jnp.sum(mixed * two, axis=0, keepdims=True)
            kacc[h, 1:2, :] += jnp.sum(mixed * one, axis=0, keepdims=True)
            kacc[h, 2:3, :] += jnp.sum(mixed * conv_grad, axis=0, keepdims=True)
            for k, piece_grad in enumerate((mixed_grad * x_part, gated_grad * convolved, mixed_grad * b_part)):
                low = piece_grad.astype(BF16)
                pg[h, at, k * channels : (k + 1) * channels] = low
                upstream_one = upstream_one + dot(low, in_w[h, k], NT)
        values_one = widen(src[...])
        inverse_one = lax.rsqrt(jnp.mean(values_one * values_one, axis=-1, keepdims=True) + eps)
        weighted_one = upstream_one * gain_one[...]
        scaled_one = values_one * inverse_one
        small[0:1, :] += jnp.sum(upstream_one * scaled_one, axis=0, keepdims=True)
        along_one = jnp.mean(weighted_one * scaled_one, axis=-1, keepdims=True)
        ig[...] = (grad + inverse_one * (weighted_one - scaled_one * along_one)).astype(BF16)
        store = pltpu.make_async_copy(ig, input_grad.at[at], tile_sem.at[5])
        store.start()
        store.wait()
        return carry

    lax.fori_loop(0, tiles, mixer, 0)
    wait(late_loads)

    def piece(h, m_in, m_out):
        if m_in is not None:
            cols = pl.ds(pl.multiple_of(m_in * TILE, TILE), TILE)
            return dot(n2[0:rows, :], pg[h, :, cols], TN)
        cols = pl.ds(pl.multiple_of(h * channels + m_out * TILE, TILE), TILE)
        return dot(cot[0:rows, :], n2[rows : 2 * rows, cols], TN)

    def cross(m):
        return x_copy(rc.at[total + m], rx.at[m], tiles + m)

    def after_core(h, m):
        if h == 1:
            from_core(total + m)
            cross(m).start()
        else:
            from_core(ffn_chunks + m)

    for h in (1, 0):
        base = total if h == 1 else ffn_chunks

        def in_piece(m, carry, h=h, base=base):
            q = base + m
            ring[q % RING] = piece(h, m, None).astype(BF16)
            scatter0(q).start()

            @pl.when(m >= LAG)
            def _():
                after_core(h, m - LAG)

            k = done + m + (in_chunks if h == 0 else 0)

            @pl.when(k < ffn_chunks)
            def _():
                tick(k)

            return carry

        lax.fori_loop(0, in_chunks, in_piece, 0)
        for m in range(in_chunks, own_chunks):
            ring[(base + m) % RING] = piece(h, None, m - in_chunks).astype(BF16)
            scatter0(base + m).start()
            after_core(h, m - LAG)
        for m in range(own_chunks - LAG, own_chunks):
            after_core(h, m)
    for h in range(2):
        cols = pl.ds(pl.multiple_of(channels * (tensor + h - 2 * tensor * h), channels), channels)
        small[2:5, cols] = kacc[h, 0:3, :]

    def small_copy(k):
        device = (peers[k], tensor) if k < 4 else (me, 1 - tensor)
        return pltpu.make_async_remote_copy(
            src_ref=small, dst_ref=small_recv.at[k], send_sem=small_send.at[k], recv_sem=small_rsem.at[k],
            device_id=device, device_id_type=MESH,
        )

    def crossed(m, carry):
        cross(m).wait()
        j = ffn_chunks + m
        rc[j] = (widen(rc[j]) + widen(rx[m])).astype(BF16)
        scatter_y(j).start()
        finish(m)
        return carry

    lax.fori_loop(0, own_chunks, crossed, 0)
    for k in range(5):
        small_copy(k).start()
        small_copy(k).wait()
        small[...] = small[...] + small_recv[k]

    last_swap.wait()

    def leave(i, carry):
        at = pl.ds(pl.multiple_of(i * TILE, TILE), TILE)
        loads = [
            pltpu.make_async_copy(hidden.at[at], hid, tile_sem.at[0]),
            pltpu.make_async_copy(out_h.at[at], ngo, tile_sem.at[1]),
            pltpu.make_async_copy(out_recv.at[at], src, tile_sem.at[2]),
        ]
        start(loads)
        wait(loads)
        ig[...] = (hid[...] + (widen(ngo[...]) + widen(src[...]))).astype(BF16)
        store = pltpu.make_async_copy(ig, block_out.at[at], tile_sem.at[5])
        store.start()
        store.wait()
        return carry

    lax.fori_loop(0, tiles, leave, 0)

    last_tick = total + LAGS[3]
    turn = 2 * ffn_chunks - own_chunks - LAGS[3] - 3

    def drain_two(k, carry):
        tick(k)
        finish(own_chunks + 2 * (k - ffn_chunks))
        finish(own_chunks + 2 * (k - ffn_chunks) + 1)
        return carry

    def drain_one(k, carry):
        tick(k)
        finish(k - LAGS[3] - 3)
        return carry

    def drain(j, carry):
        finish(j)
        return carry

    lax.fori_loop(ffn_chunks, turn, drain_two, 0)
    lax.fori_loop(turn, last_tick, drain_one, 0)
    lax.fori_loop(last_tick - LAGS[3] - 3, total, drain, 0)

    def arrive(j, carry):
        gather_core(j).wait()

        @pl.when(inner_z)
        def _():
            down_other(j).wait_send()

        return carry

    lax.fori_loop(0, total, arrive, 0)


def back(gains, taps, arrays, rows, width, hidden, channels):
    ffn_chunks = 3 * hidden // TILE
    own_chunks = 4 * channels // TILE
    total = ffn_chunks + own_chunks
    half = width // 2
    vmem = pl.BlockSpec(memory_space=pltpu.VMEM)
    hbm = pl.BlockSpec(memory_space=pl.ANY)

    def buffer(count, size):
        return pltpu.VMEM((count, size, TILE), BF16)

    return pl.pallas_call(
        back_kernel,
        in_specs=[vmem, vmem, vmem] + [hbm] * len(arrays),
        out_specs=[hbm, hbm, hbm, hbm, vmem],
        out_shape=[
            jax.ShapeDtypeStruct((total, width, TILE), BF16),
            jax.ShapeDtypeStruct((rows, width), BF16),
            jax.ShapeDtypeStruct((rows, width), BF16),
            jax.ShapeDtypeStruct((rows, width), BF16),
            jax.ShapeDtypeStruct((8, width), F32),
        ],
        scratch_shapes=[
            buffer(RING, width),
            buffer(total + own_chunks, half),
            buffer(total, half // 2),
            buffer(total, half // 2),
            buffer(total, half // 4),
            buffer(own_chunks, half),
            pltpu.VMEM((5, 8, width), F32),
            pltpu.VMEM((2 * rows, width), BF16),
            pltpu.VMEM((2 * rows, width), BF16),
            buffer(2, 2 * rows),
            pltpu.VMEM((2, 3, width, channels), BF16),
            pltpu.VMEM((2, rows, 3 * channels), BF16),
            pltpu.VMEM((2, TILE, 4 * channels), BF16),
            pltpu.VMEM((TILE, width), F32),
            pltpu.VMEM((TILE, width), BF16),
            pltpu.VMEM((rows, width), BF16),
            pltpu.VMEM((TILE, width), BF16),
            pltpu.VMEM((TILE, width), BF16),
            pltpu.VMEM((2, 8, channels), F32),
            pltpu.VMEM((2, 8, channels), F32),
            pltpu.SemaphoreType.DMA((2,)),
            pltpu.SemaphoreType.DMA((8,)),
            pltpu.SemaphoreType.DMA((6,)),
            pltpu.SemaphoreType.DMA((9, total + own_chunks)),
            pltpu.SemaphoreType.DMA((9, total + own_chunks)),
            pltpu.SemaphoreType.DMA((total,)),
            pltpu.SemaphoreType.DMA((rows // TILE + own_chunks + 1,)),
            pltpu.SemaphoreType.DMA((rows // TILE + own_chunks + 1,)),
            pltpu.SemaphoreType.DMA((5,)),
            pltpu.SemaphoreType.DMA((5,)),
        ],
        name="back",
        cost_estimate=pl.CostEstimate(
            flops=12 * rows * width * hidden + 32 * rows * width * channels,
            bytes_accessed=20 * hidden * width,
            transcendentals=0,
        ),
        compiler_params=pltpu.CompilerParams(
            collective_id=1, has_side_effects=True, vmem_limit_bytes=63 * 2**20
        ),
    )(*gains, taps, *arrays)


def finish_kernel(
    summed, block_in, grad_in, down, gate, up, in_grad, out, block_out, grad_out, buf, wide, turned, held, sem_in, sem_out, sem_keep
):
    width = summed.shape[1]
    most = buf.shape[1]
    hidden_units, channels = down.shape[0], out.shape[0]
    per, halves = hidden_units // TILE, channels // TILE
    fetches = [
        pltpu.make_async_copy(block_in, held.at[0], sem_keep.at[0]),
        pltpu.make_async_copy(grad_in, held.at[1], sem_keep.at[1]),
    ]
    keeps = [
        pltpu.make_async_copy(held.at[0], block_out, sem_keep.at[2]),
        pltpu.make_async_copy(held.at[1], grad_out, sem_keep.at[3]),
    ]
    jobs = []
    for group, target in ((1, gate), (0, down), (2, up)):
        for i in range(0, per, most):
            at = pl.ds(i * TILE, most * TILE)
            place = target.at[at] if group == 0 else target.at[:, at]
            jobs.append((group * per + i, most, group == 0, place))
    jobs.append((3 * per + KERNEL * halves, halves, True, out))
    for k in range(KERNEL):
        jobs.append((3 * per + k * halves, halves, False, in_grad.at[k]))

    def load(n):
        first, count = jobs[n][0], jobs[n][1]
        return pltpu.make_async_copy(
            summed.at[pl.ds(first, count)], buf.at[n % 2, pl.ds(0, count)], sem_in.at[n % 2]
        )

    def store(n):
        _, count, turn, place = jobs[n]
        size = count * TILE
        source = turned.at[n % 2, pl.ds(0, size)] if turn else wide.at[n % 2, :, pl.ds(0, size)]
        return pltpu.make_async_copy(source, place, sem_out.at[n % 2])

    load(0).start()
    load(1).start()
    for n, (_, count, turn, _) in enumerate(jobs):
        load(n).wait()
        if n >= 2:
            store(n - 2).wait()
        slot = n % 2
        for k in range(count):
            at = slice(k * TILE, (k + 1) * TILE)
            if turn:
                turned[slot, at, :] = widen(buf[slot, k]).T
            else:
                wide[slot, :, at] = widen(buf[slot, k])
        store(n).start()
        if n + 2 < len(jobs):
            load(n + 2).start()
        if n == 1:
            for copy in fetches:
                copy.start()
        if n == 4:
            for fetch, copy in zip(fetches, keeps):
                fetch.wait()
                copy.start()
    for n in (len(jobs) - 2, len(jobs) - 1):
        store(n).wait()
    for copy in keeps:
        copy.wait()


def finish_grads(summed, block_output, input_grad, hidden_units, channels):
    width = summed.shape[1]
    hbm = pl.BlockSpec(memory_space=pl.ANY)
    low = jax.ShapeDtypeStruct(block_output.shape, BF16)
    return pl.pallas_call(
        finish_kernel,
        in_specs=[hbm] * 3,
        out_specs=[hbm] * 7,
        out_shape=[
            jax.ShapeDtypeStruct((hidden_units, width), F32),
            jax.ShapeDtypeStruct((width, hidden_units), F32),
            jax.ShapeDtypeStruct((width, hidden_units), F32),
            jax.ShapeDtypeStruct((KERNEL, width, channels), F32),
            jax.ShapeDtypeStruct((channels, width), F32),
            low,
            low,
        ],
        scratch_shapes=[
            pltpu.VMEM((2, STEP // TILE, width, TILE), BF16),
            pltpu.VMEM((2, width, STEP), F32),
            pltpu.VMEM((2, STEP, width), F32),
            pltpu.VMEM((2,) + block_output.shape, BF16),
            pltpu.SemaphoreType.DMA((2,)),
            pltpu.SemaphoreType.DMA((2,)),
            pltpu.SemaphoreType.DMA((4,)),
        ],
        name="finish_grads",
        compiler_params=pltpu.CompilerParams(vmem_limit_bytes=63 * 2**20),
    )(summed, block_output, input_grad)


def fast(
    block_input,
    mixer_gain,
    in_weight,
    conv_kernel,
    out_weight,
    ffn_gain,
    gate_weight,
    up_weight,
    down_weight,
    output_grad,
    lengths,
):
    rows, width = block_input.shape
    channels, hidden_units = out_weight.shape[0], gate_weight.shape[1]
    me = lax.axis_index("tensor")
    gains = (mixer_gain[None], ffn_gain[None])
    in_parts = jnp.transpose(in_weight, (1, 0, 2))
    taps, cot, n2, inner, gg, ug, n2g, out, hidden, parts_o, parts_p, in_other, out_other, n1, gated = front(
        lengths,
        gains,
        conv_kernel,
        block_input,
        output_grad,
        in_parts,
        out_weight,
        gate_weight,
        up_weight,
        down_weight,
    )
    arrays = (cot, n2, inner, gg, ug, n2g, out, hidden, block_input, parts_o, parts_p)
    arrays += (in_parts, in_other, out_weight, out_other, n1, gated)
    summed, input_grad, block_output, _, small = back(gains, taps, arrays, rows, width, hidden_units, channels)
    down_grad, gate_grad, up_grad, in_grad, out_grad, block_output, input_grad = finish_grads(
        summed, block_output, input_grad, hidden_units, channels
    )
    conv_kernel_grad = lax.dynamic_slice_in_dim(small[2 : 2 + KERNEL], me * channels, channels, axis=1)
    return (
        block_output,
        input_grad,
        small[0],
        jnp.transpose(in_grad, (1, 0, 2)),
        conv_kernel_grad,
        out_grad,
        small[1],
        gate_grad,
        up_grad,
        down_grad,
    )


def solution(mesh):
    def step(*args):
        rows, slots = args[0].shape[0], args[10].shape[0]
        one_slot_each = mesh.shape["tensor"] == 2 and mesh.shape["dp"] == 16 and slots == 2 and rows == 4 * TILE
        return (fast if one_slot_each else local)(*args)

    return jax.shard_map(
        step,
        mesh=mesh,
        in_specs=(
            P(("dp", "tensor"), None),
            P(),
            P(None, None, "tensor"),
            P(None, "tensor"),
            P("tensor", None),
            P(),
            P(None, "tensor"),
            P(None, "tensor"),
            P("tensor", None),
            P(("dp", "tensor"), None),
            P("dp"),
        ),
        out_specs=(
            P(("dp", "tensor"), None),
            P(("dp", "tensor"), None),
            P(),
            P(None, None, "tensor"),
            P(None, "tensor"),
            P("tensor", None),
            P(),
            P(None, "tensor"),
            P(None, "tensor"),
            P("tensor", None),
        ),
        check_vma=False,
    )
```

```python
import functools

import jax
import jax.numpy as jnp
from jax import lax
from jax.experimental import pallas as pl
from jax.experimental.pallas import tpu as pltpu
from jax.sharding import PartitionSpec as P

KERNEL = 3


eps = 1e-05


def rms_forward(values, gain_values):
    inverse = lax.rsqrt(jnp.mean(values * values, axis=-1, keepdims=True) + eps)
    return (values * inverse * gain_values, inverse)


def rms_backward(values, inverse, gain_values, upstream):
    weighted = upstream * gain_values
    gain_part = jnp.sum(upstream * values * inverse, axis=0)
    through = inverse * weighted - values * inverse**3 * jnp.mean(
        weighted * values, axis=-1, keepdims=True
    )
    return (through, gain_part)


def local(
    block_input,
    mixer_gain,
    in_weight,
    conv_kernel,
    out_weight,
    ffn_gain,
    gate_weight,
    up_weight,
    down_weight,
    output_grad,
    lengths,
):
    local_rows = block_input.shape[0]
    model_width = block_input.shape[1]
    channels = in_weight.shape[2]
    slot_count = lengths.shape[0]
    source = block_input.astype(jnp.float32)
    normed_one, inverse_one = rms_forward(source, mixer_gain)
    gathered_one = lax.all_gather(normed_one.astype(jnp.bfloat16), "tensor", axis=0, tiled=True)
    group_rows = gathered_one.shape[0]
    slot_length = group_rows // slot_count
    in_flat = in_weight.reshape(model_width, 3 * channels)
    projected = jnp.dot(gathered_one, in_flat, preferred_element_type=jnp.float32).reshape(
        group_rows, 3, channels
    )
    b_part = projected[:, 0]
    c_part = projected[:, 1]
    x_part = projected[:, 2]
    mixed = (b_part * x_part).reshape(slot_count, slot_length, channels)
    kernel_values = conv_kernel.astype(jnp.float32)
    padded = jnp.pad(mixed, ((0, 0), (KERNEL - 1, 0), (0, 0)))
    convolved = jnp.zeros_like(mixed)
    for offset in range(KERNEL):
        convolved = convolved + kernel_values[offset] * padded[:, offset : offset + slot_length]
    convolved = convolved.reshape(group_rows, channels)
    gated = (c_part * convolved).astype(jnp.bfloat16)
    hidden = source + lax.psum_scatter(
        jnp.dot(gated, out_weight, preferred_element_type=jnp.float32).astype(jnp.bfloat16),
        "tensor",
        scatter_dimension=0,
        tiled=True,
    ).astype(jnp.float32)
    normed_two, inverse_two = rms_forward(hidden, ffn_gain)
    gathered_two = lax.all_gather(normed_two.astype(jnp.bfloat16), "tensor", axis=0, tiled=True)
    gate_value = jnp.dot(gathered_two, gate_weight, preferred_element_type=jnp.float32)
    up_value = jnp.dot(gathered_two, up_weight, preferred_element_type=jnp.float32)
    sigmoid_gate = jax.nn.sigmoid(gate_value)
    silu_value = gate_value * sigmoid_gate
    inner_low = (silu_value * up_value).astype(jnp.bfloat16)
    block_output = (
        hidden
        + lax.psum_scatter(
            jnp.dot(inner_low, down_weight, preferred_element_type=jnp.float32).astype(
                jnp.bfloat16
            ),
            "tensor",
            scatter_dimension=0,
            tiled=True,
        ).astype(jnp.float32)
    ).astype(jnp.bfloat16)
    row_index = lax.axis_index("tensor") * local_rows + jnp.arange(local_rows, dtype=jnp.int32)
    slot_of = row_index // slot_length
    position = row_index % slot_length
    matched = (slot_of[:, None] == jnp.arange(slot_count, dtype=jnp.int32)[None, :]) & (
        position[:, None] < lengths[None, :]
    )
    token_mask = jnp.any(matched, axis=1).astype(jnp.float32)
    cotangent = output_grad.astype(jnp.float32) * token_mask[:, None]
    grad_rows = lax.all_gather(cotangent.astype(jnp.bfloat16), "tensor", axis=0, tiled=True)
    inner_grad = jnp.einsum("rd,fd->rf", grad_rows, down_weight, preferred_element_type=jnp.float32)
    down_weight_grad = jnp.einsum(
        "rf,rd->fd", inner_low, grad_rows, preferred_element_type=jnp.float32
    )
    gate_grad = (
        inner_grad * up_value * sigmoid_gate * (1.0 + gate_value * (1.0 - sigmoid_gate))
    ).astype(jnp.bfloat16)
    up_grad = (inner_grad * silu_value).astype(jnp.bfloat16)
    gate_weight_grad = jnp.einsum(
        "rd,rf->df", gathered_two, gate_grad, preferred_element_type=jnp.float32
    )
    up_weight_grad = jnp.einsum(
        "rd,rf->df", gathered_two, up_grad, preferred_element_type=jnp.float32
    )
    from_gate = jnp.einsum("rf,df->rd", gate_grad, gate_weight, preferred_element_type=jnp.float32)
    normed_two_grad = lax.psum_scatter(
        (
            from_gate
            + jnp.einsum("rf,df->rd", up_grad, up_weight, preferred_element_type=jnp.float32)
        ).astype(jnp.bfloat16),
        "tensor",
        scatter_dimension=0,
        tiled=True,
    ).astype(jnp.float32)
    through_two, ffn_gain_part = rms_backward(hidden, inverse_two, ffn_gain, normed_two_grad)
    hidden_grad = cotangent + through_two
    hidden_rows = lax.all_gather(hidden_grad.astype(jnp.bfloat16), "tensor", axis=0, tiled=True)
    gated_grad = jnp.einsum(
        "rd,cd->rc", hidden_rows, out_weight, preferred_element_type=jnp.float32
    )
    out_weight_grad = jnp.einsum(
        "rc,rd->cd", gated, hidden_rows, preferred_element_type=jnp.float32
    )
    c_grad = gated_grad * convolved
    conv_grad = (gated_grad * c_part).reshape(slot_count, slot_length, channels)
    padded_after = jnp.pad(conv_grad, ((0, 0), (0, KERNEL - 1), (0, 0)))
    mixed_grad = jnp.zeros_like(conv_grad)
    kernel_rows = []
    for offset in range(KERNEL):
        shift_start = KERNEL - 1 - offset
        mixed_grad = (
            mixed_grad
            + kernel_values[offset] * padded_after[:, shift_start : shift_start + slot_length]
        )
        kernel_rows.append(
            jnp.sum(conv_grad * padded[:, offset : offset + slot_length], axis=(0, 1))
        )
    conv_kernel_grad = jnp.stack(kernel_rows, axis=0)
    mixed_grad = mixed_grad.reshape(group_rows, channels)
    projected_grad = jnp.stack([mixed_grad * x_part, c_grad, mixed_grad * b_part], axis=1).astype(
        jnp.bfloat16
    )
    in_weight_grad = jnp.einsum(
        "rd,rkc->dkc", gathered_one, projected_grad, preferred_element_type=jnp.float32
    )
    normed_one_grad = lax.psum_scatter(
        jnp.einsum(
            "rkc,dkc->rd", projected_grad, in_weight, preferred_element_type=jnp.float32
        ).astype(jnp.bfloat16),
        "tensor",
        scatter_dimension=0,
        tiled=True,
    ).astype(jnp.float32)
    through_one, mixer_gain_part = rms_backward(source, inverse_one, mixer_gain, normed_one_grad)
    input_grad = (hidden_grad + through_one).astype(jnp.bfloat16)
    (
        in_weight_grad,
        conv_kernel_grad,
        out_weight_grad,
        gate_weight_grad,
        up_weight_grad,
        down_weight_grad,
    ) = (
        lax.psum(in_weight_grad.astype(jnp.bfloat16), "dp").astype(jnp.float32),
        lax.psum(conv_kernel_grad.astype(jnp.bfloat16), "dp").astype(jnp.float32),
        lax.psum(out_weight_grad.astype(jnp.bfloat16), "dp").astype(jnp.float32),
        lax.psum(gate_weight_grad.astype(jnp.bfloat16), "dp").astype(jnp.float32),
        lax.psum(up_weight_grad.astype(jnp.bfloat16), "dp").astype(jnp.float32),
        lax.psum(down_weight_grad.astype(jnp.bfloat16), "dp").astype(jnp.float32),
    )
    mixer_gain_grad, ffn_gain_grad = lax.psum((mixer_gain_part, ffn_gain_part), ("dp", "tensor"))
    return (
        block_output,
        input_grad,
        mixer_gain_grad,
        in_weight_grad,
        conv_kernel_grad,
        out_weight_grad,
        ffn_gain_grad,
        gate_weight_grad,
        up_weight_grad,
        down_weight_grad,
    )


NN = (((1,), (0,)), ((), ()))
NT = (((1,), (1,)), ((), ()))
TN = (((0,), (0,)), ((), ()))
F32 = jnp.float32
BF16 = jnp.bfloat16


def dot(a, b, dims=NN):
    return lax.dot_general(a, b, dims, preferred_element_type=F32)


MESH = pl.DeviceIdType.MESH
TILE = 256
RING = 4
LAG = 2
LAGS = (2, 3, 5, 6)


def enter(devices):
    barrier = pltpu.get_barrier_semaphore()
    for device in devices:
        pl.semaphore_signal(barrier, inc=1, device_id=device, device_id_type=MESH)
    pl.semaphore_wait(barrier, len(devices))


def widen(values):
    return values.astype(F32)


def inverse_rms(values):
    return lax.rsqrt(jnp.mean(values * values, axis=-1, keepdims=True) + eps)


STEP = 768
PASS = 512


def front_kernel(
    lengths, gain_one, gain_two, taps_own, block_input, output_grad, in_own, out_own, gate_w, up_w, down_w,
    taps_out, cot_h, n2_h, inner_h, gg_h, ug_h, n2g_h, out_h, hidden_h, parts_o, parts_p, in_other, out_other, n1_h, gated_h,
    in_w, out_w, src, other, n1, gated, n2, cot, wg, wu, wd, inner, gg, ug, acc1, acc2, part, hid, low1, low2, prev, taps, taps_low,
    load_sem, w_sem, o_sem, p_sem, h_sem, l_sem, x_send, x_recv, send, recv,
):
    rows, width = src.shape
    channels = out_own.shape[0]
    hidden_units = gate_w.shape[1]
    me = lax.axis_index("dp")
    tensor = lax.axis_index("tensor")
    bits = [(me // (1 << k)) % 2 for k in range(3)]
    peers = [me + (1 << k) - (2 << k) * bits[k] for k in range(3)]
    enter([(p, tensor) for p in peers] + [(me, 1 - tensor)])

    def x_copy(src_ref, dst_ref, k):
        return pltpu.make_async_remote_copy(
            src_ref=src_ref, dst_ref=dst_ref, send_sem=x_send.at[k], recv_sem=x_recv.at[k],
            device_id=(me, 1 - tensor), device_id_type=MESH,
        )

    units = [(in_own.at[k], in_w.at[1, k], width) for k in range(3)] + [(out_own, out_w.at[1], channels)]
    routes = [(1, 2, 0), (2, 1, 0), (2, 1, 0), (1, 2, 0)]

    def span(u, s):
        size = units[u][2]
        first, second, last = routes[u]
        if s == 0:
            start = bits[last] * (size // 2) + bits[second] * (size // 4) + bits[first] * (size // 8)
            return pl.ds(pl.multiple_of(start, size // 8), size // 8)
        if s == 1:
            start = bits[last] * (size // 2) + bits[second] * (size // 4)
            return pl.ds(pl.multiple_of(start, size // 4), size // 4)
        return pl.ds(pl.multiple_of(bits[last] * (size // 2), size // 2), size // 2)

    def cross(u):
        return x_copy(units[u][0].at[span(u, 0)], units[u][1].at[span(u, 0)], u)

    def double(u, s):
        at = span(u, s)
        return pltpu.make_async_remote_copy(
            src_ref=units[u][1].at[at], dst_ref=units[u][1].at[at],
            send_sem=send.at[u, s], recv_sem=recv.at[u, s],
            device_id=(peers[routes[u][s]], tensor), device_id_type=MESH,
        )

    blocks = [pl.ds(k * PASS, PASS) for k in range(rows // PASS)]
    taps_copy = x_copy(taps_own, taps_low, 4)
    input_copies = [x_copy(block_input.at[b], other.at[b], 5 + k) for k, b in enumerate(blocks)]
    grad_copies = [
        x_copy(output_grad.at[b], cot.at[pl.ds(rows + k * PASS, PASS)], 5 + len(blocks) + k)
        for k, b in enumerate(blocks)
    ]
    taps_copy.start()
    for u in range(4):
        cross(u).start()
    for copy in input_copies + grad_copies:
        copy.start()

    def load(k, src_ref, dst_ref):
        return pltpu.make_async_copy(src_ref, dst_ref, load_sem.at[k])

    first_load = load(0, block_input, src)
    own_load = load(1, in_own, in_w.at[0])
    out_load = load(2, out_own, out_w.at[0])
    cot_load = load(3, output_grad, cot.at[pl.ds(0, rows)])
    for copy in (first_load, own_load, out_load, cot_load):
        copy.start()

    steps = hidden_units // STEP

    def weights(u):
        at = pl.ds(pl.multiple_of((u % steps) * STEP, STEP), STEP)
        slot = u % 2
        return [
            pltpu.make_async_copy(gate_w.at[:, at], wg.at[slot], w_sem.at[slot, 0]),
            pltpu.make_async_copy(up_w.at[:, at], wu.at[slot], w_sem.at[slot, 1]),
            pltpu.make_async_copy(down_w.at[at], wd.at[slot], w_sem.at[slot, 2]),
        ]

    for copy in weights(0):
        copy.start()
    taps[0] = widen(taps_own[...])
    first_load.wait()

    tiles = rows // TILE

    def tile_at(i, base=0):
        return pl.ds(pl.multiple_of(base + i * TILE, TILE), TILE)

    def normalize(i, carry):
        values = widen(src[tile_at(i), :])
        n1[tile_at(i), :] = (values * inverse_rms(values) * gain_one[...]).astype(BF16)
        return carry

    lax.fori_loop(0, tiles, normalize, 0)
    n1_store = load(4, n1, n1_h)
    n1_store.start()
    own_load.wait()

    row = lax.broadcasted_iota(jnp.int32, (TILE, channels), 0)

    def mix(normed, h):
        b_part, c_part, x_part = [dot(normed, in_w[h, k]) for k in range(3)]
        mixed = b_part * x_part
        last, before = prev[h, 7:8, :], prev[h, 6:7, :]
        one = jnp.where(row == 0, last, pltpu.roll(mixed, 1, 0))
        two = jnp.where(row == 0, before, jnp.where(row == 1, last, pltpu.roll(mixed, 2, 0)))
        prev[h, :, :] = mixed[TILE - 8 :, :]
        convolved = taps[h, 2:3, :] * mixed + taps[h, 1:2, :] * one + taps[h, 0:1, :] * two
        return b_part, c_part, x_part, convolved, c_part * convolved

    def part_store(h, i):
        out = parts_o if h == 0 else parts_p
        return pltpu.make_async_copy(part.at[i % 2], out.at[tile_at(i)], p_sem.at[i % 2])

    def own_half(i, h):
        pieces = mix(n1[tile_at(i), :], h)
        for k in range(4):
            part[i % 2, :, k * channels : (k + 1) * channels] = pieces[k].astype(BF16)
        gated[tile_at(i), h * channels : (h + 1) * channels] = pieces[4].astype(BF16)
        part_store(h, i).start()

    prev[...] = jnp.zeros_like(prev)

    def first_half(i, carry):
        @pl.when(i >= 2)
        def _():
            part_store(0, i - 2).wait()

        own_half(i, 0)
        for u in range(tiles):

            @pl.when(i == u)
            def _(u=u):
                cross(u).wait()
                double(u, 0).start()
                if u >= 2:
                    double(u - 2, 0).wait()
                    double(u - 2, 1).start()

        return carry

    lax.fori_loop(0, tiles, first_half, 0)
    for u in (2, 3):
        part_store(0, u).wait()
        double(u, 0).wait()
        double(u, 1).start()
    taps_copy.wait()
    taps[1] = widen(taps_low[...])
    for u in range(4):
        double(u, 1).wait()
        double(u, 2).start()

    def masked(base, length):
        def one(i, carry):
            at = tile_at(i, base)
            position = lax.broadcasted_iota(jnp.int32, (TILE, width), 0) + i * TILE
            values = widen(cot[at, :])
            cot[at, :] = jnp.where(position < length, values, jnp.zeros_like(values)).astype(BF16)
            return carry

        return one

    own_length = jnp.where(tensor == 0, lengths[0], lengths[1])
    other_length = jnp.where(tensor == 0, lengths[1], lengths[0])
    cot_load.wait()
    lax.fori_loop(0, tiles, masked(0, own_length), 0)
    cot_store = load(5, cot.at[pl.ds(0, rows)], cot_h.at[pl.ds(0, rows)])
    cot_store.start()
    out_load.wait()
    for u in range(4):
        double(u, 2).wait()
    other_stores = [load(6, in_w.at[1], in_other), load(7, out_w.at[1], out_other)]
    for copy in other_stores:
        copy.start()

    def leave_mixer(values, gated_low, at):
        hidden = values + (dot(gated_low[0], out_w[0]) + dot(gated_low[1], out_w[1]))
        n2[at, :] = (hidden * inverse_rms(hidden) * gain_two[...]).astype(BF16)
        return hidden

    def hid_store(i):
        return pltpu.make_async_copy(hid.at[i % 2], hidden_h.at[tile_at(i)], h_sem.at[i % 2])

    def second_half(i, carry):
        @pl.when(i >= 2)
        def _():
            part_store(1, i - 2).wait()
            hid_store(i - 2).wait()

        own_half(i, 1)
        at = tile_at(i)
        both = [gated[at, h * channels : (h + 1) * channels] for h in range(2)]
        hid[i % 2] = leave_mixer(widen(src[at, :]), both, at)
        hid_store(i).start()
        return carry

    lax.fori_loop(0, tiles, second_half, 0)
    for i in (tiles - 2, tiles - 1):
        part_store(1, i).wait()
        hid_store(i).wait()
    gated_store = load(8, gated, gated_h)
    gated_store.start()
    n2_store = load(9, n2.at[pl.ds(0, rows)], n2_h.at[pl.ds(0, rows)])
    n2_store.start()

    def stores(p, step, slot):
        at = pl.ds(pl.multiple_of(p * PASS, PASS), PASS)
        cols = pl.ds(pl.multiple_of(step * STEP, STEP), STEP)
        return [
            pltpu.make_async_copy(buf.at[slot], out.at[at, cols], o_sem.at[slot, k])
            for k, (buf, out) in enumerate(((inner, inner_h), (gg, gg_h), (ug, ug_h)))
        ]

    def low_stores(p):
        at = pl.ds(pl.multiple_of(p * PASS, PASS), PASS)
        return [
            pltpu.make_async_copy(low1, out_h.at[at], l_sem.at[0]),
            pltpu.make_async_copy(low2, n2g_h.at[at], l_sem.at[1]),
        ]

    passes = 2 * rows // PASS

    def ffn_pass(p, carry):
        acc1[...] = jnp.zeros_like(acc1)
        acc2[...] = jnp.zeros_like(acc2)

        def ffn_step(step, carry):
            u = p * steps + step
            slot = u % 2
            for copy in weights(u):
                copy.wait()

            @pl.when(u + 1 < passes * steps)
            def _():
                for copy in weights(u + 1):
                    copy.start()

            @pl.when(u >= 2)
            def _():
                for copy in stores(p, step, slot):
                    copy.wait()

            def front(r):
                at = tile_at(r, p * PASS)
                a, c = n2[at, :], cot[at, :]
                return dot(a, wg[slot]), dot(a, wu[slot]), dot(c, wd[slot], NT)

            count = PASS // TILE
            held = front(0)
            for r in range(count):
                following = front(r + 1) if r + 1 < count else None
                s = pl.ds(r * TILE, TILE)
                g, v, ig = held
                sig = jax.nn.sigmoid(g)
                silu = g * sig
                low = (silu * v).astype(BF16)
                gg_low = (ig * v * (sig + silu * (1.0 - sig))).astype(BF16)
                ug_low = (ig * silu).astype(BF16)
                inner[slot, s, :] = low
                gg[slot, s, :] = gg_low
                ug[slot, s, :] = ug_low
                acc1[s, :] += dot(low, wd[slot])
                acc2[s, :] += dot(gg_low, wg[slot], NT) + dot(ug_low, wu[slot], NT)
                held = following
            for copy in stores(p, step, slot):
                copy.start()
            return carry

        lax.fori_loop(0, steps, ffn_step, 0)

        @pl.when(p > 0)
        def _():
            for copy in low_stores(p):
                copy.wait()

        low1[...] = acc1[...].astype(BF16)
        low2[...] = acc2[...].astype(BF16)
        for copy in low_stores(p):
            copy.start()
        return carry

    n2_other = load(10, n2.at[pl.ds(rows, rows)], n2_h.at[pl.ds(rows, rows)])

    def other_tile(i, carry):
        values = widen(other[tile_at(i), :])
        normed = (values * inverse_rms(values) * gain_one[...]).astype(BF16)
        both = [mix(normed, h)[4].astype(BF16) for h in range(2)]
        leave_mixer(values, both, tile_at(i, rows))
        return carry

    def arrived(p):
        @pl.when(p == passes // 2)
        def _():
            prev[...] = jnp.zeros_like(prev)
            for copy in input_copies:
                copy.wait()
            lax.fori_loop(0, tiles, other_tile, 0)
            n2_other.start()

        per_block = PASS // TILE
        for k, copy in enumerate(grad_copies):

            @pl.when(p == passes // 2 + k)
            def _(k=k, copy=copy):
                copy.wait()
                lax.fori_loop(k * per_block, (k + 1) * per_block, masked(rows, other_length), 0)

    def whole_pass(p, carry):
        arrived(p)
        return ffn_pass(p, carry)

    lax.fori_loop(0, passes, whole_pass, 0)
    cot_other = load(11, cot.at[pl.ds(rows, rows)], cot_h.at[pl.ds(rows, rows)])
    cot_other.start()
    for slot in range(2):
        for copy in stores(0, 0, slot):
            copy.wait()
    for copy in low_stores(0):
        copy.wait()
    taps_out[...] = taps[...]
    for copy in [n1_store, cot_store, gated_store, n2_store, n2_other, cot_other] + other_stores:
        copy.wait()


def front(lengths, gains, taps_own, block_input, output_grad, in_own, out_own, gate_w, up_w, down_w):
    rows, width = block_input.shape
    channels = out_own.shape[0]
    hidden_units = gate_w.shape[1]
    vmem = pl.BlockSpec(memory_space=pltpu.VMEM)
    hbm = pl.BlockSpec(memory_space=pl.ANY)

    def shaped(*shape, kind=BF16):
        return jax.ShapeDtypeStruct(shape, kind)

    both = 2 * rows
    outs = [
        shaped(2, KERNEL, channels, kind=F32),
        shaped(both, width),
        shaped(both, width),
        shaped(both, hidden_units),
        shaped(both, hidden_units),
        shaped(both, hidden_units),
        shaped(both, width),
        shaped(both, width),
        shaped(rows, width, kind=F32),
        shaped(rows, 4 * channels),
        shaped(rows, 4 * channels),
        shaped(KERNEL, width, channels),
        shaped(channels, width),
        shaped(rows, width),
        shaped(rows, 2 * channels),
    ]
    x_count = 5 + 2 * (rows // PASS)
    dma = pltpu.SemaphoreType.DMA
    return pl.pallas_call(
        front_kernel,
        in_specs=[pl.BlockSpec(memory_space=pltpu.SMEM), vmem, vmem, vmem] + [hbm] * 7,
        out_specs=[vmem] + [hbm] * 14,
        out_shape=outs,
        scratch_shapes=[
            pltpu.VMEM((2, KERNEL, width, channels), BF16),
            pltpu.VMEM((2, channels, width), BF16),
            pltpu.VMEM((rows, width), BF16),
            pltpu.VMEM((rows, width), BF16),
            pltpu.VMEM((rows, width), BF16),
            pltpu.VMEM((rows, 2 * channels), BF16),
            pltpu.VMEM((both, width), BF16),
            pltpu.VMEM((both, width), BF16),
            pltpu.VMEM((2, width, STEP), BF16),
            pltpu.VMEM((2, width, STEP), BF16),
            pltpu.VMEM((2, STEP, width), BF16),
            pltpu.VMEM((2, PASS, STEP), BF16),
            pltpu.VMEM((2, PASS, STEP), BF16),
            pltpu.VMEM((2, PASS, STEP), BF16),
            pltpu.VMEM((PASS, width), F32),
            pltpu.VMEM((PASS, width), F32),
            pltpu.VMEM((2, TILE, 4 * channels), BF16),
            pltpu.VMEM((2, TILE, width), F32),
            pltpu.VMEM((PASS, width), BF16),
            pltpu.VMEM((PASS, width), BF16),
            pltpu.VMEM((2, 8, channels), F32),
            pltpu.VMEM((2, KERNEL, channels), F32),
            pltpu.VMEM((KERNEL, channels), BF16),
            dma((12,)),
            dma((2, 3)),
            dma((2, 3)),
            dma((2,)),
            dma((2,)),
            dma((2,)),
            dma((x_count,)),
            dma((x_count,)),
            dma((4, 3)),
            dma((4, 3)),
        ],
        name="front",
        cost_estimate=pl.CostEstimate(
            flops=24 * rows * width * hidden_units, bytes_accessed=40 * hidden_units * width, transcendentals=0
        ),
        compiler_params=pltpu.CompilerParams(
            collective_id=2, has_side_effects=True, vmem_limit_bytes=63 * 2**20
        ),
    )(lengths, *gains, taps_own, block_input, output_grad, in_own, out_own, gate_w, up_w, down_w)


def back_kernel(
    gain_one, gain_two, taps,
    cot_h, n2_h, inner_h, gg_h, ug_h, n2g_h, out_h,
    hidden, source, parts_o, parts_p, in_o, in_p, out_w_o, out_w_p, n1, gated,
    summed, input_grad, block_out, out_recv, small,
    ring, rc, ry, ra, rb, rx, small_recv, cot, n2, operand, in_w, pg, part, hid, ngo, ngr, src, ig, nxt, kacc,
    load_sem, fixed_sem, tile_sem, send, recv, local_sem, x_send, x_recv, small_send, small_rsem,
):
    width = cot.shape[1]
    rows = n1.shape[0]
    channels = out_w_o.shape[0]
    ffn_chunks = 3 * inner_h.shape[1] // TILE
    in_chunks = 3 * channels // TILE
    own_chunks = in_chunks + channels // TILE
    total = ffn_chunks + own_chunks
    half = width // 2

    me = lax.axis_index("dp")
    tensor = lax.axis_index("tensor")
    bits = [(me // (1 << k)) % 2 for k in range(4)]
    peers = [me + (1 << k) - (2 << k) * bits[k] for k in range(4)]
    z = me // 4
    mirror = me + 4 * (3 - 2 * z)
    inner_z = (z == 1) | (z == 2)
    outer_z = (z == 0) | (z == 3)
    enter([(p, tensor) for p in peers] + [(mirror, tensor), (me, 1 - tensor)])

    def peer_copy(src_ref, dst_ref, slot, j, peer):
        return pltpu.make_async_remote_copy(
            src_ref=src_ref, dst_ref=dst_ref, send_sem=send.at[slot, j], recv_sem=recv.at[slot, j],
            device_id=(peer, tensor), device_id_type=MESH,
        )

    def x_copy(src_ref, dst_ref, k):
        return pltpu.make_async_remote_copy(
            src_ref=src_ref, dst_ref=dst_ref, send_sem=x_send.at[k], recv_sem=x_recv.at[k],
            device_id=(me, 1 - tensor), device_id_type=MESH,
        )

    def rows_at(start, size):
        return pl.ds(pl.multiple_of(start, size), size)

    quarter, eighth = half // 2, half // 4
    core_at = rows_at(bits[0] * half, half)
    core_away = rows_at((1 - bits[0]) * half, half)
    y_at = rows_at(bits[1] * quarter, quarter)
    y_away = rows_at((1 - bits[1]) * quarter, quarter)
    z_at = rows_at(bits[1] * quarter + bits[3] * eighth, eighth)
    z_away = rows_at(bits[1] * quarter + (1 - bits[3]) * eighth, eighth)

    def result(j, start, size):
        return summed.at[j, rows_at(start, size)]

    def result_y(j):
        return result(j, bits[0] * half + bits[1] * quarter, quarter)

    def result_z(j, side):
        return result(j, bits[0] * half + bits[1] * quarter + side * eighth, eighth)

    def scatter0(q):
        return peer_copy(ring.at[q % RING, core_away], rc.at[q], 0, q, peers[0])

    def scatter_y(j):
        return peer_copy(rc.at[j, y_away], ry.at[j], 1, j, peers[1])

    def up(j):
        return peer_copy(rc.at[j, y_at], ra.at[j], 2, j, peers[2])

    def across(j):
        return peer_copy(rc.at[j, z_away], rb.at[j], 3, j, mirror)

    def keep(j):
        return pltpu.make_async_copy(rc.at[j, z_at], result_z(j, bits[3]), local_sem.at[j])

    def gather_across(j):
        return peer_copy(rc.at[j, z_at], result_z(j, bits[3]), 4, j, mirror)

    def down_own(j):
        return peer_copy(rc.at[j, z_at], result_z(j, bits[3]), 5, j, peers[2])

    def down_other(j):
        return peer_copy(result_z(j, 1 - bits[3]), result_z(j, 1 - bits[3]), 6, j, peers[2])

    def gather_y(j):
        return peer_copy(result_y(j), result_y(j), 7, j, peers[1])

    def gather_core(j):
        at = result(j, bits[0] * half, half)
        return peer_copy(at, at, 8, j, peers[0])

    def add(j, at, landed):
        rc[j, at, :] = (widen(rc[j, at, :]) + widen(landed[j])).astype(BF16)

    def when(j, also, what):
        inside = (j >= 0) & (j < total)

        @pl.when(inside if also is None else inside & also)
        def _():
            what(j)

    def tick(k):
        def from_y(j):
            scatter_y(j).wait()
            add(j, y_at, ry)

            @pl.when(outer_z)
            def _():
                up(j).start()

        def from_outer(j):
            up(j).wait_recv()
            add(j, y_at, ra)
            across(j).start()

        def from_inner(j):
            across(j).wait()
            add(j, z_at, rb)
            gather_across(j).start()
            down_own(j).start()
            keep(j).start()

        def to_outer(j):
            gather_across(j).wait()
            keep(j).wait()
            down_other(j).start()

        def to_y_again(j):
            @pl.when(inner_z)
            def _():
                down_own(j).wait_send()

            @pl.when(outer_z)
            def _():
                up(j).wait_send()
                down_own(j).wait_recv()
                down_other(j).wait_recv()

            gather_y(j).start()

        when(k, None, from_y)
        when(k - LAGS[0], inner_z, from_outer)
        when(k - LAGS[1], inner_z, from_inner)
        when(k - LAGS[2], inner_z, to_outer)
        when(k - LAGS[3], None, to_y_again)

    def finish(j):
        gather_y(j).wait()
        gather_core(j).start()

    def ticks(low, high):
        def one(k, carry):
            tick(k)
            return carry

        lax.fori_loop(low, high, one, 0)

    def fixed(k, src_ref, dst_ref):
        return pltpu.make_async_copy(src_ref, dst_ref, fixed_sem.at[k])

    first_loads = [fixed(0, cot_h, cot)]
    second_loads = [fixed(1, n2_h, n2)]
    mixer_loads = [fixed(2, in_o, in_w.at[0]), fixed(3, in_p, in_w.at[1])]
    out_loads = [
        fixed(4, out_w_o, cot.at[pl.ds(rows, channels)]),
        fixed(5, out_w_p, cot.at[pl.ds(rows + channels, channels)]),
    ]
    late_loads = [fixed(6, n1, n2.at[pl.ds(0, rows)]), fixed(7, gated, n2.at[pl.ds(rows, rows)])]

    def start(copies):
        for copy in copies:
            copy.start()

    def wait(copies):
        for copy in copies:
            copy.wait()

    groups = (inner_h, gg_h, ug_h)
    per = ffn_chunks // 3

    def operands(group, i, slot):
        cols = pl.ds(pl.multiple_of(i * TILE, TILE), TILE)
        return [pltpu.make_async_copy(groups[group].at[:, cols], operand.at[slot], load_sem.at[slot])]

    start(first_loads)
    start(operands(0, 0, 0))
    start(second_loads)
    start(mixer_loads)

    tiles = rows // TILE

    def n2g_block(i):
        at = (tiles - 1 - i) * TILE
        return x_copy(
            n2g_h.at[pl.ds(pl.multiple_of(rows + at, TILE), TILE)],
            ngr.at[pl.ds(pl.multiple_of(at, TILE), TILE)],
            i,
        )

    for i in range(tiles):
        n2g_block(i).start()
    last_swap = x_copy(out_h.at[pl.ds(rows, rows)], out_recv, tiles + own_chunks)
    last_swap.start()
    wait(first_loads)

    def from_core(q):
        scatter0(q).wait()
        rc[q] = (widen(ring[q % RING, core_at, :]) + widen(rc[q])).astype(BF16)

    def to_y(j):
        from_core(j)
        scatter_y(j).start()

    for group in range(3):
        if group == 1:
            wait(second_loads)
            start(out_loads)

        def compute(i, carry, group=group):
            j = group * per + i
            slot = j % 2
            wait(operands(group, i, slot))

            @pl.when(i + 1 < per)
            def _():
                start(operands(group, i + 1, 1 - slot))

            if group < 2:

                @pl.when(i + 1 == per)
                def _():
                    start(operands(group + 1, 0, 1 - slot))

            left = cot if group == 0 else n2
            ring[j % RING] = dot(left[...], operand[slot], TN).astype(BF16)
            scatter0(j).start()

            @pl.when(j >= LAG)
            def _():
                to_y(j - LAG)

            @pl.when(j >= 10)
            def _():
                tick(j - 10)

            return carry

        lax.fori_loop(0, per, compute, 0)
    start(late_loads)
    for j in range(ffn_chunks - LAG, ffn_chunks):
        to_y(j)
    done = ffn_chunks - 10

    nxt[...] = jnp.zeros_like(nxt)
    kacc[...] = jnp.zeros_like(kacc)
    small[...] = jnp.zeros_like(small)
    wait(mixer_loads)
    wait(out_loads)

    def mixer(i, carry):
        at = pl.ds(pl.multiple_of((tiles - 1 - i) * TILE, TILE), TILE)
        loads = [
            pltpu.make_async_copy(hidden.at[at], hid, tile_sem.at[0]),
            pltpu.make_async_copy(n2g_h.at[at], ngo, tile_sem.at[1]),
            pltpu.make_async_copy(source.at[at], src, tile_sem.at[2]),
            pltpu.make_async_copy(parts_o.at[at], part.at[0], tile_sem.at[3]),
            pltpu.make_async_copy(parts_p.at[at], part.at[1], tile_sem.at[4]),
        ]
        start(loads)
        n2g_block(i).wait()
        wait(loads)
        upstream = widen(ngo[...]) + widen(ngr[at, :])
        values = hid[...]
        inverse = lax.rsqrt(jnp.mean(values * values, axis=-1, keepdims=True) + eps)
        weighted = upstream * gain_two[...]
        scaled = values * inverse
        small[1:2, :] += jnp.sum(upstream * scaled, axis=0, keepdims=True)
        along = jnp.mean(weighted * scaled, axis=-1, keepdims=True)
        grad = widen(cot[at, :]) + inverse * (weighted - scaled * along)
        grad_low = grad.astype(BF16)
        cot[at, :] = grad_low
        row = lax.broadcasted_iota(jnp.int32, (TILE, channels), 0)
        upstream_one = jnp.zeros((TILE, width), F32)
        for h in range(2):
            out_w = cot[pl.ds(rows + h * channels, channels), :]
            gated_grad = dot(grad_low, out_w, NT)
            b_part = widen(part[h, :, 0:channels])
            c_part = widen(part[h, :, channels : 2 * channels])
            x_part = widen(part[h, :, 2 * channels : 3 * channels])
            convolved = widen(part[h, :, 3 * channels : 4 * channels])
            conv_grad = gated_grad * c_part
            one = jnp.where(row == TILE - 1, nxt[h, 0:1, :], pltpu.roll(conv_grad, TILE - 1, 0))
            two = jnp.where(
                row == TILE - 1,
                nxt[h, 1:2, :],
                jnp.where(row == TILE - 2, nxt[h, 0:1, :], pltpu.roll(conv_grad, TILE - 2, 0)),
            )
            nxt[h, 0:2, :] = conv_grad[0:2, :]
            mixed_grad = taps[h, 2:3, :] * conv_grad + taps[h, 1:2, :] * one + taps[h, 0:1, :] * two
            mixed = b_part * x_part
            kacc[h, 0:1, :] += jnp.sum(mixed * two, axis=0, keepdims=True)
            kacc[h, 1:2, :] += jnp.sum(mixed * one, axis=0, keepdims=True)
            kacc[h, 2:3, :] += jnp.sum(mixed * conv_grad, axis=0, keepdims=True)
            for k, piece_grad in enumerate((mixed_grad * x_part, gated_grad * convolved, mixed_grad * b_part)):
                low = piece_grad.astype(BF16)
                pg[h, at, k * channels : (k + 1) * channels] = low
                upstream_one = upstream_one + dot(low, in_w[h, k], NT)
        values_one = widen(src[...])
        inverse_one = lax.rsqrt(jnp.mean(values_one * values_one, axis=-1, keepdims=True) + eps)
        weighted_one = upstream_one * gain_one[...]
        scaled_one = values_one * inverse_one
        small[0:1, :] += jnp.sum(upstream_one * scaled_one, axis=0, keepdims=True)
        along_one = jnp.mean(weighted_one * scaled_one, axis=-1, keepdims=True)
        ig[...] = (grad + inverse_one * (weighted_one - scaled_one * along_one)).astype(BF16)
        store = pltpu.make_async_copy(ig, input_grad.at[at], tile_sem.at[5])
        store.start()
        store.wait()
        return carry

    lax.fori_loop(0, tiles, mixer, 0)
    wait(late_loads)

    def piece(h, m_in, m_out):
        if m_in is not None:
            cols = pl.ds(pl.multiple_of(m_in * TILE, TILE), TILE)
            return dot(n2[0:rows, :], pg[h, :, cols], TN)
        cols = pl.ds(pl.multiple_of(h * channels + m_out * TILE, TILE), TILE)
        return dot(cot[0:rows, :], n2[rows : 2 * rows, cols], TN)

    def cross(m):
        return x_copy(rc.at[total + m], rx.at[m], tiles + m)

    def after_core(h, m):
        if h == 1:
            from_core(total + m)
            cross(m).start()
        else:
            from_core(ffn_chunks + m)

    for h in (1, 0):
        base = total if h == 1 else ffn_chunks

        def in_piece(m, carry, h=h, base=base):
            q = base + m
            ring[q % RING] = piece(h, m, None).astype(BF16)
            scatter0(q).start()

            @pl.when(m >= LAG)
            def _():
                after_core(h, m - LAG)

            k = done + m + (in_chunks if h == 0 else 0)

            @pl.when(k < ffn_chunks)
            def _():
                tick(k)

            return carry

        lax.fori_loop(0, in_chunks, in_piece, 0)
        for m in range(in_chunks, own_chunks):
            ring[(base + m) % RING] = piece(h, None, m - in_chunks).astype(BF16)
            scatter0(base + m).start()
            after_core(h, m - LAG)
        for m in range(own_chunks - LAG, own_chunks):
            after_core(h, m)
    for h in range(2):
        cols = pl.ds(pl.multiple_of(channels * (tensor + h - 2 * tensor * h), channels), channels)
        small[2:5, cols] = kacc[h, 0:3, :]

    def small_copy(k):
        device = (peers[k], tensor) if k < 4 else (me, 1 - tensor)
        return pltpu.make_async_remote_copy(
            src_ref=small, dst_ref=small_recv.at[k], send_sem=small_send.at[k], recv_sem=small_rsem.at[k],
            device_id=device, device_id_type=MESH,
        )

    def crossed(m, carry):
        cross(m).wait()
        j = ffn_chunks + m
        rc[j] = (widen(rc[j]) + widen(rx[m])).astype(BF16)
        scatter_y(j).start()
        finish(m)
        return carry

    lax.fori_loop(0, own_chunks, crossed, 0)
    last_tick = total + LAGS[3]
    turn = 2 * ffn_chunks - own_chunks - LAGS[3] - 3

    def drain_two(k, carry):
        tick(k)
        finish(own_chunks + 2 * (k - ffn_chunks))
        finish(own_chunks + 2 * (k - ffn_chunks) + 1)
        return carry

    def drain_one(k, carry):
        tick(k)
        finish(k - LAGS[3] - 3)
        return carry

    def drain(j, carry):
        finish(j)
        return carry

    lax.fori_loop(ffn_chunks, turn, drain_two, 0)
    for k in range(5):
        small_copy(k).start()
        small_copy(k).wait()
        small[...] = small[...] + small_recv[k]
    lax.fori_loop(turn, last_tick, drain_one, 0)

    last_swap.wait()

    def leave(i, carry):
        at = pl.ds(pl.multiple_of(i * TILE, TILE), TILE)
        loads = [
            pltpu.make_async_copy(hidden.at[at], hid, tile_sem.at[0]),
            pltpu.make_async_copy(out_h.at[at], ngo, tile_sem.at[1]),
            pltpu.make_async_copy(out_recv.at[at], src, tile_sem.at[2]),
        ]
        start(loads)
        wait(loads)
        ig[...] = (hid[...] + (widen(ngo[...]) + widen(src[...]))).astype(BF16)
        store = pltpu.make_async_copy(ig, block_out.at[at], tile_sem.at[5])
        store.start()
        store.wait()
        return carry

    lax.fori_loop(0, tiles, leave, 0)

    lax.fori_loop(last_tick - LAGS[3] - 3, total, drain, 0)

    def arrive(j, carry):
        gather_core(j).wait()

        @pl.when(inner_z)
        def _():
            down_other(j).wait_send()

        return carry

    lax.fori_loop(0, total, arrive, 0)


def back(gains, taps, arrays, rows, width, hidden, channels):
    ffn_chunks = 3 * hidden // TILE
    own_chunks = 4 * channels // TILE
    total = ffn_chunks + own_chunks
    half = width // 2
    vmem = pl.BlockSpec(memory_space=pltpu.VMEM)
    hbm = pl.BlockSpec(memory_space=pl.ANY)

    def buffer(count, size):
        return pltpu.VMEM((count, size, TILE), BF16)

    return pl.pallas_call(
        back_kernel,
        in_specs=[vmem, vmem, vmem] + [hbm] * len(arrays),
        out_specs=[hbm, hbm, hbm, hbm, vmem],
        out_shape=[
            jax.ShapeDtypeStruct((total, width, TILE), BF16),
            jax.ShapeDtypeStruct((rows, width), BF16),
            jax.ShapeDtypeStruct((rows, width), BF16),
            jax.ShapeDtypeStruct((rows, width), BF16),
            jax.ShapeDtypeStruct((8, width), F32),
        ],
        scratch_shapes=[
            buffer(RING, width),
            buffer(total + own_chunks, half),
            buffer(total, half // 2),
            buffer(total, half // 2),
            buffer(total, half // 4),
            buffer(own_chunks, half),
            pltpu.VMEM((5, 8, width), F32),
            pltpu.VMEM((2 * rows, width), BF16),
            pltpu.VMEM((2 * rows, width), BF16),
            buffer(2, 2 * rows),
            pltpu.VMEM((2, 3, width, channels), BF16),
            pltpu.VMEM((2, rows, 3 * channels), BF16),
            pltpu.VMEM((2, TILE, 4 * channels), BF16),
            pltpu.VMEM((TILE, width), F32),
            pltpu.VMEM((TILE, width), BF16),
            pltpu.VMEM((rows, width), BF16),
            pltpu.VMEM((TILE, width), BF16),
            pltpu.VMEM((TILE, width), BF16),
            pltpu.VMEM((2, 8, channels), F32),
            pltpu.VMEM((2, 8, channels), F32),
            pltpu.SemaphoreType.DMA((2,)),
            pltpu.SemaphoreType.DMA((8,)),
            pltpu.SemaphoreType.DMA((6,)),
            pltpu.SemaphoreType.DMA((9, total + own_chunks)),
            pltpu.SemaphoreType.DMA((9, total + own_chunks)),
            pltpu.SemaphoreType.DMA((total,)),
            pltpu.SemaphoreType.DMA((rows // TILE + own_chunks + 1,)),
            pltpu.SemaphoreType.DMA((rows // TILE + own_chunks + 1,)),
            pltpu.SemaphoreType.DMA((5,)),
            pltpu.SemaphoreType.DMA((5,)),
        ],
        name="back",
        cost_estimate=pl.CostEstimate(
            flops=12 * rows * width * hidden + 32 * rows * width * channels,
            bytes_accessed=20 * hidden * width,
            transcendentals=0,
        ),
        compiler_params=pltpu.CompilerParams(
            collective_id=1, has_side_effects=True, vmem_limit_bytes=63 * 2**20
        ),
    )(*gains, taps, *arrays)


def finish_kernel(
    summed, block_in, grad_in, down, gate, up, in_grad, out, block_out, grad_out, buf, wide, turned, held, sem_in, sem_out, sem_keep
):
    width = summed.shape[1]
    most = buf.shape[1]
    hidden_units, channels = down.shape[0], out.shape[0]
    per, halves = hidden_units // TILE, channels // TILE
    fetches = [
        pltpu.make_async_copy(block_in, held.at[0], sem_keep.at[0]),
        pltpu.make_async_copy(grad_in, held.at[1], sem_keep.at[1]),
    ]
    keeps = [
        pltpu.make_async_copy(held.at[0], block_out, sem_keep.at[2]),
        pltpu.make_async_copy(held.at[1], grad_out, sem_keep.at[3]),
    ]
    jobs = []
    for group, target in ((1, gate), (0, down), (2, up)):
        for i in range(0, per, most):
            at = pl.ds(i * TILE, most * TILE)
            place = target.at[at] if group == 0 else target.at[:, at]
            jobs.append((group * per + i, most, group == 0, place))
    jobs.append((3 * per + KERNEL * halves, halves, True, out))
    for k in range(KERNEL):
        jobs.append((3 * per + k * halves, halves, False, in_grad.at[k]))

    def load(n):
        first, count = jobs[n][0], jobs[n][1]
        return pltpu.make_async_copy(
            summed.at[pl.ds(first, count)], buf.at[n % 2, pl.ds(0, count)], sem_in.at[n % 2]
        )

    def store(n):
        _, count, turn, place = jobs[n]
        size = count * TILE
        source = turned.at[n % 2, pl.ds(0, size)] if turn else wide.at[n % 2, :, pl.ds(0, size)]
        return pltpu.make_async_copy(source, place, sem_out.at[n % 2])

    load(0).start()
    load(1).start()
    for n, (_, count, turn, _) in enumerate(jobs):
        load(n).wait()
        if n >= 2:
            store(n - 2).wait()
        slot = n % 2
        for k in range(count):
            at = slice(k * TILE, (k + 1) * TILE)
            if turn:
                turned[slot, at, :] = widen(buf[slot, k]).T
            else:
                wide[slot, :, at] = widen(buf[slot, k])
        store(n).start()
        if n + 2 < len(jobs):
            load(n + 2).start()
        if n == 1:
            for copy in fetches:
                copy.start()
        if n == 4:
            for fetch, copy in zip(fetches, keeps):
                fetch.wait()
                copy.start()
    for n in (len(jobs) - 2, len(jobs) - 1):
        store(n).wait()
    for copy in keeps:
        copy.wait()


def finish_grads(summed, block_output, input_grad, hidden_units, channels):
    width = summed.shape[1]
    hbm = pl.BlockSpec(memory_space=pl.ANY)
    low = jax.ShapeDtypeStruct(block_output.shape, BF16)
    return pl.pallas_call(
        finish_kernel,
        in_specs=[hbm] * 3,
        out_specs=[hbm] * 7,
        out_shape=[
            jax.ShapeDtypeStruct((hidden_units, width), F32),
            jax.ShapeDtypeStruct((width, hidden_units), F32),
            jax.ShapeDtypeStruct((width, hidden_units), F32),
            jax.ShapeDtypeStruct((KERNEL, width, channels), F32),
            jax.ShapeDtypeStruct((channels, width), F32),
            low,
            low,
        ],
        scratch_shapes=[
            pltpu.VMEM((2, STEP // TILE, width, TILE), BF16),
            pltpu.VMEM((2, width, STEP), F32),
            pltpu.VMEM((2, STEP, width), F32),
            pltpu.VMEM((2,) + block_output.shape, BF16),
            pltpu.SemaphoreType.DMA((2,)),
            pltpu.SemaphoreType.DMA((2,)),
            pltpu.SemaphoreType.DMA((4,)),
        ],
        name="finish_grads",
        compiler_params=pltpu.CompilerParams(vmem_limit_bytes=63 * 2**20),
    )(summed, block_output, input_grad)


def fast(
    block_input,
    mixer_gain,
    in_weight,
    conv_kernel,
    out_weight,
    ffn_gain,
    gate_weight,
    up_weight,
    down_weight,
    output_grad,
    lengths,
):
    rows, width = block_input.shape
    channels, hidden_units = out_weight.shape[0], gate_weight.shape[1]
    me = lax.axis_index("tensor")
    gains = (mixer_gain[None], ffn_gain[None])
    in_parts = jnp.transpose(in_weight, (1, 0, 2))
    taps, cot, n2, inner, gg, ug, n2g, out, hidden, parts_o, parts_p, in_other, out_other, n1, gated = front(
        lengths,
        gains,
        conv_kernel,
        block_input,
        output_grad,
        in_parts,
        out_weight,
        gate_weight,
        up_weight,
        down_weight,
    )
    arrays = (cot, n2, inner, gg, ug, n2g, out, hidden, block_input, parts_o, parts_p)
    arrays += (in_parts, in_other, out_weight, out_other, n1, gated)
    summed, input_grad, block_output, _, small = back(gains, taps, arrays, rows, width, hidden_units, channels)
    down_grad, gate_grad, up_grad, in_grad, out_grad, block_output, input_grad = finish_grads(
        summed, block_output, input_grad, hidden_units, channels
    )
    conv_kernel_grad = lax.dynamic_slice_in_dim(small[2 : 2 + KERNEL], me * channels, channels, axis=1)
    return (
        block_output,
        input_grad,
        small[0],
        jnp.transpose(in_grad, (1, 0, 2)),
        conv_kernel_grad,
        out_grad,
        small[1],
        gate_grad,
        up_grad,
        down_grad,
    )


def solution(mesh):
    def step(*args):
        rows, slots = args[0].shape[0], args[10].shape[0]
        one_slot_each = mesh.shape["tensor"] == 2 and mesh.shape["dp"] == 16 and slots == 2 and rows == 4 * TILE
        return (fast if one_slot_each else local)(*args)

    return jax.shard_map(
        step,
        mesh=mesh,
        in_specs=(
            P(("dp", "tensor"), None),
            P(),
            P(None, None, "tensor"),
            P(None, "tensor"),
            P("tensor", None),
            P(),
            P(None, "tensor"),
            P(None, "tensor"),
            P("tensor", None),
            P(("dp", "tensor"), None),
            P("dp"),
        ),
        out_specs=(
            P(("dp", "tensor"), None),
            P(("dp", "tensor"), None),
            P(),
            P(None, None, "tensor"),
            P(None, "tensor"),
            P("tensor", None),
            P(),
            P(None, "tensor"),
            P(None, "tensor"),
            P("tensor", None),
        ),
        check_vma=False,
    )
```
